32 devices in a mesh: dp: 4 (over y, core), tensor: 8 (over z, x).
Axes of the slice: x: 2, y: 2, z: 4, core: 2. Of those that a mesh axis runs over, the one named last changes fastest.
Arguments:
- gate_pre: bfloat16 [1024, 16384], P('dp', 'tensor'), may hold values from -6 to 6
- up_pre: bfloat16 [1024, 16384], P('dp', 'tensor'), may hold values from -6 to 6
- down_weight: bfloat16 [16384, 4096], P('tensor', 'dp'), may hold values from -0.046875 to 0.046875
- factors: float32 [9, 512, 32, 64], P(None, 'tensor'), may hold values from -0.3 to 0.3
- out_grad: bfloat16 [1024, 4096], P('dp'), may hold values from -6 to 6
Outputs:
- output: bfloat16 [1024, 4096], P('dp')
- gate_grad: bfloat16 [1024, 16384], P('dp', 'tensor')
- up_grad: bfloat16 [1024, 16384], P('dp', 'tensor')
- factor_grads: float32 [9, 512, 32, 64], P(None, 'tensor')
The draws below stay inside these ranges and needn't reach their ends.
All inputs are finite; a program needn't handle non-finite values.
Results may differ from the reference program's by a relative error of at most 0.012.
The reference program's roundings to bfloat16 on the way count: a program that leaves them out, or rounds other values in their place, can miss the bound.
Values may be sent and summed in bfloat16 or wider, within the bound.
No kernel may reach another device: no remote copies, remote signals or barrier semaphores. Data moves between devices by JAX's collectives and lax.ppermute only.
A program may use at most 192 MiB of HBM per device.

```python
import math
import jax
import jax.numpy as jnp
from jax import lax

D = 4096
FF = 16384
HALF = 32
FACTORS = 9
TOKENS = 1024


def block_scale(rng, dims, pieces, least, top_value):
    def one(axis_at, blocks):
        draws = jax.random.uniform(jax.random.fold_in(jax.random.fold_in(rng, 6), axis_at), (blocks,), jnp.float32, least / len(pieces), top_value / len(pieces))
        return jnp.repeat(jnp.exp(draws), dims[axis_at] // blocks).reshape((-1,) + (1,) * (len(dims) - axis_at - 1))

    factor_of = one(*pieces[0])
    for cut in pieces[1:]:
        factor_of = factor_of * one(*cut)
    return factor_of


def bell_draw(key, shape, width, limit, cuts=(), held_as=jnp.bfloat16):
    values = jax.random.normal(key, shape, jnp.float32) * width
    if len(cuts) > 0:
        values = block_scale(key, shape, cuts, -0.22, 0.18) * values
    return jnp.clip(values, min=-limit, max=limit).astype(held_as)


def setup_inputs(seed: int = 0) -> dict:
    key_of = jax.random.split(jax.random.key(seed), 6)
    gate_pre = bell_draw(key_of[0], (TOKENS, FF), 1.0, 6.0, ((0, 4), (1, 8)))
    up_pre = bell_draw(key_of[1], (TOKENS, FF), 1.0, 6.0, ((0, 4), (1, 8)))
    down_weight = bell_draw(key_of[2], (FF, D), FF ** -0.5, 0.046875, ((0, 8), (1, 4)))
    factors = bell_draw(key_of[3], (FACTORS, FF // HALF, HALF, 2 * HALF), 0.05, 0.3, ((1, 8),), jnp.float32)
    out_grad = bell_draw(key_of[4], (TOKENS, D), 1.0, 6.0, ((0, 4),))
    return {"gate_pre": gate_pre, "up_pre": up_pre, "down_weight": down_weight, "factors": factors, "out_grad": out_grad}


highest = lax.Precision.HIGHEST

def with_identity(blocks, bit_values):
    row_index = jnp.arange(HALF, dtype=jnp.int32)[None, :, None]
    col_index = jnp.arange(2 * HALF, dtype=jnp.int32)[None, None, :]
    select = (col_index == bit_values[:, None, None] * HALF + row_index).astype(jnp.float32)
    rounded = lax.optimization_barrier((blocks + select).astype(jnp.bfloat16))
    return rounded.astype(jnp.float32)

def factor_apply(values, blocks, stride):
    token_rows = values.shape[0]
    groups = blocks.shape[0] // (2 * stride)
    paired = values.astype(jnp.float32).reshape(token_rows, groups, 2, stride, HALF)
    mixing = blocks.reshape(groups, 2, stride, HALF, 2, HALF)
    result = jnp.einsum('tapbc,asbrpc->tasbr', paired, mixing, precision=highest)
    return result.reshape(token_rows, -1)

def factor_back(grad_out, inputs, blocks, stride):
    token_rows = grad_out.shape[0]
    groups = blocks.shape[0] // (2 * stride)
    grad_view = grad_out.astype(jnp.float32).reshape(token_rows, groups, 2, stride, HALF)
    input_view = inputs.astype(jnp.float32).reshape(token_rows, groups, 2, stride, HALF)
    mixing = blocks.reshape(groups, 2, stride, HALF, 2, HALF)
    block_grad = jnp.einsum('tasbr,tapbc->asbrpc', grad_view, input_view, precision=highest)
    input_grad = jnp.einsum('asbrpc,tasbr->tapbc', mixing, grad_view, precision=highest)
    return (input_grad.reshape(token_rows, -1), block_grad.reshape(blocks.shape))

def reference(gate_pre, up_pre, down_weight, factors, out_grad):
    gate_value = gate_pre.astype(jnp.float32)
    up_value = up_pre.astype(jnp.float32)
    sigmoid_gate = jax.nn.sigmoid(gate_value)
    hidden = (gate_value * sigmoid_gate * up_value).astype(jnp.bfloat16)
    positions = jnp.arange(FF // HALF, dtype=jnp.int32)
    rotated = [hidden]
    block_list = []
    for factor_index in range(FACTORS):
        bit_values = positions // 2 ** factor_index % 2
        blocks = with_identity(factors[factor_index], bit_values)
        block_list.append(blocks)
        rotated.append(factor_apply(rotated[-1], blocks, 2 ** factor_index).astype(jnp.bfloat16))
    output = jnp.dot(rotated[-1], down_weight, preferred_element_type=jnp.float32).astype(jnp.bfloat16)
    back_grad = lax.dot_general(out_grad, down_weight, (((1,), (1,)), ((), ())), preferred_element_type=jnp.float32).astype(jnp.bfloat16)
    grad_list = [None] * FACTORS
    for factor_index in reversed(range(FACTORS)):
        input_grad, block_grad = factor_back(back_grad, rotated[factor_index], block_list[factor_index], 2 ** factor_index)
        grad_list[factor_index] = block_grad
        back_grad = input_grad.astype(jnp.bfloat16)
    factor_grads = jnp.stack(grad_list) * (1.0 / math.sqrt(TOKENS))
    back_value = back_grad.astype(jnp.float32)
    gate_grad = (back_value * up_value * sigmoid_gate * (1.0 + gate_value * (1.0 - sigmoid_gate))).astype(jnp.bfloat16)
    up_grad = (back_value * gate_value * sigmoid_gate).astype(jnp.bfloat16)
    return (output, gate_grad, up_grad, factor_grads)
```

```python
import functools
import math

import jax
import jax.numpy as jnp
from jax import lax
from jax.experimental import pallas as pl
from jax.experimental.pallas import tpu as pltpu
from jax.sharding import PartitionSpec as P

HALF = 32
FACTORS = 9
LANES = 256
PER = LANES // HALF
VMEM_LIMIT = 48 * 1024 * 1024
F32 = jnp.float32
BF16 = jnp.bfloat16


def iota(shape, axis):
    return lax.broadcasted_iota(jnp.int32, shape, axis)


def with_identity(block, stride, group):
    row = iota((LANES, 2 * HALF), 0)
    col = iota((LANES, 2 * HALF), 1)
    if stride < PER:
        bit = (row // HALF // stride) & 1
    else:
        bit = (group // (stride // PER)) & 1
    select = (col == bit * HALF + (row & (HALF - 1))).astype(F32)
    return (block + select).astype(BF16)


def inner_matrix(mixing, stride):
    col = iota((2 * HALF, LANES), 0)
    lane = iota((2 * HALF, LANES), 1)
    spread = (col == ((lane // HALF // stride) & 1) * HALF + (lane & (HALF - 1))).astype(BF16)
    full = jnp.dot(mixing, spread, preferred_element_type=F32)
    row = iota((LANES, LANES), 0) // HALF
    unit = iota((LANES, LANES), 1) // HALF
    mask = (unit == row) | (unit == (row ^ stride))
    return jnp.where(mask, full, 0.0).astype(BF16)


def outer_matrix(mixing, bit):
    col = iota((2 * HALF, LANES), 0)
    lane = iota((2 * HALF, LANES), 1)
    spread = (col == bit * HALF + (lane & (HALF - 1))).astype(BF16)
    full = jnp.dot(mixing, spread, preferred_element_type=F32)
    mask = iota((LANES, LANES), 0) // HALF == iota((LANES, LANES), 1) // HALF
    return jnp.where(mask, full, 0.0).astype(BF16)


def dot_nt(a, b):
    return lax.dot_general(a, b, (((1,), (1,)), ((), ())), preferred_element_type=F32)


def dot_tn(a, b):
    return lax.dot_general(a, b, (((0,), (0,)), ((), ())), preferred_element_type=F32)


def fold(get_tile, columns_of):
    lane = iota((HALF, 128), 1)
    rows = []
    for low in range(PER // 2):
        out = None
        for upper in range(2):
            i = low + upper * (PER // 2)
            for unit_block, source, column in columns_of(i):
                tile = get_tile(source, i, unit_block // 4)
                place = upper * 2 * HALF + column * HALF
                shift = (place - (unit_block % 4) * HALF) % 128
                if shift:
                    tile = pltpu.roll(tile, shift, 1)
                if out is None:
                    out = tile
                else:
                    out = jnp.where((lane >= place) & (lane < place + HALF), tile, out)
        rows.append(out)
    return rows


def apply_forward(values, mixing_of, stride, groups):
    if stride < PER:
        for g in range(groups):
            matrix = inner_matrix(mixing_of(g), stride)
            values[g] = dot_nt(values[g], matrix).astype(BF16)
        return
    step = stride // PER
    for g in range(groups):
        if g & step:
            continue
        h = g | step
        low, high = values[g], values[h]
        for member, bit in ((g, 0), (h, 1)):
            mixing = mixing_of(member)
            new = dot_nt(low, outer_matrix(mixing, 0)) + dot_nt(high, outer_matrix(mixing, 1))
            values[member] = new.astype(BF16)


def apply_backward(grads, inputs, mixing_of, stride, groups, store_grad):
    if stride < PER:
        for g in range(groups):
            matrix = inner_matrix(mixing_of(g), stride)
            grad = grads[g]
            outer = dot_tn(grad, inputs(g))

            def columns_of(i):
                bit = (i // stride) & 1
                return ((i, 0, bit), (i ^ stride, 0, 1 - bit))

            def tile(source, i, part):
                return outer[i * HALF : (i + 1) * HALF, part * 128 : (part + 1) * 128]

            store_grad(g, fold(tile, columns_of))
            grads[g] = jnp.dot(grad, matrix, preferred_element_type=F32).astype(BF16)
        return
    step = stride // PER
    for g in range(groups):
        if g & step:
            continue
        h = g | step
        low, high = inputs(g), inputs(h)
        totals = [None, None]
        for member in (g, h):
            mixing = mixing_of(member)
            grad = grads[member]
            products = (dot_tn(grad, low), dot_tn(grad, high))

            def tile(source, i, part):
                return products[source][i * HALF : (i + 1) * HALF, part * 128 : (part + 1) * 128]

            store_grad(member, fold(tile, lambda i: ((i, 0, 0), (i, 1, 1))))
            for bit in range(2):
                term = jnp.dot(grad, outer_matrix(mixing, bit), preferred_element_type=F32)
                totals[bit] = term if totals[bit] is None else totals[bit] + term
        grads[g] = totals[0].astype(BF16)
        grads[h] = totals[1].astype(BF16)


def forward_local(gate_pre, up_pre, factors, count):
    rows, width = gate_pre.shape
    groups = width // LANES

    def kernel(gate_ref, up_ref, factor_ref, saved_ref, out_ref, values):
        k = pl.program_id(0)

        @pl.when(k == 0)
        def _():
            for g in range(groups):
                cut = pl.ds(g * LANES, LANES)
                gate = gate_ref[:, cut].astype(F32)
                hidden = gate * jax.nn.sigmoid(gate) * up_ref[:, cut].astype(F32)
                values[g] = hidden.astype(BF16)

        for step in range(count):

            @pl.when(k == step)
            def _(step=step):
                saved_ref[0] = values[...]
                stride = 2**step
                apply_forward(
                    values,
                    lambda g: with_identity(factor_ref[0, g], stride, g),
                    stride,
                    groups,
                )

        @pl.when(k == count - 1)
        def _():
            out_ref[...] = values[...]

    shape = (groups, rows, LANES)
    return pl.pallas_call(
        kernel,
        grid=(count,),
        in_specs=[
            pl.BlockSpec((rows, width), lambda k: (0, 0)),
            pl.BlockSpec((rows, width), lambda k: (0, 0)),
            pl.BlockSpec((1, groups, LANES, 2 * HALF), lambda k: (k, 0, 0, 0)),
        ],
        out_specs=[
            pl.BlockSpec((1,) + shape, lambda k: (k, 0, 0, 0)),
            pl.BlockSpec(shape, lambda k: (0, 0, 0)),
        ],
        out_shape=[
            jax.ShapeDtypeStruct((count,) + shape, BF16),
            jax.ShapeDtypeStruct(shape, BF16),
        ],
        scratch_shapes=[pltpu.VMEM(shape, BF16)],
        compiler_params=pltpu.CompilerParams(vmem_limit_bytes=VMEM_LIMIT),
        name="forward_local",
    )(gate_pre, up_pre, factors)


def forward_cross(values_in, mixing, strides):
    groups, rows, _ = values_in.shape
    count = len(strides)

    def kernel(in_ref, mixing_ref, saved_ref, out_ref, values):
        k = pl.program_id(0)

        @pl.when(k == 0)
        def _():
            values[...] = in_ref[...]

        for step in range(count):

            @pl.when(k == step)
            def _(step=step):
                saved_ref[0] = values[...]
                apply_forward(values, lambda g: mixing_ref[0, g], strides[step], groups)

        @pl.when(k == count - 1)
        def _():
            out_ref[...] = values[...]

    shape = (groups, rows, LANES)
    return pl.pallas_call(
        kernel,
        grid=(count,),
        in_specs=[
            pl.BlockSpec(shape, lambda k: (0, 0, 0)),
            pl.BlockSpec((1, groups, LANES, 2 * HALF), lambda k: (k, 0, 0, 0)),
        ],
        out_specs=[
            pl.BlockSpec((1,) + shape, lambda k: (k, 0, 0, 0)),
            pl.BlockSpec(shape, lambda k: (0, 0, 0)),
        ],
        out_shape=[
            jax.ShapeDtypeStruct((count,) + shape, BF16),
            jax.ShapeDtypeStruct(shape, BF16),
        ],
        scratch_shapes=[pltpu.VMEM(shape, BF16)],
        compiler_params=pltpu.CompilerParams(vmem_limit_bytes=VMEM_LIMIT),
        name="forward_cross",
    )(values_in, mixing)


def backward_cross(back, saved, mixing, strides):
    groups, rows, _ = back.shape
    count = len(strides)

    def kernel(in_ref, saved_ref, mixing_ref, out_ref, grad_ref, grads):
        k = pl.program_id(0)

        @pl.when(k == 0)
        def _():
            grads[...] = in_ref[...]

        for step in range(count):

            @pl.when(k == step)
            def _(step=step):
                def store(g, tiles):
                    for low, tile in enumerate(tiles):
                        grad_ref[g, 0, low * HALF : (low + 1) * HALF, :] = tile

                apply_backward(
                    grads,
                    lambda g: saved_ref[0, g],
                    lambda g: mixing_ref[0, g],
                    strides[count - 1 - step],
                    groups,
                    store,
                )

        @pl.when(k == count - 1)
        def _():
            out_ref[...] = grads[...]

    shape = (groups, rows, LANES)
    return pl.pallas_call(
        kernel,
        grid=(count,),
        in_specs=[
            pl.BlockSpec(shape, lambda k: (0, 0, 0)),
            pl.BlockSpec((1,) + shape, lambda k: (count - 1 - k, 0, 0, 0)),
            pl.BlockSpec((1, groups, LANES, 2 * HALF), lambda k: (count - 1 - k, 0, 0, 0)),
        ],
        out_specs=[
            pl.BlockSpec(shape, lambda k: (0, 0, 0)),
            pl.BlockSpec((groups, 1, 128, 128), lambda k: (0, count - 1 - k, 0, 0)),
        ],
        out_shape=[
            jax.ShapeDtypeStruct(shape, BF16),
            jax.ShapeDtypeStruct((groups, count, 128, 128), F32),
        ],
        scratch_shapes=[pltpu.VMEM(shape, BF16)],
        compiler_params=pltpu.CompilerParams(vmem_limit_bytes=VMEM_LIMIT),
        name="backward_cross",
    )(back, saved, mixing)


def backward_local(back, saved, factors, gate_pre, up_pre, count):
    groups, rows, _ = back.shape
    width = groups * LANES

    def kernel(in_ref, saved_ref, factor_ref, gate_ref, up_ref, dgate_ref, dup_ref, grad_ref, grads):
        k = pl.program_id(0)

        @pl.when(k == 0)
        def _():
            grads[...] = in_ref[...]

        for step in range(count):

            @pl.when(k == step)
            def _(step=step):
                stride = 2 ** (count - 1 - step)

                def store(g, tiles):
                    for low, tile in enumerate(tiles):
                        grad_ref[g, 0, low * HALF : (low + 1) * HALF, :] = tile

                apply_backward(
                    grads,
                    lambda g: saved_ref[0, g],
                    lambda g: with_identity(factor_ref[0, g], stride, g),
                    stride,
                    groups,
                    store,
                )

        @pl.when(k == count - 1)
        def _():
            for g in range(groups):
                cut = pl.ds(g * LANES, LANES)
                gate = gate_ref[:, cut].astype(F32)
                value = grads[g].astype(F32)
                sig = jax.nn.sigmoid(gate)
                dgate = value * up_ref[:, cut].astype(F32) * sig * (1.0 + gate * (1.0 - sig))
                dgate_ref[:, cut] = dgate.astype(BF16)
                dup_ref[:, cut] = (value * gate * sig).astype(BF16)

    shape = (groups, rows, LANES)
    whole = pl.BlockSpec((rows, width), lambda k: (0, 0))
    return pl.pallas_call(
        kernel,
        grid=(count,),
        in_specs=[
            pl.BlockSpec(shape, lambda k: (0, 0, 0)),
            pl.BlockSpec((1,) + shape, lambda k: (count - 1 - k, 0, 0, 0)),
            pl.BlockSpec((1, groups, LANES, 2 * HALF), lambda k: (count - 1 - k, 0, 0, 0)),
            whole,
            whole,
        ],
        out_specs=[
            whole,
            whole,
            pl.BlockSpec((groups, 1, 128, 128), lambda k: (0, count - 1 - k, 0, 0)),
        ],
        out_shape=[
            jax.ShapeDtypeStruct((rows, width), BF16),
            jax.ShapeDtypeStruct((rows, width), BF16),
            jax.ShapeDtypeStruct((groups, count, 128, 128), F32),
        ],
        scratch_shapes=[pltpu.VMEM(shape, BF16)],
        compiler_params=pltpu.CompilerParams(vmem_limit_bytes=VMEM_LIMIT),
        name="backward_local",
    )(back, saved, factors, gate_pre, up_pre)


def back_matmul(own_grad, other_grad, own_weight, other_weight):
    chips, rows, features = own_grad.shape
    groups = own_weight.shape[0] // LANES

    def kernel(a_ref, b_ref, w_ref, v_ref, keep_ref, send_ref):
        for chip in range(chips):
            total = dot_nt(a_ref[chip], w_ref[...]) + dot_nt(b_ref[chip], v_ref[...])
            if chip == 0:
                keep_ref[0] = total
            else:
                send_ref[chip - 1, 0] = total.astype(BF16)

    grads = pl.BlockSpec((chips, rows, features), lambda g: (0, 0, 0))
    weights = pl.BlockSpec((LANES, features), lambda g: (g, 0))
    return pl.pallas_call(
        kernel,
        grid=(groups,),
        in_specs=[grads, grads, weights, weights],
        out_specs=[
            pl.BlockSpec((1, rows, LANES), lambda g: (g, 0, 0)),
            pl.BlockSpec((chips - 1, 1, rows, LANES), lambda g: (0, g, 0, 0)),
        ],
        out_shape=[
            jax.ShapeDtypeStruct((groups, rows, LANES), F32),
            jax.ShapeDtypeStruct((chips - 1, groups, rows, LANES), BF16),
        ],
        compiler_params=pltpu.CompilerParams(vmem_limit_bytes=VMEM_LIMIT),
        name="back_matmul",
    )(own_grad, other_grad, own_weight, other_weight)


def output_matmul(values, own_weight, other_weight, core, pieces):
    chips = len(values)
    groups, rows, _ = values[0].shape
    features = own_weight.shape[1]
    tiles = features // LANES
    part = rows // pieces

    def kernel(core_ref, *refs):
        value_refs, own_ref, other_ref, out_ref = refs[:chips], refs[-3], refs[-2], refs[-1]
        j = pl.program_id(0)

        def run(w_ref):
            for chip in range(chips):
                total = None
                for g in range(groups):
                    term = jnp.dot(
                        value_refs[chip][g],
                        w_ref[g * LANES : (g + 1) * LANES, :],
                        preferred_element_type=F32,
                    )
                    total = term if total is None else total + term
                out_ref[:, chip] = total.astype(BF16).reshape(pieces, part, LANES)

        @pl.when(j < tiles)
        def _():
            run(own_ref)

        @pl.when(j >= tiles)
        def _():
            run(other_ref)

    value_spec = pl.BlockSpec((groups, rows, LANES), lambda j, c: (0, 0, 0))
    return pl.pallas_call(
        kernel,
        grid_spec=pltpu.PrefetchScalarGridSpec(
            num_scalar_prefetch=1,
            grid=(2 * tiles,),
            in_specs=[value_spec] * chips
            + [
                pl.BlockSpec((groups * LANES, LANES), lambda j, c: (0, jnp.minimum(j, tiles - 1))),
                pl.BlockSpec((groups * LANES, LANES), lambda j, c: (0, jnp.maximum(j - tiles, 0))),
            ],
            out_specs=pl.BlockSpec(
                (pieces, chips, part, LANES),
                lambda j, c: (0, 0, 0, ((j // tiles) ^ c[0]) * tiles + j % tiles),
            ),
        ),
        out_shape=jax.ShapeDtypeStruct((pieces, chips, part, 2 * features), BF16),
        compiler_params=pltpu.CompilerParams(vmem_limit_bytes=VMEM_LIMIT),
        name="output_matmul",
    )(core, *values, own_weight, other_weight)


def flip(block, axis, bits):
    count = lax.axis_size(axis)
    return lax.ppermute(block, axis, [(i, i ^ bits) for i in range(count)])


def to_pieces(values, count):
    groups, rows, _ = values.shape
    if groups == count:
        return values
    return values.transpose(1, 0, 2).reshape(rows, count, -1).transpose(1, 0, 2)


def from_pieces(pieces):
    count, rows, lanes = pieces.shape
    if lanes == LANES:
        return pieces
    return pieces.transpose(1, 0, 2).reshape(rows, -1, LANES).transpose(1, 0, 2)


def swap_layout(values, count):
    moved = lax.all_to_all(to_pieces(values, count), "tensor", 0, 0)
    return from_pieces(moved)


def unpack(packed):
    return jnp.concatenate([packed[..., : 2 * HALF], packed[..., 2 * HALF :]], axis=-2)


def reduce_tokens(grads, core, chips):
    half = grads.shape[0] // 2
    keep = lax.dynamic_slice_in_dim(grads, core * half, half, 0)
    send = lax.dynamic_slice_in_dim(grads, (1 - core) * half, half, 0)
    mine = keep + flip(send, "dp", 1)
    rounded = mine.astype(BF16)
    total = mine
    for r in range(1, chips):
        total = total + flip(rounded, "dp", 2 * r).astype(F32)
    other = flip(total, "dp", 1)
    first = jnp.where(core == 0, total, other)
    second = jnp.where(core == 0, other, total)
    return jnp.concatenate([first, second], axis=0)


def body(gate_pre, up_pre, down_weight, factors, out_grad):
    rows, width = gate_pre.shape
    features = down_weight.shape[1]
    halves = width // HALF
    groups = width // LANES
    local_bits = halves.bit_length() - 1
    cross = FACTORS - local_bits
    count = lax.axis_size("tensor")
    chips = lax.axis_size("dp") // 2
    hp = halves // count
    dp = lax.axis_index("dp")
    tensor = lax.axis_index("tensor")
    core = dp & 1
    chip = dp >> 1

    row_index = jnp.arange(HALF, dtype=jnp.int32)[None, None, :, None]
    col_index = jnp.arange(2 * HALF, dtype=jnp.int32)[None, None, None, :]
    bits = (tensor >> jnp.arange(cross, dtype=jnp.int32)) & 1
    select = col_index == bits[:, None, None, None] * HALF + row_index
    mixing = (factors[local_bits:] + select.astype(F32)).astype(BF16)
    mixing = mixing.reshape(cross, count, hp * HALF, 2 * HALF).transpose(1, 0, 2, 3)
    mixing = mixing.reshape(count, cross * hp * HALF, 2 * HALF)
    middle = cross * hp * HALF // 2
    mixing = jnp.concatenate([mixing[:, :middle], mixing[:, middle:]], axis=-1)
    mixing = lax.all_to_all(mixing, "tensor", 0, 0)
    mixing = jnp.concatenate([mixing[..., : 2 * HALF], mixing[..., 2 * HALF :]], axis=1)
    mixing = mixing.reshape(count, cross, hp * HALF, 2 * HALF).transpose(1, 0, 2, 3)
    mixing = mixing.reshape(cross, groups, LANES, 2 * HALF)

    other_weight = flip(down_weight, "dp", 1)

    def features_of(array, chip_index, core_index):
        return lax.dynamic_slice_in_dim(array, (2 * chip_index + core_index) * features, features, 1)

    grads_here = [(features_of(out_grad, chip, core), features_of(out_grad, chip, 1 - core))]
    for r in range(1, chips):
        there = chip ^ r
        grads_here.append(
            (
                flip(features_of(out_grad, there, core), "dp", 2 * r),
                flip(features_of(out_grad, there, 1 - core), "dp", 2 * r),
            )
        )
    own_grad = jnp.stack([pair[0] for pair in grads_here])
    other_grad = jnp.stack([pair[1] for pair in grads_here])
    kept, sent = back_matmul(own_grad, other_grad, down_weight, other_weight)
    back = kept
    for r in range(1, chips):
        back = back + flip(sent[r - 1], "dp", 2 * r).astype(F32)
    back = back.astype(BF16)

    grouped = factors.reshape(FACTORS, groups, LANES, 2 * HALF)
    saved_local, values = forward_local(gate_pre, up_pre, grouped, local_bits)
    values = swap_layout(values, count)
    strides = [hp * 2**bit for bit in range(cross)]
    saved_cross, values = forward_cross(values, mixing, strides)
    values = swap_layout(values, count)
    all_values = [values] + [flip(values, "dp", 2 * r) for r in range(1, chips)]
    partial = output_matmul(
        all_values, down_weight, other_weight, core.reshape(1).astype(jnp.int32), count
    )
    pieces = lax.all_to_all(partial, "tensor", 0, 0)
    piece = jnp.sum(pieces.astype(F32), axis=0).astype(BF16)
    parts = [piece[0]] + [flip(piece[r], "dp", 2 * r) for r in range(1, chips)]
    stacked = jnp.stack(parts)
    piece = jnp.concatenate(
        [lax.dynamic_index_in_dim(stacked, j ^ chip, 0, keepdims=False) for j in range(chips)],
        axis=1,
    )
    output = lax.all_gather(piece, "tensor", axis=0, tiled=True)

    back = swap_layout(back, count)
    back, grads_cross = backward_cross(back, saved_cross, mixing, strides)
    back = swap_layout(back, count)
    gate_grad, up_grad, grads_local = backward_local(
        back, saved_local, grouped, gate_pre, up_pre, local_bits
    )
    if hp == PER:
        grads_cross = lax.all_to_all(grads_cross.astype(BF16), "tensor", 0, 0).astype(F32)
    else:
        grads_cross = unpack(grads_cross).transpose(1, 0, 2, 3)
        grads_cross = grads_cross.reshape(cross, count, hp * HALF, 2 * HALF).transpose(1, 0, 2, 3)
        grads_cross = lax.all_to_all(grads_cross.astype(BF16), "tensor", 0, 0).astype(F32)
        grads_cross = grads_cross.transpose(1, 0, 2, 3).reshape(cross, groups, LANES, 2 * HALF)
        grads_cross = jnp.concatenate([grads_cross[..., :128, :], grads_cross[..., 128:, :]], axis=-1)
        grads_cross = grads_cross.transpose(1, 0, 2, 3)
    sums = []
    for grads in (grads_local, grads_cross):
        number = grads.shape[1]
        total = reduce_tokens(grads.reshape(groups * number, 128, 128), core, chips)
        sums.append(total.reshape(groups, number, 128, 128))
    total = jnp.concatenate(sums, axis=1).transpose(1, 0, 2, 3)
    scale = 1.0 / math.sqrt(rows * lax.axis_size("dp"))
    factor_grads = (unpack(total) * scale).reshape(factors.shape)
    return (output, gate_grad, up_grad, factor_grads)


def solution(mesh):
    return jax.shard_map(
        body,
        mesh=mesh,
        in_specs=(
            P("dp", "tensor"),
            P("dp", "tensor"),
            P("tensor", "dp"),
            P(None, "tensor", None, None),
            P("dp", None),
        ),
        out_specs=(
            P("dp", None),
            P("dp", "tensor"),
            P("dp", "tensor"),
            P(None, "tensor", None, None),
        ),
        check_vma=False,
    )
```

```python
import functools
import math

import jax
import jax.numpy as jnp
from jax import lax
from jax.experimental import pallas as pl
from jax.experimental.pallas import tpu as pltpu
from jax.sharding import PartitionSpec as P

HALF = 32
FACTORS = 9
LANES = 256
PER = LANES // HALF
VMEM_LIMIT = 48 * 1024 * 1024
F32 = jnp.float32
BF16 = jnp.bfloat16


def iota(shape, axis):
    return lax.broadcasted_iota(jnp.int32, shape, axis)


def with_identity(block, stride, group):
    row = iota((LANES, 2 * HALF), 0)
    col = iota((LANES, 2 * HALF), 1)
    if stride < PER:
        bit = (row // HALF // stride) & 1
    else:
        bit = (group // (stride // PER)) & 1
    select = (col == bit * HALF + (row & (HALF - 1))).astype(F32)
    return (block + select).astype(BF16)


def spread_matrix(depth, bit, offset):
    col = iota((depth, LANES), 0)
    lane = iota((depth, LANES), 1)
    return (col == bit(lane) * HALF + (lane & (HALF - 1)) + offset).astype(BF16)


def expand(mixing, bit):
    depth = mixing.shape[1]
    full = jnp.dot(mixing, spread_matrix(depth, bit, 0), preferred_element_type=F32)
    if depth == 2 * HALF:
        return full
    rest = jnp.dot(mixing, spread_matrix(depth, bit, 2 * HALF), preferred_element_type=F32)
    return jnp.concatenate([full, rest], axis=0)


def inner_matrix(mixing, stride):
    full = expand(mixing, lambda lane: (lane // HALF // stride) & 1)
    row = iota((LANES, LANES), 0) // HALF
    unit = iota((LANES, LANES), 1) // HALF
    mask = (unit == row) | (unit == (row ^ stride))
    return jnp.where(mask, full, 0.0).astype(BF16)


def outer_matrix(mixing, bit):
    full = expand(mixing, lambda lane: bit)
    mask = iota((LANES, LANES), 0) // HALF == iota((LANES, LANES), 1) // HALF
    return jnp.where(mask, full, 0.0).astype(BF16)


def dot_nt(a, b):
    return lax.dot_general(a, b, (((1,), (1,)), ((), ())), preferred_element_type=F32)


def dot_tn(a, b):
    return lax.dot_general(a, b, (((0,), (0,)), ((), ())), preferred_element_type=F32)


def fold(get_tile, columns_of):
    lane = iota((HALF, 128), 1)
    rows = []
    for low in range(PER // 2):
        out = None
        for upper in range(2):
            i = low + upper * (PER // 2)
            for unit_block, source, column in columns_of(i):
                tile = get_tile(source, i, unit_block // 4)
                place = upper * 2 * HALF + column * HALF
                shift = (place - (unit_block % 4) * HALF) % 128
                if shift:
                    tile = pltpu.roll(tile, shift, 1)
                if out is None:
                    out = tile
                else:
                    out = jnp.where((lane >= place) & (lane < place + HALF), tile, out)
        rows.append(out)
    return rows


def apply_forward(values, mixing_of, stride, groups):
    if stride < PER:
        for g in range(groups):
            matrix = inner_matrix(mixing_of(g), stride)
            values[g] = dot_nt(values[g], matrix).astype(BF16)
        return
    step = stride // PER
    for g in range(groups):
        if g & step:
            continue
        h = g | step
        low, high = values[g], values[h]
        for member, bit in ((g, 0), (h, 1)):
            mixing = mixing_of(member)
            new = dot_nt(low, outer_matrix(mixing, 0)) + dot_nt(high, outer_matrix(mixing, 1))
            values[member] = new.astype(BF16)


def apply_backward(grads, inputs, mixing_of, stride, groups, store_grad):
    if stride < PER:
        for g in range(groups):
            matrix = inner_matrix(mixing_of(g), stride)
            grad = grads[g]
            outer = dot_tn(grad, inputs(g))

            def columns_of(i):
                bit = (i // stride) & 1
                return ((i, 0, bit), (i ^ stride, 0, 1 - bit))

            def tile(source, i, part):
                return outer[i * HALF : (i + 1) * HALF, part * 128 : (part + 1) * 128]

            store_grad(g, fold(tile, columns_of))
            grads[g] = jnp.dot(grad, matrix, preferred_element_type=F32).astype(BF16)
        return
    step = stride // PER
    for g in range(groups):
        if g & step:
            continue
        h = g | step
        low, high = inputs(g), inputs(h)
        totals = [None, None]
        for member in (g, h):
            mixing = mixing_of(member)
            grad = grads[member]
            products = (dot_tn(grad, low), dot_tn(grad, high))

            def tile(source, i, part):
                return products[source][i * HALF : (i + 1) * HALF, part * 128 : (part + 1) * 128]

            store_grad(member, fold(tile, lambda i: ((i, 0, 0), (i, 1, 1))))
            for bit in range(2):
                term = jnp.dot(grad, outer_matrix(mixing, bit), preferred_element_type=F32)
                totals[bit] = term if totals[bit] is None else totals[bit] + term
        grads[g] = totals[0].astype(BF16)
        grads[h] = totals[1].astype(BF16)


def forward_local(gate_pre, up_pre, factors, count):
    rows, width = gate_pre.shape
    groups = width // LANES

    def kernel(gate_ref, up_ref, factor_ref, saved_ref, out_ref, values):
        k = pl.program_id(0)

        @pl.when(k == 0)
        def _():
            for g in range(groups):
                cut = pl.ds(g * LANES, LANES)
                gate = gate_ref[:, cut].astype(F32)
                hidden = gate * jax.nn.sigmoid(gate) * up_ref[:, cut].astype(F32)
                values[g] = hidden.astype(BF16)

        for step in range(count):

            @pl.when(k == step)
            def _(step=step):
                saved_ref[0] = values[...]
                stride = 2**step
                apply_forward(
                    values,
                    lambda g: with_identity(factor_ref[0, g], stride, g),
                    stride,
                    groups,
                )

        @pl.when(k == count - 1)
        def _():
            out_ref[...] = values[...]

    shape = (groups, rows, LANES)
    return pl.pallas_call(
        kernel,
        grid=(count,),
        in_specs=[
            pl.BlockSpec((rows, width), lambda k: (0, 0)),
            pl.BlockSpec((rows, width), lambda k: (0, 0)),
            pl.BlockSpec((1, groups, LANES, 2 * HALF), lambda k: (k, 0, 0, 0)),
        ],
        out_specs=[
            pl.BlockSpec((1,) + shape, lambda k: (k, 0, 0, 0)),
            pl.BlockSpec(shape, lambda k: (0, 0, 0)),
        ],
        out_shape=[
            jax.ShapeDtypeStruct((count,) + shape, BF16),
            jax.ShapeDtypeStruct(shape, BF16),
        ],
        scratch_shapes=[pltpu.VMEM(shape, BF16)],
        compiler_params=pltpu.CompilerParams(vmem_limit_bytes=VMEM_LIMIT),
        name="forward_local",
    )(gate_pre, up_pre, factors)


def prepare_mixing(factors, place, local_bits):
    _, groups, _, _ = factors.shape
    cross = factors.shape[0] - local_bits
    half = LANES // 4

    def kernel(place_ref, factor_ref, out_ref):
        k = pl.program_id(0)
        bit = lax.shift_right_logical(place_ref[0], k) & 1
        start = pl.multiple_of(place_ref[1] * half, half)
        row = iota((half, 2 * HALF), 0) & (HALF - 1)
        select = (iota((half, 2 * HALF), 1) == bit * HALF + row).astype(F32)
        for g in range(groups):
            low = factor_ref[0, g, pl.ds(start, half), :] + select
            high = factor_ref[0, g, pl.ds(2 * half + start, half), :] + select
            out_ref[g, 0] = jnp.concatenate([low, high], axis=1).astype(BF16)

    return pl.pallas_call(
        kernel,
        grid_spec=pltpu.PrefetchScalarGridSpec(
            num_scalar_prefetch=1,
            grid=(cross,),
            in_specs=[
                pl.BlockSpec((1, groups, LANES, 2 * HALF), lambda k, c: (local_bits + k, 0, 0, 0))
            ],
            out_specs=pl.BlockSpec((groups, 1, half, 128), lambda k, c: (0, k, 0, 0)),
        ),
        out_shape=jax.ShapeDtypeStruct((groups, cross, half, 128), BF16),
        compiler_params=pltpu.CompilerParams(vmem_limit_bytes=VMEM_LIMIT),
        name="prepare_mixing",
    )(place, factors)


def packed_block(core, own_ref, other_ref, g):
    own, other = own_ref[g, 0], other_ref[g, 0]
    first = jnp.where(core == 0, own, other)
    second = jnp.where(core == 0, other, own)
    return jnp.concatenate([first, second], axis=0)


def store_tiles(grad_ref, core, g, tiles):
    for low, tile in enumerate(tiles):
        row = (low % 2) * HALF
        grad_ref[(low // 2) ^ core, g, 0, row : row + HALF, :] = tile


def forward_cross(values_in, own_mixing, other_mixing, order, strides):
    groups, rows, _ = values_in.shape
    count = len(strides)

    def kernel(order_ref, in_ref, own_ref, other_ref, saved_ref, out_ref, values):
        k = pl.program_id(0)

        @pl.when(k == 0)
        def _():
            values[...] = in_ref[...]

        for step in range(count):

            @pl.when(k == step)
            def _(step=step):
                saved_ref[0] = values[...]
                apply_forward(
                    values,
                    lambda g: packed_block(order_ref[0], own_ref, other_ref, g),
                    strides[step],
                    groups,
                )

        @pl.when(k == count - 1)
        def _():
            out_ref[...] = values[...]

    shape = (groups, rows, LANES)
    mixing_spec = pl.BlockSpec((groups, 1, LANES // 4, 128), lambda k, c: (0, k, 0, 0))
    return pl.pallas_call(
        kernel,
        grid_spec=pltpu.PrefetchScalarGridSpec(
            num_scalar_prefetch=1,
            grid=(count,),
            in_specs=[pl.BlockSpec(shape, lambda k, c: (0, 0, 0)), mixing_spec, mixing_spec],
            out_specs=[
                pl.BlockSpec((1,) + shape, lambda k, c: (k, 0, 0, 0)),
                pl.BlockSpec(shape, lambda k, c: (0, 0, 0)),
            ],
            scratch_shapes=[pltpu.VMEM(shape, BF16)],
        ),
        out_shape=[
            jax.ShapeDtypeStruct((count,) + shape, BF16),
            jax.ShapeDtypeStruct(shape, BF16),
        ],
        compiler_params=pltpu.CompilerParams(vmem_limit_bytes=VMEM_LIMIT),
        name="forward_cross",
    )(order, values_in, own_mixing, other_mixing)


def backward_cross(back, saved, own_mixing, other_mixing, order, strides):
    groups, rows, _ = back.shape
    count = len(strides)
    last = count - 1

    def kernel(order_ref, in_ref, saved_ref, own_ref, other_ref, out_ref, grad_ref, grads):
        k = pl.program_id(0)

        @pl.when(k == 0)
        def _():
            grads[...] = in_ref[...]

        for step in range(count):

            @pl.when(k == step)
            def _(step=step):
                apply_backward(
                    grads,
                    lambda g: saved_ref[0, g],
                    lambda g: packed_block(order_ref[0], own_ref, other_ref, g),
                    strides[last - step],
                    groups,
                    lambda g, tiles: store_tiles(grad_ref, order_ref[1], g, tiles),
                )

        @pl.when(k == last)
        def _():
            out_ref[...] = grads[...]

    shape = (groups, rows, LANES)
    mixing_spec = pl.BlockSpec((groups, 1, LANES // 4, 128), lambda k, c: (0, last - k, 0, 0))
    return pl.pallas_call(
        kernel,
        grid_spec=pltpu.PrefetchScalarGridSpec(
            num_scalar_prefetch=1,
            grid=(count,),
            in_specs=[
                pl.BlockSpec(shape, lambda k, c: (0, 0, 0)),
                pl.BlockSpec((1,) + shape, lambda k, c: (last - k, 0, 0, 0)),
                mixing_spec,
                mixing_spec,
            ],
            out_specs=[
                pl.BlockSpec(shape, lambda k, c: (0, 0, 0)),
                pl.BlockSpec((2, groups, 1, 64, 128), lambda k, c: (0, 0, last - k, 0, 0)),
            ],
            scratch_shapes=[pltpu.VMEM(shape, BF16)],
        ),
        out_shape=[
            jax.ShapeDtypeStruct(shape, BF16),
            jax.ShapeDtypeStruct((2, groups, count, 64, 128), F32),
        ],
        compiler_params=pltpu.CompilerParams(vmem_limit_bytes=VMEM_LIMIT),
        name="backward_cross",
    )(order, back, saved, own_mixing, other_mixing)


def backward_local(back, saved, factors, order, first, end, gate_pre=None, up_pre=None):
    groups, rows, _ = back.shape
    width = groups * LANES
    count = end - first
    final = gate_pre is not None

    def kernel(order_ref, in_ref, saved_ref, factor_ref, *refs):
        if final:
            gate_ref, up_ref, dgate_ref, dup_ref, grad_ref, grads = refs
        else:
            out_ref, grad_ref, grads = refs
        k = pl.program_id(0)

        @pl.when(k == 0)
        def _():
            grads[...] = in_ref[...]

        for step in range(count):

            @pl.when(k == step)
            def _(step=step):
                stride = 2 ** (end - 1 - step)
                apply_backward(
                    grads,
                    lambda g: saved_ref[0, g],
                    lambda g: with_identity(factor_ref[0, g], stride, g),
                    stride,
                    groups,
                    lambda g, tiles: store_tiles(grad_ref, order_ref[1], g, tiles),
                )

        @pl.when(k == count - 1)
        def _():
            if not final:
                out_ref[...] = grads[...]
                return
            for g in range(groups):
                cut = pl.ds(g * LANES, LANES)
                gate = gate_ref[:, cut].astype(F32)
                value = grads[g].astype(F32)
                sig = jax.nn.sigmoid(gate)
                dgate = value * up_ref[:, cut].astype(F32) * sig * (1.0 + gate * (1.0 - sig))
                dgate_ref[:, cut] = dgate.astype(BF16)
                dup_ref[:, cut] = (value * gate * sig).astype(BF16)

    shape = (groups, rows, LANES)
    whole = pl.BlockSpec((rows, width), lambda k, c: (0, 0))
    kept = pl.BlockSpec(shape, lambda k, c: (0, 0, 0))
    whole_shape = jax.ShapeDtypeStruct((rows, width), BF16)
    return pl.pallas_call(
        kernel,
        grid_spec=pltpu.PrefetchScalarGridSpec(
            num_scalar_prefetch=1,
            grid=(count,),
            in_specs=[
                kept,
                pl.BlockSpec((1,) + shape, lambda k, c: (end - 1 - k, 0, 0, 0)),
                pl.BlockSpec((1, groups, LANES, 2 * HALF), lambda k, c: (end - 1 - k, 0, 0, 0)),
            ]
            + ([whole, whole] if final else []),
            out_specs=([whole, whole] if final else [kept])
            + [pl.BlockSpec((2, groups, 1, 64, 128), lambda k, c: (0, 0, count - 1 - k, 0, 0))],
            scratch_shapes=[pltpu.VMEM(shape, BF16)],
        ),
        out_shape=([whole_shape, whole_shape] if final else [jax.ShapeDtypeStruct(shape, BF16)])
        + [jax.ShapeDtypeStruct((2, groups, count, 64, 128), F32)],
        compiler_params=pltpu.CompilerParams(vmem_limit_bytes=VMEM_LIMIT),
        name="backward_local",
    )(order, back, saved, factors, *([gate_pre, up_pre] if final else []))


def place_grads(parts, order, shape, scale, before=None):
    groups = parts[0][1][0].shape[0]
    numbers = [own[0].shape[1] for _, own, _ in parts]
    begins = [sum(numbers[:p]) for p in range(len(parts))]
    steps = sum(numbers)
    firsts = [first for first, _, _ in parts]
    arrays = [array for _, own, other in parts for array in own + other]
    terms = len(parts[0][1])

    def factor_at(k):
        index = firsts[0] + k
        for begin, first in zip(begins[1:], firsts[1:]):
            index = jnp.where(k >= begin, first + k - begin, index)
        return index

    def kernel(order_ref, *refs):
        out_ref = refs[-1]
        k = pl.program_id(0)
        for p in range(len(parts)):
            own = refs[2 * terms * p : 2 * terms * p + terms]
            other = refs[2 * terms * p + terms : 2 * terms * (p + 1)]

            @pl.when((k >= begins[p]) & (k < begins[p] + numbers[p]))
            def _(own=own, other=other):
                for g in range(groups):
                    for members, swap in ((own, 0), (other, 1)):
                        total = members[0][g, 0].astype(F32)
                        for member in members[1:]:
                            total = total + member[g, 0].astype(F32)
                        total = total * scale
                        turned = pltpu.roll(total, 64, 1)
                        start = ((order_ref[1] ^ swap) * 2) + g * PER
                        for low in range(2):
                            row = low * HALF
                            out_ref[0, start + low] = total[row : row + HALF, : 2 * HALF]
                            out_ref[0, start + low + PER // 2] = turned[row : row + HALF, : 2 * HALF]

    def spec(p):
        return pl.BlockSpec(
            (groups, 1, 64, 128),
            lambda k, c: (0, jnp.clip(k - begins[p], 0, numbers[p] - 1), 0, 0),
        )

    in_specs = [spec(p) for p in range(len(parts)) for _ in range(2 * terms)]
    if before is not None:
        in_specs.append(pl.BlockSpec(memory_space=pl.ANY))
        arrays.append(before)
    return pl.pallas_call(
        kernel,
        grid_spec=pltpu.PrefetchScalarGridSpec(
            num_scalar_prefetch=1,
            grid=(steps,),
            in_specs=in_specs,
            out_specs=pl.BlockSpec((1,) + shape[1:], lambda k, c: (factor_at(k), 0, 0, 0)),
        ),
        out_shape=jax.ShapeDtypeStruct(shape, F32),
        input_output_aliases={} if before is None else {len(arrays): 0},
        compiler_params=pltpu.CompilerParams(vmem_limit_bytes=VMEM_LIMIT),
        name="place_grads",
    )(order, *arrays)


def back_matmul(own_grad, other_grad, own_weight, other_weight):
    chips, rows, features = own_grad.shape
    groups = own_weight.shape[0] // LANES

    def kernel(a_ref, b_ref, w_ref, v_ref, keep_ref, send_ref):
        for chip in range(chips):
            total = dot_nt(a_ref[chip], w_ref[...]) + dot_nt(b_ref[chip], v_ref[...])
            if chip == 0:
                keep_ref[0] = total
            else:
                send_ref[chip - 1, 0] = total.astype(BF16)

    grads = pl.BlockSpec((chips, rows, features), lambda g: (0, 0, 0))
    weights = pl.BlockSpec((LANES, features), lambda g: (g, 0))
    return pl.pallas_call(
        kernel,
        grid=(groups,),
        in_specs=[grads, grads, weights, weights],
        out_specs=[
            pl.BlockSpec((1, rows, LANES), lambda g: (g, 0, 0)),
            pl.BlockSpec((chips - 1, 1, rows, LANES), lambda g: (0, g, 0, 0)),
        ],
        out_shape=[
            jax.ShapeDtypeStruct((groups, rows, LANES), F32),
            jax.ShapeDtypeStruct((chips - 1, groups, rows, LANES), BF16),
        ],
        compiler_params=pltpu.CompilerParams(vmem_limit_bytes=VMEM_LIMIT),
        name="back_matmul",
    )(own_grad, other_grad, own_weight, other_weight)


def output_matmul(values, weight, place, pieces):
    chips = len(values)
    groups, rows, _ = values[0].shape
    features = weight.shape[1]
    part = rows // pieces

    def kernel(place_ref, *refs):
        value_refs, w_ref = refs[:chips], refs[chips]
        out_refs, total_ref = refs[chips + 1 : chips + 3], refs[-1]
        for chip in range(chips):
            total = None
            for g in range(groups):
                term = jnp.dot(
                    value_refs[chip][g],
                    w_ref[g * LANES : (g + 1) * LANES, :],
                    preferred_element_type=F32,
                )
                total = term if total is None else total + term
            total_ref[chip] = total.astype(BF16)
            for r in range(pieces):
                start = pl.multiple_of((place_ref[0] ^ r) * part, part)
                out_refs[r % 2][r // 2, chip] = total_ref[chip, pl.ds(start, part), :]

    value_spec = pl.BlockSpec((groups, rows, LANES), lambda j, c: (0, 0, 0))
    out_spec = pl.BlockSpec((pieces // 2, chips, part, LANES), lambda j, c: (0, 0, 0, j))
    out_shape = jax.ShapeDtypeStruct((pieces // 2, chips, part, features), BF16)
    return pl.pallas_call(
        kernel,
        grid_spec=pltpu.PrefetchScalarGridSpec(
            num_scalar_prefetch=1,
            grid=(features // LANES,),
            in_specs=[value_spec] * chips
            + [pl.BlockSpec((groups * LANES, LANES), lambda j, c: (0, j))],
            out_specs=[out_spec, out_spec],
            scratch_shapes=[pltpu.VMEM((chips, rows, LANES), BF16)],
        ),
        out_shape=[out_shape, out_shape],
        compiler_params=pltpu.CompilerParams(vmem_limit_bytes=VMEM_LIMIT),
        name="output_matmul",
    )(place, *values, weight)


def place_output(pieces, place):
    _, chips, part, features = pieces[0].shape
    shape = (len(pieces) * part, 2 * chips * features)

    def kernel(place_ref, *refs):
        out_ref = refs[-1]
        for r, ref in enumerate(refs[:-1]):
            row = pl.multiple_of((place_ref[0] ^ r) * part, part)
            for k in range(2):
                for chip in range(chips):
                    block = (place_ref[1] ^ chip) * 2 + (place_ref[2] ^ k)
                    column = pl.multiple_of(block * features, features)
                    out_ref[pl.ds(row, part), pl.ds(column, features)] = ref[k, chip]

    return pl.pallas_call(
        kernel,
        grid_spec=pltpu.PrefetchScalarGridSpec(
            num_scalar_prefetch=1,
            grid=(1,),
            in_specs=[pl.BlockSpec(piece.shape, lambda k, c: (0, 0, 0, 0)) for piece in pieces],
            out_specs=pl.BlockSpec(shape, lambda k, c: (0, 0)),
        ),
        out_shape=jax.ShapeDtypeStruct(shape, BF16),
        compiler_params=pltpu.CompilerParams(vmem_limit_bytes=VMEM_LIMIT),
        name="place_output",
    )(place, *pieces)


def flip(block, axis, bits):
    count = lax.axis_size(axis)
    return lax.ppermute(block, axis, [(i, i ^ bits) for i in range(count)])


def to_pieces(values, count):
    groups, rows, _ = values.shape
    if groups == count:
        return values
    return values.transpose(1, 0, 2).reshape(rows, count, -1).transpose(1, 0, 2)


def from_pieces(pieces):
    count, rows, lanes = pieces.shape
    if lanes == LANES:
        return pieces
    return pieces.transpose(1, 0, 2).reshape(rows, -1, LANES).transpose(1, 0, 2)


def swap_layout(values, count):
    moved = lax.all_to_all(to_pieces(values, count), "tensor", 0, 0)
    return from_pieces(moved)


def add_pair(a, b):
    return a.astype(F32) + b.astype(F32)


def reduce_tokens(mine, chips):
    own = [mine] + [flip(mine, "dp", 2 * r) for r in range(1, chips)]
    other = [flip(term, "dp", 1) for term in own]
    return own, other


def scatter_sum(kept, sent):
    moved = flip(sent, "tensor", 1)
    sums = [add_pair(kept[z], moved[z]) for z in range(kept.shape[0])]
    total = sums[0]
    for z in range(1, kept.shape[0]):
        total = total + flip(sums[z].astype(BF16), "tensor", 2 * z).astype(F32)
    return total.astype(BF16)


def body(gate_pre, up_pre, down_weight, factors, out_grad):
    rows, width = gate_pre.shape
    features = down_weight.shape[1]
    halves = width // HALF
    groups = width // LANES
    local_bits = halves.bit_length() - 1
    cross = FACTORS - local_bits
    count = lax.axis_size("tensor")
    chips = lax.axis_size("dp") // 2
    hp = halves // count
    dp = lax.axis_index("dp").astype(jnp.int32)
    tensor = lax.axis_index("tensor").astype(jnp.int32)
    core = dp & 1
    chip = dp >> 1
    grouped = factors.reshape(FACTORS, groups, LANES, 2 * HALF)
    aligned = hp == PER
    place = jnp.stack([tensor, chip, core])

    if aligned:
        own_mixing = prepare_mixing(grouped, jnp.stack([tensor, core]), local_bits)
        own_mixing = lax.all_to_all(own_mixing, "tensor", 0, 0)
        other_mixing = flip(own_mixing, "dp", 1)
        order = jnp.stack([core, core])
    else:
        row_index = jnp.arange(HALF, dtype=jnp.int32)[None, None, :, None]
        col_index = jnp.arange(2 * HALF, dtype=jnp.int32)[None, None, None, :]
        bits = (tensor >> jnp.arange(cross, dtype=jnp.int32)) & 1
        select = col_index == bits[:, None, None, None] * HALF + row_index
        mixing = (factors[local_bits:] + select.astype(F32)).astype(BF16)
        mixing = mixing.reshape(cross, count, hp * HALF, 2 * HALF).transpose(1, 0, 2, 3)
        mixing = lax.all_to_all(mixing, "tensor", 0, 0).transpose(1, 0, 2, 3)
        mixing = mixing.reshape(cross, groups, LANES, 2 * HALF).transpose(1, 0, 2, 3)
        mixing = jnp.concatenate([mixing[:, :, :128], mixing[:, :, 128:]], axis=-1)
        own_mixing, other_mixing = mixing[:, :, :64], mixing[:, :, 64:]
        order = jnp.stack([0 * core, core])

    other_weight = flip(down_weight, "dp", 1)

    def features_of(array, chip_index, core_index):
        return lax.dynamic_slice_in_dim(array, (2 * chip_index + core_index) * features, features, 1)

    grads_here = [(features_of(out_grad, chip, core), features_of(out_grad, chip, 1 - core))]
    for r in range(1, chips):
        there = chip ^ r
        grads_here.append(
            (
                flip(features_of(out_grad, there, core), "dp", 2 * r),
                flip(features_of(out_grad, there, 1 - core), "dp", 2 * r),
            )
        )
    own_grad = jnp.stack([pair[0] for pair in grads_here])
    other_grad = jnp.stack([pair[1] for pair in grads_here])
    kept, sent = back_matmul(own_grad, other_grad, down_weight, other_weight)
    received = [flip(sent[r - 1], "dp", 2 * r) for r in range(1, chips)]

    strides = [hp * 2**bit for bit in range(cross)]
    saved_local, values = forward_local(gate_pre, up_pre, grouped, local_bits)
    values = swap_layout(values, count)
    saved_cross, values = forward_cross(values, own_mixing, other_mixing, order, strides)
    values = swap_layout(values, count)
    all_values = [values] + [flip(values, "dp", 2 * r) for r in range(1, chips)]
    received, _ = lax.optimization_barrier((received, values))
    chunks = []
    for weight in (down_weight, other_weight):
        piece = scatter_sum(*output_matmul(all_values, weight, place, count))
        parts = [piece[0]] + [flip(piece[r], "dp", 2 * r) for r in range(1, chips)]
        chunks.append(jnp.stack(parts))
    piece = jnp.stack(chunks)
    pieces = []
    for z in range(count // 2):
        here = piece if z == 0 else flip(piece, "tensor", 2 * z)
        pieces += [here, flip(here, "tensor", 1)]
    output = place_output(pieces, place)

    back = kept
    for term in received:
        back = back + term.astype(F32)
    back = swap_layout(back.astype(BF16), count)
    back, grads_cross = backward_cross(back, saved_cross, own_mixing, other_mixing, order, strides)
    back = swap_layout(back, count)
    middle = local_bits // 2
    back, grads_high = backward_local(back, saved_local, grouped, order, middle, local_bits)
    gate_grad, up_grad, grads_low = backward_local(
        back, saved_local, grouped, order, 0, middle, gate_pre, up_pre
    )

    def over_cores(grads):
        return (grads[0] + flip(grads[1], "dp", 1)).astype(BF16)

    mine = over_cores(grads_cross)
    if aligned:
        mine = lax.all_to_all(mine, "tensor", 0, 0)
    else:
        mine = mine.reshape(groups, cross, 2, HALF, 2, 2 * HALF)
        other = flip(mine, "dp", 1)
        first = jnp.where(core == 0, mine, other)
        second = jnp.where(core == 0, other, mine)
        full = jnp.stack([first, second], axis=2)
        full = full.transpose(1, 0, 5, 2, 3, 4, 6).reshape(cross, count, hp, HALF, 2 * HALF)
        full = lax.all_to_all(full.transpose(1, 0, 2, 3, 4), "tensor", 0, 0)
        full = full.transpose(1, 0, 2, 3, 4).reshape(cross, groups, 2, 2, 2, HALF, 2 * HALF)
        full = full.transpose(1, 0, 3, 4, 5, 2, 6).reshape(groups, cross, 2, 64, 128)
        mine = jnp.where(core == 0, full[:, :, 0], full[:, :, 1])
    scale = 1.0 / math.sqrt(rows * lax.axis_size("dp"))
    parts_cross = (local_bits,) + reduce_tokens(mine, chips)
    parts_high = (middle,) + reduce_tokens(over_cores(grads_high), chips)
    parts_low = (0,) + reduce_tokens(over_cores(grads_low), chips)
    early = place_grads([parts_high, parts_cross], order, factors.shape, scale)
    factor_grads = place_grads([parts_low], order, factors.shape, scale, early)
    return (output, gate_grad, up_grad, factor_grads)


def solution(mesh):
    return jax.shard_map(
        body,
        mesh=mesh,
        in_specs=(
            P("dp", "tensor"),
            P("dp", "tensor"),
            P("tensor", "dp"),
            P(None, "tensor", None, None),
            P("dp", None),
        ),
        out_specs=(
            P("dp", None),
            P("dp", "tensor"),
            P("dp", "tensor"),
            P(None, "tensor", None, None),
        ),
        check_vma=False,
    )
```

```python
import functools
import math

import jax
import jax.numpy as jnp
from jax import lax
from jax.experimental import pallas as pl
from jax.experimental.pallas import tpu as pltpu
from jax.sharding import PartitionSpec as P

HALF = 32
FACTORS = 9
LANES = 256
PER = LANES // HALF
VMEM_LIMIT = 48 * 1024 * 1024


def estimate(microseconds):
    return pl.CostEstimate(flops=0, transcendentals=0, bytes_accessed=int(3.6e6 * microseconds))


F32 = jnp.float32
BF16 = jnp.bfloat16


def iota(shape, axis):
    return lax.broadcasted_iota(jnp.int32, shape, axis)


def with_identity(block, stride, group):
    row = iota((LANES, 2 * HALF), 0)
    col = iota((LANES, 2 * HALF), 1)
    if stride < PER:
        bit = (row // HALF // stride) & 1
    else:
        bit = (group // (stride // PER)) & 1
    select = (col == bit * HALF + (row & (HALF - 1))).astype(F32)
    return (block + select).astype(BF16)


def spread_matrix(depth, bit, offset):
    col = iota((depth, LANES), 0)
    lane = iota((depth, LANES), 1)
    return (col == bit(lane) * HALF + (lane & (HALF - 1)) + offset).astype(BF16)


def expand(mixing, bit):
    depth = mixing.shape[1]
    full = jnp.dot(mixing, spread_matrix(depth, bit, 0), preferred_element_type=F32)
    if depth == 2 * HALF:
        return full
    rest = jnp.dot(mixing, spread_matrix(depth, bit, 2 * HALF), preferred_element_type=F32)
    return jnp.concatenate([full, rest], axis=0)


def inner_matrix(mixing, stride):
    full = expand(mixing, lambda lane: (lane // HALF // stride) & 1)
    row = iota((LANES, LANES), 0) // HALF
    unit = iota((LANES, LANES), 1) // HALF
    mask = (unit == row) | (unit == (row ^ stride))
    return jnp.where(mask, full, 0.0).astype(BF16)


def outer_matrix(mixing, bit):
    full = expand(mixing, lambda lane: bit)
    mask = iota((LANES, LANES), 0) // HALF == iota((LANES, LANES), 1) // HALF
    return jnp.where(mask, full, 0.0).astype(BF16)


def dot_nt(a, b):
    return lax.dot_general(a, b, (((1,), (1,)), ((), ())), preferred_element_type=F32)


def dot_tn(a, b):
    return lax.dot_general(a, b, (((0,), (0,)), ((), ())), preferred_element_type=F32)


def fold(get_tile, columns_of):
    lane = iota((HALF, 128), 1)
    rows = []
    for low in range(PER // 2):
        out = None
        for upper in range(2):
            i = low + upper * (PER // 2)
            for unit_block, source, column in columns_of(i):
                tile = get_tile(source, i, unit_block // 4)
                place = upper * 2 * HALF + column * HALF
                shift = (place - (unit_block % 4) * HALF) % 128
                if shift:
                    tile = pltpu.roll(tile, shift, 1)
                if out is None:
                    out = tile
                else:
                    out = jnp.where((lane >= place) & (lane < place + HALF), tile, out)
        rows.append(out)
    return rows


def apply_forward(values, mixing_of, stride, groups):
    if stride < PER:
        for g in range(groups):
            matrix = inner_matrix(mixing_of(g), stride)
            values[g] = dot_nt(values[g], matrix).astype(BF16)
        return
    step = stride // PER
    for g in range(groups):
        if g & step:
            continue
        h = g | step
        low, high = values[g], values[h]
        for member, bit in ((g, 0), (h, 1)):
            mixing = mixing_of(member)
            new = dot_nt(low, outer_matrix(mixing, 0)) + dot_nt(high, outer_matrix(mixing, 1))
            values[member] = new.astype(BF16)


def apply_backward(grads, inputs, mixing_of, stride, groups, store_grad):
    if stride < PER:
        for g in range(groups):
            matrix = inner_matrix(mixing_of(g), stride)
            grad = grads[g]
            outer = dot_tn(grad, inputs(g))

            def columns_of(i):
                bit = (i // stride) & 1
                return ((i, 0, bit), (i ^ stride, 0, 1 - bit))

            def tile(source, i, part):
                return outer[i * HALF : (i + 1) * HALF, part * 128 : (part + 1) * 128]

            store_grad(g, fold(tile, columns_of))
            grads[g] = jnp.dot(grad, matrix, preferred_element_type=F32).astype(BF16)
        return
    step = stride // PER
    for g in range(groups):
        if g & step:
            continue
        h = g | step
        low, high = inputs(g), inputs(h)
        totals = [None, None]
        for member in (g, h):
            mixing = mixing_of(member)
            grad = grads[member]
            products = (dot_tn(grad, low), dot_tn(grad, high))

            def tile(source, i, part):
                return products[source][i * HALF : (i + 1) * HALF, part * 128 : (part + 1) * 128]

            store_grad(member, fold(tile, lambda i: ((i, 0, 0), (i, 1, 1))))
            for bit in range(2):
                term = jnp.dot(grad, outer_matrix(mixing, bit), preferred_element_type=F32)
                totals[bit] = term if totals[bit] is None else totals[bit] + term
        grads[g] = totals[0].astype(BF16)
        grads[h] = totals[1].astype(BF16)


def forward_local(gate_pre, up_pre, factors, count):
    rows, width = gate_pre.shape
    groups = width // LANES

    def kernel(gate_ref, up_ref, factor_ref, saved_ref, out_ref, values):
        k = pl.program_id(0)

        @pl.when(k == 0)
        def _():
            for g in range(groups):
                cut = pl.ds(g * LANES, LANES)
                gate = gate_ref[:, cut].astype(F32)
                hidden = gate * jax.nn.sigmoid(gate) * up_ref[:, cut].astype(F32)
                values[g] = hidden.astype(BF16)

        for step in range(count):

            @pl.when(k == step)
            def _(step=step):
                saved_ref[0] = values[...]
                stride = 2**step
                apply_forward(
                    values,
                    lambda g: with_identity(factor_ref[0, g], stride, g),
                    stride,
                    groups,
                )

        @pl.when(k == count - 1)
        def _():
            out_ref[...] = values[...]

    shape = (groups, rows, LANES)
    return pl.pallas_call(
        kernel,
        grid=(count,),
        in_specs=[
            pl.BlockSpec((rows, width), lambda k: (0, 0)),
            pl.BlockSpec((rows, width), lambda k: (0, 0)),
            pl.BlockSpec((1, groups, LANES, 2 * HALF), lambda k: (k, 0, 0, 0)),
        ],
        out_specs=[
            pl.BlockSpec((1,) + shape, lambda k: (k, 0, 0, 0)),
            pl.BlockSpec(shape, lambda k: (0, 0, 0)),
        ],
        out_shape=[
            jax.ShapeDtypeStruct((count,) + shape, BF16),
            jax.ShapeDtypeStruct(shape, BF16),
        ],
        scratch_shapes=[pltpu.VMEM(shape, BF16)],
        compiler_params=pltpu.CompilerParams(vmem_limit_bytes=VMEM_LIMIT),
        name="forward_local",
        cost_estimate=estimate(11),
    )(gate_pre, up_pre, factors)


def prepare_mixing(factors, place, local_bits):
    _, groups, _, _ = factors.shape
    cross = factors.shape[0] - local_bits
    half = LANES // 4

    def kernel(place_ref, low_ref, high_ref, out_ref):
        bit = lax.shift_right_logical(place_ref[0], pl.program_id(0)) & 1
        row = iota((half, 2 * HALF), 0) & (HALF - 1)
        select = (iota((half, 2 * HALF), 1) == bit * HALF + row).astype(F32)
        for g in range(groups):
            low = low_ref[0, g] + select
            high = high_ref[0, g] + select
            out_ref[g, 0] = jnp.concatenate([low, high], axis=1).astype(BF16)

    def spec(offset):
        return pl.BlockSpec(
            (1, groups, half, 2 * HALF), lambda k, c: (local_bits + k, 0, c[1] + offset, 0)
        )

    return pl.pallas_call(
        kernel,
        grid_spec=pltpu.PrefetchScalarGridSpec(
            num_scalar_prefetch=1,
            grid=(cross,),
            in_specs=[spec(0), spec(2)],
            out_specs=pl.BlockSpec((groups, 1, half, 128), lambda k, c: (0, k, 0, 0)),
        ),
        out_shape=jax.ShapeDtypeStruct((groups, cross, half, 128), BF16),
        compiler_params=pltpu.CompilerParams(vmem_limit_bytes=VMEM_LIMIT),
        name="prepare_mixing",
        cost_estimate=estimate(3),
    )(place, factors, factors)


def packed_block(core, own_ref, other_ref, g):
    own, other = own_ref[g, 0], other_ref[g, 0]
    first = jnp.where(core == 0, own, other)
    second = jnp.where(core == 0, other, own)
    return jnp.concatenate([first, second], axis=0)


def store_tiles(grad_ref, core, g, tiles):
    for low, tile in enumerate(tiles):
        row = (low % 2) * HALF
        grad_ref[(low // 2) ^ core, g, 0, row : row + HALF, :] = tile


def forward_cross(values_in, own_mixing, other_mixing, order, strides):
    groups, rows, _ = values_in.shape
    count = len(strides)

    def kernel(order_ref, in_ref, own_ref, other_ref, saved_ref, out_ref, values):
        k = pl.program_id(0)

        @pl.when(k == 0)
        def _():
            values[...] = in_ref[...]

        for step in range(count):

            @pl.when(k == step)
            def _(step=step):
                saved_ref[0] = values[...]
                apply_forward(
                    values,
                    lambda g: packed_block(order_ref[0], own_ref, other_ref, g),
                    strides[step],
                    groups,
                )

        @pl.when(k == count - 1)
        def _():
            out_ref[...] = values[...]

    shape = (groups, rows, LANES)
    mixing_spec = pl.BlockSpec((groups, 1, LANES // 4, 128), lambda k, c: (0, k, 0, 0))
    return pl.pallas_call(
        kernel,
        grid_spec=pltpu.PrefetchScalarGridSpec(
            num_scalar_prefetch=1,
            grid=(count,),
            in_specs=[pl.BlockSpec(shape, lambda k, c: (0, 0, 0)), mixing_spec, mixing_spec],
            out_specs=[
                pl.BlockSpec((1,) + shape, lambda k, c: (k, 0, 0, 0)),
                pl.BlockSpec(shape, lambda k, c: (0, 0, 0)),
            ],
            scratch_shapes=[pltpu.VMEM(shape, BF16)],
        ),
        out_shape=[
            jax.ShapeDtypeStruct((count,) + shape, BF16),
            jax.ShapeDtypeStruct(shape, BF16),
        ],
        compiler_params=pltpu.CompilerParams(vmem_limit_bytes=VMEM_LIMIT),
        name="forward_cross",
        cost_estimate=estimate(5),
    )(order, values_in, own_mixing, other_mixing)


def backward_cross(back, saved, own_mixing, other_mixing, order, strides):
    groups, rows, _ = back.shape
    count = len(strides)
    last = count - 1

    def kernel(order_ref, in_ref, saved_ref, own_ref, other_ref, out_ref, grad_ref, grads):
        k = pl.program_id(0)

        @pl.when(k == 0)
        def _():
            grads[...] = in_ref[...]

        for step in range(count):

            @pl.when(k == step)
            def _(step=step):
                apply_backward(
                    grads,
                    lambda g: saved_ref[0, g],
                    lambda g: packed_block(order_ref[0], own_ref, other_ref, g),
                    strides[last - step],
                    groups,
                    lambda g, tiles: store_tiles(grad_ref, order_ref[1], g, tiles),
                )

        @pl.when(k == last)
        def _():
            out_ref[...] = grads[...]

    shape = (groups, rows, LANES)
    mixing_spec = pl.BlockSpec((groups, 1, LANES // 4, 128), lambda k, c: (0, last - k, 0, 0))
    return pl.pallas_call(
        kernel,
        grid_spec=pltpu.PrefetchScalarGridSpec(
            num_scalar_prefetch=1,
            grid=(count,),
            in_specs=[
                pl.BlockSpec(shape, lambda k, c: (0, 0, 0)),
                pl.BlockSpec((1,) + shape, lambda k, c: (last - k, 0, 0, 0)),
                mixing_spec,
                mixing_spec,
            ],
            out_specs=[
                pl.BlockSpec(shape, lambda k, c: (0, 0, 0)),
                pl.BlockSpec((2, groups, 1, 64, 128), lambda k, c: (0, 0, last - k, 0, 0)),
            ],
            scratch_shapes=[pltpu.VMEM(shape, BF16)],
        ),
        out_shape=[
            jax.ShapeDtypeStruct(shape, BF16),
            jax.ShapeDtypeStruct((2, groups, count, 64, 128), F32),
        ],
        compiler_params=pltpu.CompilerParams(vmem_limit_bytes=VMEM_LIMIT),
        name="backward_cross",
        cost_estimate=estimate(9),
    )(order, back, saved, own_mixing, other_mixing)


def backward_local(back, saved, factors, order, first, end, gate_pre=None, up_pre=None):
    groups, rows, _ = back.shape
    width = groups * LANES
    count = end - first
    final = gate_pre is not None

    def kernel(order_ref, in_ref, saved_ref, factor_ref, *refs):
        if final:
            gate_ref, up_ref, dgate_ref, dup_ref, grad_ref, grads = refs
        else:
            out_ref, grad_ref, grads = refs
        k = pl.program_id(0)

        @pl.when(k == 0)
        def _():
            grads[...] = in_ref[...]

        for step in range(count):

            @pl.when(k == step)
            def _(step=step):
                stride = 2 ** (end - 1 - step)
                apply_backward(
                    grads,
                    lambda g: saved_ref[0, g],
                    lambda g: with_identity(factor_ref[0, g], stride, g),
                    stride,
                    groups,
                    lambda g, tiles: store_tiles(grad_ref, order_ref[1], g, tiles),
                )

        @pl.when(k == count - 1)
        def _():
            if not final:
                out_ref[...] = grads[...]
                return
            for g in range(groups):
                cut = pl.ds(g * LANES, LANES)
                gate = gate_ref[:, cut].astype(F32)
                value = grads[g].astype(F32)
                sig = jax.nn.sigmoid(gate)
                dgate = value * up_ref[:, cut].astype(F32) * sig * (1.0 + gate * (1.0 - sig))
                dgate_ref[:, cut] = dgate.astype(BF16)
                dup_ref[:, cut] = (value * gate * sig).astype(BF16)

    shape = (groups, rows, LANES)
    whole = pl.BlockSpec((rows, width), lambda k, c: (0, 0))
    kept = pl.BlockSpec(shape, lambda k, c: (0, 0, 0))
    whole_shape = jax.ShapeDtypeStruct((rows, width), BF16)
    return pl.pallas_call(
        kernel,
        grid_spec=pltpu.PrefetchScalarGridSpec(
            num_scalar_prefetch=1,
            grid=(count,),
            in_specs=[
                kept,
                pl.BlockSpec((1,) + shape, lambda k, c: (end - 1 - k, 0, 0, 0)),
                pl.BlockSpec((1, groups, LANES, 2 * HALF), lambda k, c: (end - 1 - k, 0, 0, 0)),
            ]
            + ([whole, whole] if final else []),
            out_specs=([whole, whole] if final else [kept])
            + [pl.BlockSpec((2, groups, 1, 64, 128), lambda k, c: (0, 0, count - 1 - k, 0, 0))],
            scratch_shapes=[pltpu.VMEM(shape, BF16)],
        ),
        out_shape=([whole_shape, whole_shape] if final else [jax.ShapeDtypeStruct(shape, BF16)])
        + [jax.ShapeDtypeStruct((2, groups, count, 64, 128), F32)],
        compiler_params=pltpu.CompilerParams(vmem_limit_bytes=VMEM_LIMIT),
        name="backward_local",
        cost_estimate=estimate(9),
    )(order, back, saved, factors, *([gate_pre, up_pre] if final else []))


def place_grads(parts, order, shape, scale, before=None):
    groups = parts[0][1][0].shape[0]
    numbers = [own[0].shape[1] for _, own, _ in parts]
    begins = [sum(numbers[:p]) for p in range(len(parts))]
    steps = sum(numbers)
    firsts = [first for first, _, _ in parts]
    arrays = [array for _, own, other in parts for array in own + other]
    terms = len(parts[0][1])

    def factor_at(k):
        index = firsts[0] + k
        for begin, first in zip(begins[1:], firsts[1:]):
            index = jnp.where(k >= begin, first + k - begin, index)
        return index

    def kernel(order_ref, *refs):
        out_ref = refs[-1]
        k = pl.program_id(0)
        for p in range(len(parts)):
            own = refs[2 * terms * p : 2 * terms * p + terms]
            other = refs[2 * terms * p + terms : 2 * terms * (p + 1)]

            @pl.when((k >= begins[p]) & (k < begins[p] + numbers[p]))
            def _(own=own, other=other):
                for g in range(groups):
                    for members, swap in ((own, 0), (other, 1)):
                        total = members[0][g, 0].astype(F32)
                        for member in members[1:]:
                            total = total + member[g, 0].astype(F32)
                        total = total * scale
                        turned = pltpu.roll(total, 64, 1)
                        start = ((order_ref[1] ^ swap) * 2) + g * PER
                        for low in range(2):
                            row = low * HALF
                            out_ref[0, start + low] = total[row : row + HALF, : 2 * HALF]
                            out_ref[0, start + low + PER // 2] = turned[row : row + HALF, : 2 * HALF]

    def spec(p):
        return pl.BlockSpec(
            (groups, 1, 64, 128),
            lambda k, c: (0, jnp.clip(k - begins[p], 0, numbers[p] - 1), 0, 0),
        )

    in_specs = [spec(p) for p in range(len(parts)) for _ in range(2 * terms)]
    if before is not None:
        in_specs.append(pl.BlockSpec(memory_space=pl.ANY))
        arrays.append(before)
    return pl.pallas_call(
        kernel,
        grid_spec=pltpu.PrefetchScalarGridSpec(
            num_scalar_prefetch=1,
            grid=(steps,),
            in_specs=in_specs,
            out_specs=pl.BlockSpec((1,) + shape[1:], lambda k, c: (factor_at(k), 0, 0, 0)),
        ),
        out_shape=jax.ShapeDtypeStruct(shape, F32),
        input_output_aliases={} if before is None else {len(arrays): 0},
        compiler_params=pltpu.CompilerParams(vmem_limit_bytes=VMEM_LIMIT),
        name="place_grads",
        cost_estimate=estimate(4),
    )(order, *arrays)


def back_matmul(out_grad, received, own_weight, other_weight, place):
    rows = out_grad.shape[0]
    features = own_weight.shape[1]
    groups = own_weight.shape[0] // LANES
    others = len(received)

    def kernel(place_ref, a_ref, b_ref, *refs):
        w_ref, v_ref, keep_ref = refs[2 * others], refs[2 * others + 1], refs[2 * others + 2]
        keep_ref[0] = dot_nt(a_ref[...], w_ref[...]) + dot_nt(b_ref[...], v_ref[...])
        for r in range(others):
            total = dot_nt(refs[2 * r][...], w_ref[...]) + dot_nt(refs[2 * r + 1][...], v_ref[...])
            refs[2 * others + 3 + r][0] = total.astype(BF16)

    here = (rows, features)
    weights = pl.BlockSpec((LANES, features), lambda g, c: (g, 0))
    out = pl.BlockSpec((1, rows, LANES), lambda g, c: (g, 0, 0))
    return pl.pallas_call(
        kernel,
        grid_spec=pltpu.PrefetchScalarGridSpec(
            num_scalar_prefetch=1,
            grid=(groups,),
            in_specs=[
                pl.BlockSpec(here, lambda g, c: (0, 2 * c[1] + c[2])),
                pl.BlockSpec(here, lambda g, c: (0, 2 * c[1] + 1 - c[2])),
            ]
            + [
                pl.BlockSpec(here, lambda g, c: (0, c[2])),
                pl.BlockSpec(here, lambda g, c: (0, 1 - c[2])),
            ]
            * others
            + [weights, weights],
            out_specs=[out] * (1 + others),
        ),
        out_shape=[jax.ShapeDtypeStruct((groups, rows, LANES), F32)]
        + [jax.ShapeDtypeStruct((groups, rows, LANES), BF16)] * others,
        compiler_params=pltpu.CompilerParams(vmem_limit_bytes=VMEM_LIMIT),
        name="back_matmul",
        cost_estimate=estimate(9),
    )(place, out_grad, out_grad, *[r for r in received for _ in range(2)], own_weight, other_weight)


def output_matmul(values, own_weight, other_weight, ring):
    chips = len(values)
    groups, rows, _ = values[0].shape
    features = own_weight.shape[1]
    tiles = features // LANES
    pieces = ring.shape[0]
    part = rows // pieces

    def kernel(ring_ref, *refs):
        value_refs, own_ref, other_ref = refs[:chips], refs[chips], refs[chips + 1]
        out_refs, total_ref = refs[chips + 2 : -1], refs[-1]
        j = pl.program_id(0)

        def run(w_ref):
            for chip in range(chips):
                total = None
                for g in range(groups):
                    term = jnp.dot(
                        value_refs[chip][g],
                        w_ref[g * LANES : (g + 1) * LANES, :],
                        preferred_element_type=F32,
                    )
                    total = term if total is None else total + term
                total_ref[chip] = total.astype(BF16)
                for r in range(pieces):
                    start = pl.multiple_of(ring_ref[r] * part, part)
                    out_refs[r][chip] = total_ref[chip, pl.ds(start, part), :]

        @pl.when(j < tiles)
        def _():
            run(own_ref)

        @pl.when(j >= tiles)
        def _():
            run(other_ref)

    value_spec = pl.BlockSpec((groups, rows, LANES), lambda j, c: (0, 0, 0))
    weight_shape = (groups * LANES, LANES)
    return pl.pallas_call(
        kernel,
        grid_spec=pltpu.PrefetchScalarGridSpec(
            num_scalar_prefetch=1,
            grid=(2 * tiles,),
            in_specs=[value_spec] * chips
            + [
                pl.BlockSpec(weight_shape, lambda j, c: (0, jnp.minimum(j, tiles - 1))),
                pl.BlockSpec(weight_shape, lambda j, c: (0, jnp.maximum(j - tiles, 0))),
            ],
            out_specs=[pl.BlockSpec((chips, part, LANES), lambda j, c: (0, 0, j))] * pieces,
            scratch_shapes=[pltpu.VMEM((chips, rows, LANES), BF16)],
        ),
        out_shape=[jax.ShapeDtypeStruct((chips, part, 2 * features), BF16)] * pieces,
        compiler_params=pltpu.CompilerParams(vmem_limit_bytes=VMEM_LIMIT),
        name="output_matmul",
        cost_estimate=estimate(10),
    )(ring, *values, own_weight, other_weight)


def place_output(pieces, ring, place):
    flat = [(r, n, array) for r, cuts in enumerate(pieces) for n, array in enumerate(cuts)]
    chips, part, _ = pieces[0][0].shape
    features = sum(array.shape[2] for array in pieces[0]) // 2
    shape = (len(pieces) * part, 2 * chips * features)

    def kernel(ring_ref, place_ref, *refs):
        out_ref = refs[-1]
        for (r, n, _), ref in zip(flat, refs[:-1]):
            row = pl.multiple_of(ring_ref[r] * part, part)
            width = ref.shape[2]
            for chip in range(chips):
                for k in range(2):
                    begin = max(k * features - n * width, 0)
                    end = min((k + 1) * features - n * width, width)
                    if begin >= end:
                        continue
                    block = (place_ref[1] ^ chip) * 2 + (place_ref[2] ^ k)
                    column = block * features + (n * width + begin - k * features)
                    column = pl.multiple_of(column, 128)
                    out_ref[pl.ds(row, part), pl.ds(column, end - begin)] = ref[chip, :, begin:end]

    return pl.pallas_call(
        kernel,
        grid_spec=pltpu.PrefetchScalarGridSpec(
            num_scalar_prefetch=2,
            grid=(1,),
            in_specs=[pl.BlockSpec(a.shape, lambda k, c, d: (0, 0, 0)) for _, _, a in flat],
            out_specs=pl.BlockSpec(shape, lambda k, c, d: (0, 0)),
        ),
        out_shape=jax.ShapeDtypeStruct(shape, BF16),
        compiler_params=pltpu.CompilerParams(vmem_limit_bytes=VMEM_LIMIT),
        name="place_output",
        cost_estimate=estimate(3),
    )(ring, place, *[array for _, _, array in flat])


def flip(block, axis, bits):
    count = lax.axis_size(axis)
    return lax.ppermute(block, axis, [(i, i ^ bits) for i in range(count)])


def to_pieces(values, count):
    groups, rows, _ = values.shape
    if groups == count:
        return values
    return values.transpose(1, 0, 2).reshape(rows, count, -1).transpose(1, 0, 2)


def from_pieces(pieces):
    count, rows, lanes = pieces.shape
    if lanes == LANES:
        return pieces
    return pieces.transpose(1, 0, 2).reshape(rows, -1, LANES).transpose(1, 0, 2)


def swap_layout(values, count):
    moved = lax.all_to_all(to_pieces(values, count), "tensor", 0, 0)
    return from_pieces(moved)


def add_pair(a, b):
    return a.astype(F32) + b.astype(F32)


def reduce_tokens(mine, chips):
    own = [mine] + [flip(mine, "dp", 2 * r) for r in range(1, chips)]
    other = [flip(term, "dp", 1) for term in own]
    return own, other


def cycle(count):
    return list(range(0, count, 2)) + list(range(count - 1, 0, -2))


def shift(block, order, step):
    pairs = [(order[i], order[(i + step) % len(order)]) for i in range(len(order))]
    return lax.ppermute(block, "tensor", pairs)


def ring_sum(pieces, order):
    count = len(pieces)
    far = count // 2
    cut = pieces[far].shape[2] // 2
    up = shift(pieces[far][:, :, :cut], order, 1)
    down = shift(pieces[far][:, :, cut:], order, -1)
    first = True
    for distance in range(far - 1, 0, -1):
        above, below = pieces[distance], pieces[count - distance]
        if first:
            above = jnp.concatenate(
                [add_pair(above[:, :, :cut], up).astype(BF16), above[:, :, cut:]], axis=2
            )
            below = jnp.concatenate(
                [below[:, :, :cut], add_pair(below[:, :, cut:], down).astype(BF16)], axis=2
            )
        else:
            above = add_pair(above, up).astype(BF16)
            below = add_pair(below, down).astype(BF16)
        first = False
        up = shift(above, order, 1)
        down = shift(below, order, -1)
    return (pieces[0].astype(F32) + up.astype(F32) + down.astype(F32)).astype(BF16)


def ring_gather(piece, order):
    count = len(order)
    far = count // 2
    cut = piece.shape[2] // 2
    result = [None] * count
    result[0] = [piece]
    up = down = piece
    for distance in range(1, far):
        up = shift(up, order, 1)
        down = shift(down, order, -1)
        result[count - distance] = [up]
        result[distance] = [down]
    result[far] = [shift(up[:, :, :cut], order, 1), shift(down[:, :, cut:], order, -1)]
    return result


def body(gate_pre, up_pre, down_weight, factors, out_grad):
    rows, width = gate_pre.shape
    features = down_weight.shape[1]
    halves = width // HALF
    groups = width // LANES
    local_bits = halves.bit_length() - 1
    cross = FACTORS - local_bits
    count = lax.axis_size("tensor")
    chips = lax.axis_size("dp") // 2
    hp = halves // count
    dp = lax.axis_index("dp").astype(jnp.int32)
    tensor = lax.axis_index("tensor").astype(jnp.int32)
    core = dp & 1
    chip = dp >> 1
    grouped = factors.reshape(FACTORS, groups, LANES, 2 * HALF)
    aligned = hp == PER
    place = jnp.stack([tensor, chip, core])

    if aligned:
        own_mixing = prepare_mixing(grouped, jnp.stack([tensor, core]), local_bits)
        own_mixing = lax.all_to_all(own_mixing, "tensor", 0, 0)
        other_mixing = flip(own_mixing, "dp", 1)
        order = jnp.stack([core, core])
    else:
        row_index = jnp.arange(HALF, dtype=jnp.int32)[None, None, :, None]
        col_index = jnp.arange(2 * HALF, dtype=jnp.int32)[None, None, None, :]
        bits = (tensor >> jnp.arange(cross, dtype=jnp.int32)) & 1
        select = col_index == bits[:, None, None, None] * HALF + row_index
        mixing = (factors[local_bits:] + select.astype(F32)).astype(BF16)
        mixing = mixing.reshape(cross, count, hp * HALF, 2 * HALF).transpose(1, 0, 2, 3)
        mixing = lax.all_to_all(mixing, "tensor", 0, 0).transpose(1, 0, 2, 3)
        mixing = mixing.reshape(cross, groups, LANES, 2 * HALF).transpose(1, 0, 2, 3)
        mixing = jnp.concatenate([mixing[:, :, :128], mixing[:, :, 128:]], axis=-1)
        own_mixing, other_mixing = mixing[:, :, :64], mixing[:, :, 64:]
        order = jnp.stack([0 * core, core])

    other_weight = flip(down_weight, "dp", 1)

    crossing = [
        lax.dynamic_slice_in_dim(out_grad, (chip ^ r) * 2 * features, 2 * features, 1)
        for r in range(1, chips)
    ]
    gate_pre, up_pre, crossing = lax.optimization_barrier((gate_pre, up_pre, crossing))
    crossing = [flip(part, "dp", 2 * (r + 1)) for r, part in enumerate(crossing)]

    strides = [hp * 2**bit for bit in range(cross)]
    saved_local, values = forward_local(gate_pre, up_pre, grouped, local_bits)
    values = swap_layout(values, count)
    saved_cross, values = forward_cross(values, own_mixing, other_mixing, order, strides)
    crossing, values = lax.optimization_barrier((crossing, values))
    values = swap_layout(values, count)
    kept, *sent = back_matmul(out_grad, crossing, down_weight, other_weight, place)
    received = [flip(part, "dp", 2 * (r + 1)) for r, part in enumerate(sent)]
    all_values = [values] + [flip(values, "dp", 2 * r) for r in range(1, chips)]
    received, _ = lax.optimization_barrier((received, values))
    back = kept
    for term in received:
        back = back + term.astype(F32)
    back = swap_layout(back.astype(BF16), count)
    back, grads_cross = backward_cross(back, saved_cross, own_mixing, other_mixing, order, strides)
    all_values, back = lax.optimization_barrier((all_values, back))
    circle = cycle(count)
    spot = jnp.argmax(jnp.array(circle, jnp.int32) == tensor).astype(jnp.int32)
    steps = (spot + jnp.arange(count, dtype=jnp.int32)) % count
    ring = jnp.where(steps < count // 2, 2 * steps, 2 * (count - steps) - 1)
    piece = ring_sum(output_matmul(all_values, down_weight, other_weight, ring), circle)
    summed = piece
    piece = jnp.stack([piece[0]] + [flip(piece[r], "dp", 2 * r) for r in range(1, chips)])
    gathered = ring_gather(piece, circle)
    output = place_output(gathered, ring, place)

    back = swap_layout(back, count)
    back, _ = lax.optimization_barrier((back, summed))
    middle = local_bits // 2
    back, grads_high = backward_local(back, saved_local, grouped, order, middle, local_bits)
    back, _ = lax.optimization_barrier((back, [gathered[1], gathered[-1]]))
    gate_grad, up_grad, grads_low = backward_local(
        back, saved_local, grouped, order, 0, middle, gate_pre, up_pre
    )

    def over_cores(grads):
        return (grads[0] + flip(grads[1], "dp", 1)).astype(BF16)

    mine = over_cores(grads_cross)
    if aligned:
        mine = lax.all_to_all(mine, "tensor", 0, 0)
    else:
        mine = mine.reshape(groups, cross, 2, HALF, 2, 2 * HALF)
        other = flip(mine, "dp", 1)
        first = jnp.where(core == 0, mine, other)
        second = jnp.where(core == 0, other, mine)
        full = jnp.stack([first, second], axis=2)
        full = full.transpose(1, 0, 5, 2, 3, 4, 6).reshape(cross, count, hp, HALF, 2 * HALF)
        full = lax.all_to_all(full.transpose(1, 0, 2, 3, 4), "tensor", 0, 0)
        full = full.transpose(1, 0, 2, 3, 4).reshape(cross, groups, 2, 2, 2, HALF, 2 * HALF)
        full = full.transpose(1, 0, 3, 4, 5, 2, 6).reshape(groups, cross, 2, 64, 128)
        mine = jnp.where(core == 0, full[:, :, 0], full[:, :, 1])
    scale = 1.0 / math.sqrt(rows * lax.axis_size("dp"))
    parts_cross = (local_bits,) + reduce_tokens(mine, chips)
    parts_high = (middle,) + reduce_tokens(over_cores(grads_high), chips)
    parts_low = (0,) + reduce_tokens(over_cores(grads_low), chips)
    early = place_grads([parts_high, parts_cross], order, factors.shape, scale)
    factor_grads = place_grads([parts_low], order, factors.shape, scale, early)
    return (output, gate_grad, up_grad, factor_grads)


def solution(mesh):
    return jax.shard_map(
        body,
        mesh=mesh,
        in_specs=(
            P("dp", "tensor"),
            P("dp", "tensor"),
            P("tensor", "dp"),
            P(None, "tensor", None, None),
            P("dp", None),
        ),
        out_specs=(
            P("dp", None),
            P("dp", "tensor"),
            P("dp", "tensor"),
            P(None, "tensor", None, None),
        ),
        check_vma=False,
    )
```

```python
import functools
import math

import jax
import jax.numpy as jnp
from jax import lax
from jax.experimental import pallas as pl
from jax.experimental.pallas import tpu as pltpu
from jax.sharding import PartitionSpec as P

HALF = 32
FACTORS = 9
LANES = 256
PER = LANES // HALF
VMEM_LIMIT = 48 * 1024 * 1024


def estimate(microseconds):
    return pl.CostEstimate(flops=0, transcendentals=0, bytes_accessed=int(3.6e6 * microseconds))


F32 = jnp.float32
BF16 = jnp.bfloat16


def iota(shape, axis):
    return lax.broadcasted_iota(jnp.int32, shape, axis)


def with_identity(block, stride, group):
    row = iota((LANES, 2 * HALF), 0)
    col = iota((LANES, 2 * HALF), 1)
    if stride < PER:
        bit = (row // HALF // stride) & 1
    else:
        bit = (group // (stride // PER)) & 1
    select = (col == bit * HALF + (row & (HALF - 1))).astype(F32)
    return (block + select).astype(BF16)


def spread_matrix(depth, bit, offset):
    col = iota((depth, LANES), 0)
    lane = iota((depth, LANES), 1)
    return (col == bit(lane) * HALF + (lane & (HALF - 1)) + offset).astype(BF16)


def expand(mixing, bit):
    depth = mixing.shape[1]
    full = jnp.dot(mixing, spread_matrix(depth, bit, 0), preferred_element_type=F32)
    if depth == 2 * HALF:
        return full
    rest = jnp.dot(mixing, spread_matrix(depth, bit, 2 * HALF), preferred_element_type=F32)
    return jnp.concatenate([full, rest], axis=0)


def inner_matrix(mixing, stride):
    full = expand(mixing, lambda lane: (lane // HALF // stride) & 1)
    row = iota((LANES, LANES), 0) // HALF
    unit = iota((LANES, LANES), 1) // HALF
    mask = (unit == row) | (unit == (row ^ stride))
    return jnp.where(mask, full, 0.0).astype(BF16)


def outer_matrix(mixing, bit):
    full = expand(mixing, lambda lane: bit)
    mask = iota((LANES, LANES), 0) // HALF == iota((LANES, LANES), 1) // HALF
    return jnp.where(mask, full, 0.0).astype(BF16)


def dot_nt(a, b):
    return lax.dot_general(a, b, (((1,), (1,)), ((), ())), preferred_element_type=F32)


def dot_tn(a, b):
    return lax.dot_general(a, b, (((0,), (0,)), ((), ())), preferred_element_type=F32)


def fold(get_tile, columns_of):
    lane = iota((HALF, 128), 1)
    rows = []
    for low in range(PER // 2):
        out = None
        for upper in range(2):
            i = low + upper * (PER // 2)
            for unit_block, source, column in columns_of(i):
                tile = get_tile(source, i, unit_block // 4)
                place = upper * 2 * HALF + column * HALF
                shift = (place - (unit_block % 4) * HALF) % 128
                if shift:
                    tile = pltpu.roll(tile, shift, 1)
                if out is None:
                    out = tile
                else:
                    out = jnp.where((lane >= place) & (lane < place + HALF), tile, out)
        rows.append(out)
    return rows


def apply_forward(values, mixing_of, stride, groups):
    if stride < PER:
        for g in range(groups):
            matrix = inner_matrix(mixing_of(g), stride)
            values[g] = dot_nt(values[g], matrix).astype(BF16)
        return
    step = stride // PER
    for g in range(groups):
        if g & step:
            continue
        h = g | step
        low, high = values[g], values[h]
        for member, bit in ((g, 0), (h, 1)):
            mixing = mixing_of(member)
            new = dot_nt(low, outer_matrix(mixing, 0)) + dot_nt(high, outer_matrix(mixing, 1))
            values[member] = new.astype(BF16)


def apply_backward(grads, inputs, mixing_of, stride, groups, store_grad):
    if stride < PER:
        for g in range(groups):
            matrix = inner_matrix(mixing_of(g), stride)
            grad = grads[g]
            outer = dot_tn(grad, inputs(g))

            def columns_of(i):
                bit = (i // stride) & 1
                return ((i, 0, bit), (i ^ stride, 0, 1 - bit))

            def tile(source, i, part):
                return outer[i * HALF : (i + 1) * HALF, part * 128 : (part + 1) * 128]

            store_grad(g, fold(tile, columns_of))
            grads[g] = jnp.dot(grad, matrix, preferred_element_type=F32).astype(BF16)
        return
    step = stride // PER
    for g in range(groups):
        if g & step:
            continue
        h = g | step
        low, high = inputs(g), inputs(h)
        totals = [None, None]
        for member in (g, h):
            mixing = mixing_of(member)
            grad = grads[member]
            products = (dot_tn(grad, low), dot_tn(grad, high))

            def tile(source, i, part):
                return products[source][i * HALF : (i + 1) * HALF, part * 128 : (part + 1) * 128]

            store_grad(member, fold(tile, lambda i: ((i, 0, 0), (i, 1, 1))))
            for bit in range(2):
                term = jnp.dot(grad, outer_matrix(mixing, bit), preferred_element_type=F32)
                totals[bit] = term if totals[bit] is None else totals[bit] + term
        grads[g] = totals[0].astype(BF16)
        grads[h] = totals[1].astype(BF16)


def forward_local(gate_pre, up_pre, factors, count):
    rows, width = gate_pre.shape
    groups = width // LANES

    def kernel(gate_ref, up_ref, factor_ref, saved_ref, out_ref, values):
        k = pl.program_id(0)

        @pl.when(k == 0)
        def _():
            for g in range(groups):
                cut = pl.ds(g * LANES, LANES)
                gate = gate_ref[:, cut].astype(F32)
                hidden = gate * jax.nn.sigmoid(gate) * up_ref[:, cut].astype(F32)
                values[g] = hidden.astype(BF16)

        for step in range(count):

            @pl.when(k == step)
            def _(step=step):
                saved_ref[0] = values[...]
                stride = 2**step
                apply_forward(
                    values,
                    lambda g: with_identity(factor_ref[0, g], stride, g),
                    stride,
                    groups,
                )

        @pl.when(k == count - 1)
        def _():
            out_ref[...] = values[...]

    shape = (groups, rows, LANES)
    return pl.pallas_call(
        kernel,
        grid=(count,),
        in_specs=[
            pl.BlockSpec((rows, width), lambda k: (0, 0)),
            pl.BlockSpec((rows, width), lambda k: (0, 0)),
            pl.BlockSpec((1, groups, LANES, 2 * HALF), lambda k: (k, 0, 0, 0)),
        ],
        out_specs=[
            pl.BlockSpec((1,) + shape, lambda k: (k, 0, 0, 0)),
            pl.BlockSpec(shape, lambda k: (0, 0, 0)),
        ],
        out_shape=[
            jax.ShapeDtypeStruct((count,) + shape, BF16),
            jax.ShapeDtypeStruct(shape, BF16),
        ],
        scratch_shapes=[pltpu.VMEM(shape, BF16)],
        compiler_params=pltpu.CompilerParams(vmem_limit_bytes=VMEM_LIMIT),
        name="forward_local",
        cost_estimate=estimate(11),
    )(gate_pre, up_pre, factors)


def prepare_mixing(factors, place, local_bits):
    _, groups, _, _ = factors.shape
    cross = factors.shape[0] - local_bits
    half = LANES // 4

    def kernel(place_ref, low_ref, high_ref, out_ref):
        bit = lax.shift_right_logical(place_ref[0], pl.program_id(0)) & 1
        row = iota((half, 2 * HALF), 0) & (HALF - 1)
        select = (iota((half, 2 * HALF), 1) == bit * HALF + row).astype(F32)
        for g in range(groups):
            low = low_ref[0, g] + select
            high = high_ref[0, g] + select
            out_ref[g, 0] = jnp.concatenate([low, high], axis=1).astype(BF16)

    def spec(offset):
        return pl.BlockSpec(
            (1, groups, half, 2 * HALF), lambda k, c: (local_bits + k, 0, c[1] + offset, 0)
        )

    return pl.pallas_call(
        kernel,
        grid_spec=pltpu.PrefetchScalarGridSpec(
            num_scalar_prefetch=1,
            grid=(cross,),
            in_specs=[spec(0), spec(2)],
            out_specs=pl.BlockSpec((groups, 1, half, 128), lambda k, c: (0, k, 0, 0)),
        ),
        out_shape=jax.ShapeDtypeStruct((groups, cross, half, 128), BF16),
        compiler_params=pltpu.CompilerParams(vmem_limit_bytes=VMEM_LIMIT),
        name="prepare_mixing",
        cost_estimate=estimate(3),
    )(place, factors, factors)


def packed_block(core, own_ref, other_ref, g):
    own, other = own_ref[g, 0], other_ref[g, 0]
    first = jnp.where(core == 0, own, other)
    second = jnp.where(core == 0, other, own)
    return jnp.concatenate([first, second], axis=0)


def store_tiles(grad_ref, core, g, tiles):
    for low, tile in enumerate(tiles):
        row = (low % 2) * HALF
        grad_ref[(low // 2) ^ core, g, 0, row : row + HALF, :] = tile


def forward_cross(values_in, own_mixing, other_mixing, order, strides):
    groups, rows, _ = values_in.shape
    count = len(strides)

    def kernel(order_ref, in_ref, own_ref, other_ref, saved_ref, out_ref, values):
        k = pl.program_id(0)

        @pl.when(k == 0)
        def _():
            values[...] = in_ref[...]

        for step in range(count):

            @pl.when(k == step)
            def _(step=step):
                saved_ref[0] = values[...]
                apply_forward(
                    values,
                    lambda g: packed_block(order_ref[0], own_ref, other_ref, g),
                    strides[step],
                    groups,
                )

        @pl.when(k == count - 1)
        def _():
            out_ref[...] = values[...]

    shape = (groups, rows, LANES)
    mixing_spec = pl.BlockSpec((groups, 1, LANES // 4, 128), lambda k, c: (0, k, 0, 0))
    return pl.pallas_call(
        kernel,
        grid_spec=pltpu.PrefetchScalarGridSpec(
            num_scalar_prefetch=1,
            grid=(count,),
            in_specs=[pl.BlockSpec(shape, lambda k, c: (0, 0, 0)), mixing_spec, mixing_spec],
            out_specs=[
                pl.BlockSpec((1,) + shape, lambda k, c: (k, 0, 0, 0)),
                pl.BlockSpec(shape, lambda k, c: (0, 0, 0)),
            ],
            scratch_shapes=[pltpu.VMEM(shape, BF16)],
        ),
        out_shape=[
            jax.ShapeDtypeStruct((count,) + shape, BF16),
            jax.ShapeDtypeStruct(shape, BF16),
        ],
        compiler_params=pltpu.CompilerParams(vmem_limit_bytes=VMEM_LIMIT),
        name="forward_cross",
        cost_estimate=estimate(5),
    )(order, values_in, own_mixing, other_mixing)


def backward_cross(back, saved, own_mixing, other_mixing, order, strides):
    groups, rows, _ = back.shape
    count = len(strides)
    last = count - 1

    def kernel(order_ref, in_ref, saved_ref, own_ref, other_ref, out_ref, grad_ref, grads):
        k = pl.program_id(0)

        @pl.when(k == 0)
        def _():
            grads[...] = in_ref[...]

        for step in range(count):

            @pl.when(k == step)
            def _(step=step):
                apply_backward(
                    grads,
                    lambda g: saved_ref[0, g],
                    lambda g: packed_block(order_ref[0], own_ref, other_ref, g),
                    strides[last - step],
                    groups,
                    lambda g, tiles: store_tiles(grad_ref, order_ref[1], g, tiles),
                )

        @pl.when(k == last)
        def _():
            out_ref[...] = grads[...]

    shape = (groups, rows, LANES)
    mixing_spec = pl.BlockSpec((groups, 1, LANES // 4, 128), lambda k, c: (0, last - k, 0, 0))
    return pl.pallas_call(
        kernel,
        grid_spec=pltpu.PrefetchScalarGridSpec(
            num_scalar_prefetch=1,
            grid=(count,),
            in_specs=[
                pl.BlockSpec(shape, lambda k, c: (0, 0, 0)),
                pl.BlockSpec((1,) + shape, lambda k, c: (last - k, 0, 0, 0)),
                mixing_spec,
                mixing_spec,
            ],
            out_specs=[
                pl.BlockSpec(shape, lambda k, c: (0, 0, 0)),
                pl.BlockSpec((2, groups, 1, 64, 128), lambda k, c: (0, 0, last - k, 0, 0)),
            ],
            scratch_shapes=[pltpu.VMEM(shape, BF16)],
        ),
        out_shape=[
            jax.ShapeDtypeStruct(shape, BF16),
            jax.ShapeDtypeStruct((2, groups, count, 64, 128), F32),
        ],
        compiler_params=pltpu.CompilerParams(vmem_limit_bytes=VMEM_LIMIT),
        name="backward_cross",
        cost_estimate=estimate(9),
    )(order, back, saved, own_mixing, other_mixing)


def backward_local(back, saved, factors, order, first, end, gate_pre=None, up_pre=None):
    groups, rows, _ = back.shape
    width = groups * LANES
    count = end - first
    final = gate_pre is not None

    def kernel(order_ref, in_ref, saved_ref, factor_ref, *refs):
        if final:
            gate_ref, up_ref, dgate_ref, dup_ref, grad_ref, grads = refs
        else:
            out_ref, grad_ref, grads = refs
        k = pl.program_id(0)

        @pl.when(k == 0)
        def _():
            grads[...] = in_ref[...]

        for step in range(count):

            @pl.when(k == step)
            def _(step=step):
                stride = 2 ** (end - 1 - step)
                apply_backward(
                    grads,
                    lambda g: saved_ref[0, g],
                    lambda g: with_identity(factor_ref[0, g], stride, g),
                    stride,
                    groups,
                    lambda g, tiles: store_tiles(grad_ref, order_ref[1], g, tiles),
                )

        @pl.when(k == count - 1)
        def _():
            if not final:
                out_ref[...] = grads[...]
                return
            for g in range(groups):
                cut = pl.ds(g * LANES, LANES)
                gate = gate_ref[:, cut].astype(F32)
                value = grads[g].astype(F32)
                sig = jax.nn.sigmoid(gate)
                dgate = value * up_ref[:, cut].astype(F32) * sig * (1.0 + gate * (1.0 - sig))
                dgate_ref[:, cut] = dgate.astype(BF16)
                dup_ref[:, cut] = (value * gate * sig).astype(BF16)

    shape = (groups, rows, LANES)
    whole = pl.BlockSpec((rows, width), lambda k, c: (0, 0))
    kept = pl.BlockSpec(shape, lambda k, c: (0, 0, 0))
    whole_shape = jax.ShapeDtypeStruct((rows, width), BF16)
    return pl.pallas_call(
        kernel,
        grid_spec=pltpu.PrefetchScalarGridSpec(
            num_scalar_prefetch=1,
            grid=(count,),
            in_specs=[
                kept,
                pl.BlockSpec((1,) + shape, lambda k, c: (end - 1 - k, 0, 0, 0)),
                pl.BlockSpec((1, groups, LANES, 2 * HALF), lambda k, c: (end - 1 - k, 0, 0, 0)),
            ]
            + ([whole, whole] if final else []),
            out_specs=([whole, whole] if final else [kept])
            + [pl.BlockSpec((2, groups, 1, 64, 128), lambda k, c: (0, 0, count - 1 - k, 0, 0))],
            scratch_shapes=[pltpu.VMEM(shape, BF16)],
        ),
        out_shape=([whole_shape, whole_shape] if final else [jax.ShapeDtypeStruct(shape, BF16)])
        + [jax.ShapeDtypeStruct((2, groups, count, 64, 128), F32)],
        compiler_params=pltpu.CompilerParams(vmem_limit_bytes=VMEM_LIMIT),
        name="backward_local",
        cost_estimate=estimate(9),
    )(order, back, saved, factors, *([gate_pre, up_pre] if final else []))


def place_grads(parts, order, shape, scale, before=None):
    groups = parts[0][1][0].shape[0]
    numbers = [own[0].shape[1] for _, own, _ in parts]
    begins = [sum(numbers[:p]) for p in range(len(parts))]
    steps = sum(numbers)
    firsts = [first for first, _, _ in parts]
    arrays = [array for _, own, other in parts for array in own + other]
    terms = len(parts[0][1])

    def factor_at(k):
        index = firsts[0] + k
        for begin, first in zip(begins[1:], firsts[1:]):
            index = jnp.where(k >= begin, first + k - begin, index)
        return index

    def kernel(order_ref, *refs):
        out_ref = refs[-1]
        k = pl.program_id(0)
        for p in range(len(parts)):
            own = refs[2 * terms * p : 2 * terms * p + terms]
            other = refs[2 * terms * p + terms : 2 * terms * (p + 1)]

            @pl.when((k >= begins[p]) & (k < begins[p] + numbers[p]))
            def _(own=own, other=other):
                for g in range(groups):
                    for members, swap in ((own, 0), (other, 1)):
                        total = members[0][g, 0].astype(F32)
                        for member in members[1:]:
                            total = total + member[g, 0].astype(F32)
                        total = total * scale
                        turned = pltpu.roll(total, 64, 1)
                        start = ((order_ref[1] ^ swap) * 2) + g * PER
                        for low in range(2):
                            row = low * HALF
                            out_ref[0, start + low] = total[row : row + HALF, : 2 * HALF]
                            out_ref[0, start + low + PER // 2] = turned[row : row + HALF, : 2 * HALF]

    def spec(p):
        return pl.BlockSpec(
            (groups, 1, 64, 128),
            lambda k, c: (0, jnp.clip(k - begins[p], 0, numbers[p] - 1), 0, 0),
        )

    in_specs = [spec(p) for p in range(len(parts)) for _ in range(2 * terms)]
    if before is not None:
        in_specs.append(pl.BlockSpec(memory_space=pl.ANY))
        arrays.append(before)
    return pl.pallas_call(
        kernel,
        grid_spec=pltpu.PrefetchScalarGridSpec(
            num_scalar_prefetch=1,
            grid=(steps,),
            in_specs=in_specs,
            out_specs=pl.BlockSpec((1,) + shape[1:], lambda k, c: (factor_at(k), 0, 0, 0)),
        ),
        out_shape=jax.ShapeDtypeStruct(shape, F32),
        input_output_aliases={} if before is None else {len(arrays): 0},
        compiler_params=pltpu.CompilerParams(vmem_limit_bytes=VMEM_LIMIT),
        name="place_grads",
        cost_estimate=estimate(4),
    )(order, *arrays)


def back_matmul(out_grad, received, own_weight, other_weight, place):
    rows = out_grad.shape[0]
    features = own_weight.shape[1]
    groups = own_weight.shape[0] // LANES
    others = len(received)

    def kernel(place_ref, a_ref, b_ref, *refs):
        w_ref, v_ref, keep_ref = refs[2 * others], refs[2 * others + 1], refs[2 * others + 2]
        keep_ref[0] = dot_nt(a_ref[...], w_ref[...]) + dot_nt(b_ref[...], v_ref[...])
        for r in range(others):
            total = dot_nt(refs[2 * r][...], w_ref[...]) + dot_nt(refs[2 * r + 1][...], v_ref[...])
            refs[2 * others + 3 + r][0] = total.astype(BF16)

    here = (rows, features)
    weights = pl.BlockSpec((LANES, features), lambda g, c: (g, 0))
    out = pl.BlockSpec((1, rows, LANES), lambda g, c: (g, 0, 0))
    return pl.pallas_call(
        kernel,
        grid_spec=pltpu.PrefetchScalarGridSpec(
            num_scalar_prefetch=1,
            grid=(groups,),
            in_specs=[
                pl.BlockSpec(here, lambda g, c: (0, 2 * c[1] + c[2])),
                pl.BlockSpec(here, lambda g, c: (0, 2 * c[1] + 1 - c[2])),
            ]
            + [
                pl.BlockSpec(here, lambda g, c: (0, c[2])),
                pl.BlockSpec(here, lambda g, c: (0, 1 - c[2])),
            ]
            * others
            + [weights, weights],
            out_specs=[out] * (1 + others),
        ),
        out_shape=[jax.ShapeDtypeStruct((groups, rows, LANES), F32)]
        + [jax.ShapeDtypeStruct((groups, rows, LANES), BF16)] * others,
        compiler_params=pltpu.CompilerParams(vmem_limit_bytes=VMEM_LIMIT),
        name="back_matmul",
        cost_estimate=estimate(9),
    )(place, out_grad, out_grad, *[r for r in received for _ in range(2)], own_weight, other_weight)


def output_matmul(values, own_weight, other_weight, ring):
    chips = len(values)
    groups, rows, _ = values[0].shape
    features = own_weight.shape[1]
    tiles = features // LANES
    pieces = ring.shape[0]
    part = rows // pieces

    def kernel(ring_ref, *refs):
        value_refs, own_ref, other_ref = refs[:chips], refs[chips], refs[chips + 1]
        out_refs, total_ref = refs[chips + 2 : -1], refs[-1]
        j = pl.program_id(0)

        def run(w_ref):
            for chip in range(chips):
                total = None
                for g in range(groups):
                    term = jnp.dot(
                        value_refs[chip][g],
                        w_ref[g * LANES : (g + 1) * LANES, :],
                        preferred_element_type=F32,
                    )
                    total = term if total is None else total + term
                total_ref[chip] = total.astype(BF16)
                for r in range(pieces):
                    start = pl.multiple_of(ring_ref[r] * part, part)
                    out_refs[r][chip] = total_ref[chip, pl.ds(start, part), :]

        @pl.when(j < tiles)
        def _():
            run(own_ref)

        @pl.when(j >= tiles)
        def _():
            run(other_ref)

    value_spec = pl.BlockSpec((groups, rows, LANES), lambda j, c: (0, 0, 0))
    weight_shape = (groups * LANES, LANES)
    return pl.pallas_call(
        kernel,
        grid_spec=pltpu.PrefetchScalarGridSpec(
            num_scalar_prefetch=1,
            grid=(2 * tiles,),
            in_specs=[value_spec] * chips
            + [
                pl.BlockSpec(weight_shape, lambda j, c: (0, jnp.minimum(j, tiles - 1))),
                pl.BlockSpec(weight_shape, lambda j, c: (0, jnp.maximum(j - tiles, 0))),
            ],
            out_specs=[pl.BlockSpec((chips, part, LANES), lambda j, c: (0, 0, j))] * pieces,
            scratch_shapes=[pltpu.VMEM((chips, rows, LANES), BF16)],
        ),
        out_shape=[jax.ShapeDtypeStruct((chips, part, 2 * features), BF16)] * pieces,
        compiler_params=pltpu.CompilerParams(vmem_limit_bytes=VMEM_LIMIT),
        name="output_matmul",
        cost_estimate=estimate(10),
    )(ring, *values, own_weight, other_weight)


def place_output(pieces, ring, place):
    flat = [(r, n, array) for r, cuts in enumerate(pieces) for n, array in enumerate(cuts)]
    chips, part, _ = pieces[0][0].shape
    features = sum(array.shape[2] for array in pieces[0]) // 2
    shape = (len(pieces) * part, 2 * chips * features)

    def kernel(ring_ref, place_ref, *refs):
        out_ref = refs[-1]
        for (r, n, _), ref in zip(flat, refs[:-1]):
            row = pl.multiple_of(ring_ref[r] * part, part)
            width = ref.shape[2]
            for chip in range(chips):
                for k in range(2):
                    begin = max(k * features - n * width, 0)
                    end = min((k + 1) * features - n * width, width)
                    if begin >= end:
                        continue
                    block = (place_ref[1] ^ chip) * 2 + (place_ref[2] ^ k)
                    column = block * features + (n * width + begin - k * features)
                    column = pl.multiple_of(column, 128)
                    out_ref[pl.ds(row, part), pl.ds(column, end - begin)] = ref[chip, :, begin:end]

    return pl.pallas_call(
        kernel,
        grid_spec=pltpu.PrefetchScalarGridSpec(
            num_scalar_prefetch=2,
            grid=(1,),
            in_specs=[pl.BlockSpec(a.shape, lambda k, c, d: (0, 0, 0)) for _, _, a in flat],
            out_specs=pl.BlockSpec(shape, lambda k, c, d: (0, 0)),
        ),
        out_shape=jax.ShapeDtypeStruct(shape, BF16),
        compiler_params=pltpu.CompilerParams(vmem_limit_bytes=VMEM_LIMIT),
        name="place_output",
        cost_estimate=estimate(3),
    )(ring, place, *[array for _, _, array in flat])


def flip(block, axis, bits):
    count = lax.axis_size(axis)
    return lax.ppermute(block, axis, [(i, i ^ bits) for i in range(count)])


def to_pieces(values, count):
    groups, rows, _ = values.shape
    if groups == count:
        return values
    return values.transpose(1, 0, 2).reshape(rows, count, -1).transpose(1, 0, 2)


def from_pieces(pieces):
    count, rows, lanes = pieces.shape
    if lanes == LANES:
        return pieces
    return pieces.transpose(1, 0, 2).reshape(rows, -1, LANES).transpose(1, 0, 2)


def swap_layout(values, count):
    moved = lax.all_to_all(to_pieces(values, count), "tensor", 0, 0)
    return from_pieces(moved)


def add_pair(a, b):
    return a.astype(F32) + b.astype(F32)


def reduce_tokens(mine, chips, after=()):
    own = [mine] + [flip(mine, "dp", 2 * r) for r in range(1, chips)]
    own, _ = lax.optimization_barrier((own, after))
    other = [flip(term, "dp", 1) for term in own]
    return own, other


def cycle(count):
    return list(range(0, count, 2)) + list(range(count - 1, 0, -2))


def shift(block, order, step):
    pairs = [(order[i], order[(i + step) % len(order)]) for i in range(len(order))]
    return lax.ppermute(block, "tensor", pairs)


def ring_sum(pieces, order, beside):
    count = len(pieces)
    far = count // 2
    cut = pieces[far].shape[2] // 2
    up = shift(pieces[far][:, :, :cut], order, 1)
    down = shift(pieces[far][:, :, cut:], order, -1)
    up, down, beside = lax.optimization_barrier((up, down, beside))
    first = True
    for distance in range(far - 1, 0, -1):
        above, below = pieces[distance], pieces[count - distance]
        if first:
            above = jnp.concatenate(
                [add_pair(above[:, :, :cut], up).astype(BF16), above[:, :, cut:]], axis=2
            )
            below = jnp.concatenate(
                [below[:, :, :cut], add_pair(below[:, :, cut:], down).astype(BF16)], axis=2
            )
        else:
            above = add_pair(above, up).astype(BF16)
            below = add_pair(below, down).astype(BF16)
        first = False
        up = shift(above, order, 1)
        down = shift(below, order, -1)
    total = (pieces[0].astype(F32) + up.astype(F32) + down.astype(F32)).astype(BF16)
    return total, beside


def ring_gather(piece, order, first_work, second_work):
    count = len(order)
    far = count // 2
    cut = piece.shape[2] // 2
    result = [None] * count
    result[0] = [piece]
    up = down = piece
    for distance in range(1, far):
        up = shift(up, order, 1)
        down = shift(down, order, -1)
        if distance == 1:
            up, down, first = lax.optimization_barrier((up, down, first_work()))
        if distance == 2:
            up, down, second = lax.optimization_barrier((up, down, second_work(first)))
        result[count - distance] = [up]
        result[distance] = [down]
    result[far] = [shift(up[:, :, :cut], order, 1), shift(down[:, :, cut:], order, -1)]
    return result, first, second, (up, down)


def body(gate_pre, up_pre, down_weight, factors, out_grad):
    rows, width = gate_pre.shape
    features = down_weight.shape[1]
    halves = width // HALF
    groups = width // LANES
    local_bits = halves.bit_length() - 1
    cross = FACTORS - local_bits
    count = lax.axis_size("tensor")
    chips = lax.axis_size("dp") // 2
    hp = halves // count
    dp = lax.axis_index("dp").astype(jnp.int32)
    tensor = lax.axis_index("tensor").astype(jnp.int32)
    core = dp & 1
    chip = dp >> 1
    grouped = factors.reshape(FACTORS, groups, LANES, 2 * HALF)
    aligned = hp == PER
    place = jnp.stack([tensor, chip, core])

    slices = [
        lax.dynamic_slice_in_dim(out_grad, (chip ^ r) * 2 * features, 2 * features, 1)
        for r in range(1, chips)
    ]
    grouped, slices = lax.optimization_barrier((grouped, slices))

    if aligned:
        own_mixing = prepare_mixing(grouped, jnp.stack([tensor, core]), local_bits)
        own_mixing = lax.all_to_all(own_mixing, "tensor", 0, 0)
        other_mixing = flip(own_mixing, "dp", 1)
        order = jnp.stack([core, core])
    else:
        row_index = jnp.arange(HALF, dtype=jnp.int32)[None, None, :, None]
        col_index = jnp.arange(2 * HALF, dtype=jnp.int32)[None, None, None, :]
        bits = (tensor >> jnp.arange(cross, dtype=jnp.int32)) & 1
        select = col_index == bits[:, None, None, None] * HALF + row_index
        mixing = (factors[local_bits:] + select.astype(F32)).astype(BF16)
        mixing = mixing.reshape(cross, count, hp * HALF, 2 * HALF).transpose(1, 0, 2, 3)
        mixing = lax.all_to_all(mixing, "tensor", 0, 0).transpose(1, 0, 2, 3)
        mixing = mixing.reshape(cross, groups, LANES, 2 * HALF).transpose(1, 0, 2, 3)
        mixing = jnp.concatenate([mixing[:, :, :128], mixing[:, :, 128:]], axis=-1)
        own_mixing, other_mixing = mixing[:, :, :64], mixing[:, :, 64:]
        order = jnp.stack([0 * core, core])

    other_weight = flip(down_weight, "dp", 1)

    strides = [hp * 2**bit for bit in range(cross)]
    crossing = [flip(part, "dp", 2 * (r + 1)) for r, part in enumerate(slices)]
    saved_local, values = forward_local(gate_pre, up_pre, grouped, local_bits)
    values, crossing = lax.optimization_barrier((values, crossing))

    values = swap_layout(values, count)
    kept, *sent = back_matmul(out_grad, crossing, down_weight, other_weight, place)
    received = [flip(part, "dp", 2 * (r + 1)) for r, part in enumerate(sent)]
    values, kept, _ = lax.optimization_barrier((values, kept, sent))
    saved_cross, values = forward_cross(values, own_mixing, other_mixing, order, strides)
    values, received = lax.optimization_barrier((values, received))
    values = swap_layout(values, count)
    back = kept
    for term in received:
        back = back + term.astype(F32)
    back = back.astype(BF16)
    values, back = lax.optimization_barrier((values, back))
    all_values = [values] + [flip(values, "dp", 2 * r) for r in range(1, chips)]
    back = swap_layout(back, count)

    circle = cycle(count)
    spot = jnp.argmax(jnp.array(circle, jnp.int32) == tensor).astype(jnp.int32)
    steps = (spot + jnp.arange(count, dtype=jnp.int32)) % count
    ring = jnp.where(steps < count // 2, 2 * steps, 2 * (count - steps) - 1)
    shares = output_matmul(all_values, down_weight, other_weight, ring)
    back, shares = lax.optimization_barrier((back, shares))
    back, grads_cross = backward_cross(back, saved_cross, own_mixing, other_mixing, order, strides)
    summed, back = ring_sum(shares, circle, back)
    back = swap_layout(back, count)
    piece = jnp.stack([summed[0]] + [flip(summed[r], "dp", 2 * r) for r in range(1, chips)])
    back, _ = lax.optimization_barrier((back, summed))
    middle = local_bits // 2

    def first_half():
        return backward_local(back, saved_local, grouped, order, middle, local_bits)

    def second_half(first):
        return backward_local(
            first[0], saved_local, grouped, order, 0, middle, gate_pre, up_pre
        )

    gathered, first, second, hop = ring_gather(piece, circle, first_half, second_half)
    _, grads_high = first
    gate_grad, up_grad, grads_low = second

    def over_cores(grads):
        return (grads[0] + flip(grads[1], "dp", 1)).astype(BF16)

    mine = over_cores(grads_cross)
    if aligned:
        mine = lax.all_to_all(mine, "tensor", 0, 0)
    else:
        mine = mine.reshape(groups, cross, 2, HALF, 2, 2 * HALF)
        other = flip(mine, "dp", 1)
        first = jnp.where(core == 0, mine, other)
        second = jnp.where(core == 0, other, mine)
        full = jnp.stack([first, second], axis=2)
        full = full.transpose(1, 0, 5, 2, 3, 4, 6).reshape(cross, count, hp, HALF, 2 * HALF)
        full = lax.all_to_all(full.transpose(1, 0, 2, 3, 4), "tensor", 0, 0)
        full = full.transpose(1, 0, 2, 3, 4).reshape(cross, groups, 2, 2, 2, HALF, 2 * HALF)
        full = full.transpose(1, 0, 3, 4, 5, 2, 6).reshape(groups, cross, 2, 64, 128)
        mine = jnp.where(core == 0, full[:, :, 0], full[:, :, 1])
    mine, _ = lax.optimization_barrier((mine, hop))
    scale = 1.0 / math.sqrt(rows * lax.axis_size("dp"))
    parts_cross = (local_bits,) + reduce_tokens(mine, chips)
    parts_high = (middle,) + reduce_tokens(over_cores(grads_high), chips)
    parts_low = (0,) + reduce_tokens(over_cores(grads_low), chips, gathered)
    early = place_grads([parts_high, parts_cross], order, factors.shape, scale)
    gathered, early = lax.optimization_barrier((gathered, early))
    output = place_output(gathered, ring, place)
    factor_grads = place_grads([parts_low], order, factors.shape, scale, early)
    return (output, gate_grad, up_grad, factor_grads)


def solution(mesh):
    return jax.shard_map(
        body,
        mesh=mesh,
        in_specs=(
            P("dp", "tensor"),
            P("dp", "tensor"),
            P("tensor", "dp"),
            P(None, "tensor", None, None),
            P("dp", None),
        ),
        out_specs=(
            P("dp", None),
            P("dp", "tensor"),
            P("dp", "tensor"),
            P(None, "tensor", None, None),
        ),
        check_vma=False,
    )
```

```python
import functools
import math

import jax
import jax.numpy as jnp
from jax import lax
from jax.experimental import pallas as pl
from jax.experimental.pallas import tpu as pltpu
from jax.sharding import PartitionSpec as P

HALF = 32
FACTORS = 9
LANES = 256
PER = LANES // HALF
VMEM_LIMIT = 48 * 1024 * 1024


def estimate(microseconds):
    return pl.CostEstimate(flops=0, transcendentals=0, bytes_accessed=int(3.6e5 * microseconds))


F32 = jnp.float32
BF16 = jnp.bfloat16


def in_hbm(shape, dtype):
    return pltpu.HBM(shape, dtype)


def from_hbm(*arrays):
    return [pltpu.with_memory_space_constraint(array, pltpu.HBM) for array in arrays]


def iota(shape, axis):
    return lax.broadcasted_iota(jnp.int32, shape, axis)


def with_identity(block, stride, group):
    row = iota((LANES, 2 * HALF), 0)
    col = iota((LANES, 2 * HALF), 1)
    if stride < PER:
        bit = (row // HALF // stride) & 1
    else:
        bit = (group // (stride // PER)) & 1
    select = (col == bit * HALF + (row & (HALF - 1))).astype(F32)
    return (block + select).astype(BF16)


def spread_matrix(depth, bit, offset):
    col = iota((depth, LANES), 0)
    lane = iota((depth, LANES), 1)
    return (col == bit(lane) * HALF + (lane & (HALF - 1)) + offset).astype(BF16)


def expand(mixing, bit):
    depth = mixing.shape[1]
    full = jnp.dot(mixing, spread_matrix(depth, bit, 0), preferred_element_type=F32)
    if depth == 2 * HALF:
        return full
    rest = jnp.dot(mixing, spread_matrix(depth, bit, 2 * HALF), preferred_element_type=F32)
    return jnp.concatenate([full, rest], axis=0)


def inner_matrix(mixing, stride):
    full = expand(mixing, lambda lane: (lane // HALF // stride) & 1)
    row = iota((LANES, LANES), 0) // HALF
    unit = iota((LANES, LANES), 1) // HALF
    mask = (unit == row) | (unit == (row ^ stride))
    return jnp.where(mask, full, 0.0).astype(BF16)


def outer_matrix(mixing, bit):
    full = expand(mixing, lambda lane: bit)
    mask = iota((LANES, LANES), 0) // HALF == iota((LANES, LANES), 1) // HALF
    return jnp.where(mask, full, 0.0).astype(BF16)


def dot_nt(a, b):
    return lax.dot_general(a, b, (((1,), (1,)), ((), ())), preferred_element_type=F32)


def dot_tn(a, b):
    return lax.dot_general(a, b, (((0,), (0,)), ((), ())), preferred_element_type=F32)


def fold(get_tile, columns_of):
    lane = iota((HALF, 128), 1)
    rows = []
    for low in range(PER // 2):
        out = None
        for upper in range(2):
            i = low + upper * (PER // 2)
            for unit_block, source, column in columns_of(i):
                tile = get_tile(source, i, unit_block // 4)
                place = upper * 2 * HALF + column * HALF
                shift = (place - (unit_block % 4) * HALF) % 128
                if shift:
                    tile = pltpu.roll(tile, shift, 1)
                if out is None:
                    out = tile
                else:
                    out = jnp.where((lane >= place) & (lane < place + HALF), tile, out)
        rows.append(out)
    return rows


def apply_forward(values, mixing_of, stride, groups):
    if stride < PER:
        for g in range(groups):
            matrix = inner_matrix(mixing_of(g), stride)
            values[g] = dot_nt(values[g], matrix).astype(BF16)
        return
    step = stride // PER
    for g in range(groups):
        if g & step:
            continue
        h = g | step
        low, high = values[g], values[h]
        for member, bit in ((g, 0), (h, 1)):
            mixing = mixing_of(member)
            new = dot_nt(low, outer_matrix(mixing, 0)) + dot_nt(high, outer_matrix(mixing, 1))
            values[member] = new.astype(BF16)


def apply_backward(grads, inputs, mixing_of, stride, groups, store_grad):
    if stride < PER:
        for g in range(groups):
            matrix = inner_matrix(mixing_of(g), stride)
            grad = grads[g]
            outer = dot_tn(grad, inputs(g))

            def columns_of(i):
                bit = (i // stride) & 1
                return ((i, 0, bit), (i ^ stride, 0, 1 - bit))

            def tile(source, i, part):
                return outer[i * HALF : (i + 1) * HALF, part * 128 : (part + 1) * 128]

            store_grad(g, fold(tile, columns_of))
            grads[g] = jnp.dot(grad, matrix, preferred_element_type=F32).astype(BF16)
        return
    step = stride // PER
    for g in range(groups):
        if g & step:
            continue
        h = g | step
        low, high = inputs(g), inputs(h)
        totals = [None, None]
        for member in (g, h):
            mixing = mixing_of(member)
            grad = grads[member]
            products = (dot_tn(grad, low), dot_tn(grad, high))

            def tile(source, i, part):
                return products[source][i * HALF : (i + 1) * HALF, part * 128 : (part + 1) * 128]

            store_grad(member, fold(tile, lambda i: ((i, 0, 0), (i, 1, 1))))
            for bit in range(2):
                term = jnp.dot(grad, outer_matrix(mixing, bit), preferred_element_type=F32)
                totals[bit] = term if totals[bit] is None else totals[bit] + term
        grads[g] = totals[0].astype(BF16)
        grads[h] = totals[1].astype(BF16)


def forward_local(gate_pre, up_pre, factors, count):
    rows, width = gate_pre.shape
    groups = width // LANES

    def kernel(gate_ref, up_ref, factor_ref, saved_ref, out_ref, values):
        k = pl.program_id(0)

        @pl.when(k == 0)
        def _():
            for g in range(groups):
                cut = pl.ds(g * LANES, LANES)
                gate = gate_ref[:, cut].astype(F32)
                hidden = gate * jax.nn.sigmoid(gate) * up_ref[:, cut].astype(F32)
                values[g] = hidden.astype(BF16)

        for step in range(count):

            @pl.when(k == step)
            def _(step=step):
                saved_ref[0] = values[...]
                stride = 2**step
                apply_forward(
                    values,
                    lambda g: with_identity(factor_ref[0, g], stride, g),
                    stride,
                    groups,
                )

        @pl.when(k == count - 1)
        def _():
            out_ref[...] = values[...]

    shape = (groups, rows, LANES)
    return pl.pallas_call(
        kernel,
        grid=(count,),
        in_specs=[
            pl.BlockSpec((rows, width), lambda k: (0, 0)),
            pl.BlockSpec((rows, width), lambda k: (0, 0)),
            pl.BlockSpec((1, groups, LANES, 2 * HALF), lambda k: (k, 0, 0, 0)),
        ],
        out_specs=[
            pl.BlockSpec((1,) + shape, lambda k: (k, 0, 0, 0)),
            pl.BlockSpec(shape, lambda k: (0, 0, 0)),
        ],
        out_shape=[
            in_hbm((count,) + shape, BF16),
            in_hbm(shape, BF16),
        ],
        scratch_shapes=[pltpu.VMEM(shape, BF16)],
        compiler_params=pltpu.CompilerParams(vmem_limit_bytes=VMEM_LIMIT),
        name="forward_local",
        cost_estimate=estimate(11),
    )(*from_hbm(gate_pre, up_pre, factors))


def prepare_mixing(factors, place, local_bits):
    _, groups, _, _ = factors.shape
    cross = factors.shape[0] - local_bits
    half = LANES // 4

    def kernel(place_ref, low_ref, high_ref, out_ref):
        bit = lax.shift_right_logical(place_ref[0], pl.program_id(0)) & 1
        row = iota((half, 2 * HALF), 0) & (HALF - 1)
        select = (iota((half, 2 * HALF), 1) == bit * HALF + row).astype(F32)
        for g in range(groups):
            low = low_ref[0, g] + select
            high = high_ref[0, g] + select
            out_ref[g, 0] = jnp.concatenate([low, high], axis=1).astype(BF16)

    def spec(offset):
        return pl.BlockSpec(
            (1, groups, half, 2 * HALF), lambda k, c: (local_bits + k, 0, c[1] + offset, 0)
        )

    return pl.pallas_call(
        kernel,
        grid_spec=pltpu.PrefetchScalarGridSpec(
            num_scalar_prefetch=1,
            grid=(cross,),
            in_specs=[spec(0), spec(2)],
            out_specs=pl.BlockSpec((groups, 1, half, 128), lambda k, c: (0, k, 0, 0)),
        ),
        out_shape=in_hbm((groups, cross, half, 128), BF16),
        compiler_params=pltpu.CompilerParams(vmem_limit_bytes=VMEM_LIMIT),
        name="prepare_mixing",
        cost_estimate=estimate(3),
    )(place, *from_hbm(factors, factors))


def packed_block(core, own_ref, other_ref, g):
    own, other = own_ref[g, 0], other_ref[g, 0]
    first = jnp.where(core == 0, own, other)
    second = jnp.where(core == 0, other, own)
    return jnp.concatenate([first, second], axis=0)


def store_tiles(grad_ref, core, g, tiles):
    for low, tile in enumerate(tiles):
        row = (low % 2) * HALF
        grad_ref[(low // 2) ^ core, g, 0, row : row + HALF, :] = tile


def forward_cross(values_in, own_mixing, other_mixing, order, strides):
    groups, rows, _ = values_in.shape
    count = len(strides)

    def kernel(order_ref, in_ref, own_ref, other_ref, saved_ref, out_ref, values):
        k = pl.program_id(0)

        @pl.when(k == 0)
        def _():
            values[...] = in_ref[...]

        for step in range(count):

            @pl.when(k == step)
            def _(step=step):
                saved_ref[0] = values[...]
                apply_forward(
                    values,
                    lambda g: packed_block(order_ref[0], own_ref, other_ref, g),
                    strides[step],
                    groups,
                )

        @pl.when(k == count - 1)
        def _():
            out_ref[...] = values[...]

    shape = (groups, rows, LANES)
    mixing_spec = pl.BlockSpec((groups, 1, LANES // 4, 128), lambda k, c: (0, k, 0, 0))
    return pl.pallas_call(
        kernel,
        grid_spec=pltpu.PrefetchScalarGridSpec(
            num_scalar_prefetch=1,
            grid=(count,),
            in_specs=[pl.BlockSpec(shape, lambda k, c: (0, 0, 0)), mixing_spec, mixing_spec],
            out_specs=[
                pl.BlockSpec((1,) + shape, lambda k, c: (k, 0, 0, 0)),
                pl.BlockSpec(shape, lambda k, c: (0, 0, 0)),
            ],
            scratch_shapes=[pltpu.VMEM(shape, BF16)],
        ),
        out_shape=[
            in_hbm((count,) + shape, BF16),
            in_hbm(shape, BF16),
        ],
        compiler_params=pltpu.CompilerParams(vmem_limit_bytes=VMEM_LIMIT),
        name="forward_cross",
        cost_estimate=estimate(5),
    )(order, *from_hbm(values_in, own_mixing, other_mixing))


def backward_cross(back, saved, own_mixing, other_mixing, order, strides):
    groups, rows, _ = back.shape
    count = len(strides)
    last = count - 1

    def kernel(order_ref, in_ref, saved_ref, own_ref, other_ref, out_ref, grad_ref, grads):
        k = pl.program_id(0)

        @pl.when(k == 0)
        def _():
            grads[...] = in_ref[...]

        for step in range(count):

            @pl.when(k == step)
            def _(step=step):
                apply_backward(
                    grads,
                    lambda g: saved_ref[0, g],
                    lambda g: packed_block(order_ref[0], own_ref, other_ref, g),
                    strides[last - step],
                    groups,
                    lambda g, tiles: store_tiles(grad_ref, order_ref[1], g, tiles),
                )

        @pl.when(k == last)
        def _():
            out_ref[...] = grads[...]

    shape = (groups, rows, LANES)
    mixing_spec = pl.BlockSpec((groups, 1, LANES // 4, 128), lambda k, c: (0, last - k, 0, 0))
    return pl.pallas_call(
        kernel,
        grid_spec=pltpu.PrefetchScalarGridSpec(
            num_scalar_prefetch=1,
            grid=(count,),
            in_specs=[
                pl.BlockSpec(shape, lambda k, c: (0, 0, 0)),
                pl.BlockSpec((1,) + shape, lambda k, c: (last - k, 0, 0, 0)),
                mixing_spec,
                mixing_spec,
            ],
            out_specs=[
                pl.BlockSpec(shape, lambda k, c: (0, 0, 0)),
                pl.BlockSpec((2, groups, 1, 64, 128), lambda k, c: (0, 0, last - k, 0, 0)),
            ],
            scratch_shapes=[pltpu.VMEM(shape, BF16)],
        ),
        out_shape=[
            in_hbm(shape, BF16),
            in_hbm((2, groups, count, 64, 128), F32),
        ],
        compiler_params=pltpu.CompilerParams(vmem_limit_bytes=VMEM_LIMIT),
        name="backward_cross",
        cost_estimate=estimate(90),
    )(order, *from_hbm(back, saved, own_mixing, other_mixing))


def backward_local(back, saved, factors, order, first, end, gate_pre=None, up_pre=None):
    groups, rows, _ = back.shape
    width = groups * LANES
    count = end - first
    final = gate_pre is not None

    def kernel(order_ref, in_ref, saved_ref, factor_ref, *refs):
        if final:
            gate_ref, up_ref, dgate_ref, dup_ref, grad_ref, grads = refs
        else:
            out_ref, grad_ref, grads = refs
        k = pl.program_id(0)

        @pl.when(k == 0)
        def _():
            grads[...] = in_ref[...]

        for step in range(count):

            @pl.when(k == step)
            def _(step=step):
                stride = 2 ** (end - 1 - step)
                apply_backward(
                    grads,
                    lambda g: saved_ref[0, g],
                    lambda g: with_identity(factor_ref[0, g], stride, g),
                    stride,
                    groups,
                    lambda g, tiles: store_tiles(grad_ref, order_ref[1], g, tiles),
                )

        @pl.when(k == count - 1)
        def _():
            if not final:
                out_ref[...] = grads[...]
                return
            for g in range(groups):
                cut = pl.ds(g * LANES, LANES)
                gate = gate_ref[:, cut].astype(F32)
                value = grads[g].astype(F32)
                sig = jax.nn.sigmoid(gate)
                dgate = value * up_ref[:, cut].astype(F32) * sig * (1.0 + gate * (1.0 - sig))
                dgate_ref[:, cut] = dgate.astype(BF16)
                dup_ref[:, cut] = (value * gate * sig).astype(BF16)

    shape = (groups, rows, LANES)
    whole = pl.BlockSpec((rows, width), lambda k, c: (0, 0))
    kept = pl.BlockSpec(shape, lambda k, c: (0, 0, 0))
    whole_shape = in_hbm((rows, width), BF16)
    return pl.pallas_call(
        kernel,
        grid_spec=pltpu.PrefetchScalarGridSpec(
            num_scalar_prefetch=1,
            grid=(count,),
            in_specs=[
                kept,
                pl.BlockSpec((1,) + shape, lambda k, c: (end - 1 - k, 0, 0, 0)),
                pl.BlockSpec((1, groups, LANES, 2 * HALF), lambda k, c: (end - 1 - k, 0, 0, 0)),
            ]
            + ([whole, whole] if final else []),
            out_specs=([whole, whole] if final else [kept])
            + [pl.BlockSpec((2, groups, 1, 64, 128), lambda k, c: (0, 0, count - 1 - k, 0, 0))],
            scratch_shapes=[pltpu.VMEM(shape, BF16)],
        ),
        out_shape=([whole_shape, whole_shape] if final else [in_hbm(shape, BF16)])
        + [in_hbm((2, groups, count, 64, 128), F32)],
        compiler_params=pltpu.CompilerParams(vmem_limit_bytes=VMEM_LIMIT),
        name="backward_local",
        cost_estimate=estimate(90),
    )(order, *from_hbm(back, saved, factors, *([gate_pre, up_pre] if final else [])))


def place_grads(parts, order, shape, scale, before=None):
    groups = parts[0][1][0].shape[0]
    numbers = [own[0].shape[1] for _, own, _ in parts]
    begins = [sum(numbers[:p]) for p in range(len(parts))]
    steps = sum(numbers)
    firsts = [first for first, _, _ in parts]
    arrays = [array for _, own, other in parts for array in own + other]
    terms = len(parts[0][1])

    def factor_at(k):
        index = firsts[0] + k
        for begin, first in zip(begins[1:], firsts[1:]):
            index = jnp.where(k >= begin, first + k - begin, index)
        return index

    def kernel(order_ref, *refs):
        out_ref = refs[-1]
        k = pl.program_id(0)
        for p in range(len(parts)):
            own = refs[2 * terms * p : 2 * terms * p + terms]
            other = refs[2 * terms * p + terms : 2 * terms * (p + 1)]

            @pl.when((k >= begins[p]) & (k < begins[p] + numbers[p]))
            def _(own=own, other=other):
                for g in range(groups):
                    for members, swap in ((own, 0), (other, 1)):
                        total = members[0][g, 0].astype(F32)
                        for member in members[1:]:
                            total = total + member[g, 0].astype(F32)
                        total = total * scale
                        turned = pltpu.roll(total, 64, 1)
                        start = ((order_ref[1] ^ swap) * 2) + g * PER
                        for low in range(2):
                            row = low * HALF
                            out_ref[0, start + low] = total[row : row + HALF, : 2 * HALF]
                            out_ref[0, start + low + PER // 2] = turned[row : row + HALF, : 2 * HALF]

    def spec(p):
        return pl.BlockSpec(
            (groups, 1, 64, 128),
            lambda k, c: (0, jnp.clip(k - begins[p], 0, numbers[p] - 1), 0, 0),
        )

    in_specs = [spec(p) for p in range(len(parts)) for _ in range(2 * terms)]
    if before is not None:
        in_specs.append(pl.BlockSpec(memory_space=pl.ANY))
        arrays.append(before)
    return pl.pallas_call(
        kernel,
        grid_spec=pltpu.PrefetchScalarGridSpec(
            num_scalar_prefetch=1,
            grid=(steps,),
            in_specs=in_specs,
            out_specs=pl.BlockSpec((1,) + shape[1:], lambda k, c: (factor_at(k), 0, 0, 0)),
        ),
        out_shape=in_hbm(shape, F32),
        input_output_aliases={} if before is None else {len(arrays): 0},
        compiler_params=pltpu.CompilerParams(vmem_limit_bytes=VMEM_LIMIT),
        name="place_grads",
        cost_estimate=estimate(4),
    )(order, *arrays)


def back_matmul(grads, first, own_weight, other_weight, place, dtype):
    rows = grads.shape[0]
    features = own_weight.shape[1]
    groups = own_weight.shape[0] // LANES

    def kernel(place_ref, a_ref, b_ref, w_ref, v_ref, out_ref):
        out_ref[0] = (dot_nt(a_ref[...], w_ref[...]) + dot_nt(b_ref[...], v_ref[...])).astype(dtype)

    weights = pl.BlockSpec((LANES, features), lambda g, c: (g, 0))
    return pl.pallas_call(
        kernel,
        grid_spec=pltpu.PrefetchScalarGridSpec(
            num_scalar_prefetch=1,
            grid=(groups,),
            in_specs=[
                pl.BlockSpec((rows, features), lambda g, c: (0, first(c) + c[2])),
                pl.BlockSpec((rows, features), lambda g, c: (0, first(c) + 1 - c[2])),
                weights,
                weights,
            ],
            out_specs=pl.BlockSpec((1, rows, LANES), lambda g, c: (g, 0, 0)),
        ),
        out_shape=in_hbm((groups, rows, LANES), dtype),
        compiler_params=pltpu.CompilerParams(vmem_limit_bytes=VMEM_LIMIT),
        name="back_matmul",
        cost_estimate=estimate(5),
    )(place, *from_hbm(grads, grads, own_weight, other_weight))


def output_matmul(values, own_weight, other_weight, ring):
    chips = len(values)
    groups, rows, _ = values[0].shape
    features = own_weight.shape[1]
    tiles = features // LANES
    pieces = ring.shape[0]
    part = rows // pieces

    def kernel(ring_ref, *refs):
        value_refs, own_ref, other_ref = refs[:chips], refs[chips], refs[chips + 1]
        out_refs, total_ref, left_ref = refs[chips + 2 : -2], refs[-2], refs[-1]
        j = pl.program_id(0)

        @pl.when(j == 0)
        def _():
            for chip in range(chips):
                for g in range(groups):
                    left_ref[
                        chip * rows : (chip + 1) * rows, g * LANES : (g + 1) * LANES
                    ] = value_refs[chip][g]

        def run(w_ref):
            total = jnp.dot(left_ref[...], w_ref[...], preferred_element_type=F32).astype(BF16)
            for chip in range(chips):
                total_ref[chip] = total[chip * rows : (chip + 1) * rows]
                for r in range(pieces):
                    start = pl.multiple_of(ring_ref[r] * part, part)
                    out_refs[r][chip] = total_ref[chip, pl.ds(start, part), :]

        @pl.when(j < tiles)
        def _():
            run(own_ref)

        @pl.when(j >= tiles)
        def _():
            run(other_ref)

    value_spec = pl.BlockSpec((groups, rows, LANES), lambda j, c: (0, 0, 0))
    weight_shape = (groups * LANES, LANES)
    return pl.pallas_call(
        kernel,
        grid_spec=pltpu.PrefetchScalarGridSpec(
            num_scalar_prefetch=1,
            grid=(2 * tiles,),
            in_specs=[value_spec] * chips
            + [
                pl.BlockSpec(weight_shape, lambda j, c: (0, jnp.minimum(j, tiles - 1))),
                pl.BlockSpec(weight_shape, lambda j, c: (0, jnp.maximum(j - tiles, 0))),
            ],
            out_specs=[pl.BlockSpec((chips, part, LANES), lambda j, c: (0, 0, j))] * pieces,
            scratch_shapes=[
                pltpu.VMEM((chips, rows, LANES), BF16),
                pltpu.VMEM((chips * rows, groups * LANES), BF16),
            ],
        ),
        out_shape=[in_hbm((chips, part, 2 * features), BF16)] * pieces,
        compiler_params=pltpu.CompilerParams(vmem_limit_bytes=VMEM_LIMIT),
        name="output_matmul",
        cost_estimate=estimate(10),
    )(ring, *from_hbm(*values, own_weight, other_weight))


def place_output(pieces, ring, place):
    flat = [(r, n, array) for r, cuts in enumerate(pieces) for n, array in enumerate(cuts)]
    chips, part, _ = pieces[0][0].shape
    features = sum(array.shape[2] for array in pieces[0]) // 2
    shape = (len(pieces) * part, 2 * chips * features)

    def kernel(ring_ref, place_ref, *refs):
        out_ref = refs[-1]
        for (r, n, _), ref in zip(flat, refs[:-1]):
            row = pl.multiple_of(ring_ref[r] * part, part)
            width = ref.shape[2]
            for chip in range(chips):
                for k in range(2):
                    begin = max(k * features - n * width, 0)
                    end = min((k + 1) * features - n * width, width)
                    if begin >= end:
                        continue
                    block = (place_ref[1] ^ chip) * 2 + (place_ref[2] ^ k)
                    column = block * features + (n * width + begin - k * features)
                    column = pl.multiple_of(column, 128)
                    out_ref[pl.ds(row, part), pl.ds(column, end - begin)] = ref[chip, :, begin:end]

    return pl.pallas_call(
        kernel,
        grid_spec=pltpu.PrefetchScalarGridSpec(
            num_scalar_prefetch=2,
            grid=(1,),
            in_specs=[pl.BlockSpec(a.shape, lambda k, c, d: (0, 0, 0)) for _, _, a in flat],
            out_specs=pl.BlockSpec(shape, lambda k, c, d: (0, 0)),
        ),
        out_shape=in_hbm(shape, BF16),
        compiler_params=pltpu.CompilerParams(vmem_limit_bytes=VMEM_LIMIT),
        name="place_output",
        cost_estimate=estimate(3),
    )(ring, place, *[array for _, _, array in flat])


def flip(block, axis, bits):
    count = lax.axis_size(axis)
    return lax.ppermute(block, axis, [(i, i ^ bits) for i in range(count)])


def to_pieces(values, count):
    groups, rows, _ = values.shape
    if groups == count:
        return values
    return values.transpose(1, 0, 2).reshape(rows, count, -1).transpose(1, 0, 2)


def from_pieces(pieces):
    count, rows, lanes = pieces.shape
    if lanes == LANES:
        return pieces
    return pieces.transpose(1, 0, 2).reshape(rows, -1, LANES).transpose(1, 0, 2)


def swap_layout(values, count):
    moved = lax.all_to_all(to_pieces(values, count), "tensor", 0, 0)
    return from_pieces(moved)


def add_pair(a, b):
    return a.astype(F32) + b.astype(F32)


def over_chips(mine, chips):
    return [mine] + [flip(mine, "dp", 2 * r) for r in range(1, chips)]


def with_other(own):
    return own, [flip(term, "dp", 1) for term in own]


def over_cores(grads):
    return (grads[0] + flip(grads[1], "dp", 1)).astype(BF16)


def to_owners(mine, core, cross, count, hp):
    if hp == PER:
        return lax.all_to_all(mine, "tensor", 0, 0)
    groups = mine.shape[0]
    mine = mine.reshape(groups, cross, 2, HALF, 2, 2 * HALF)
    other = flip(mine, "dp", 1)
    first = jnp.where(core == 0, mine, other)
    second = jnp.where(core == 0, other, mine)
    full = jnp.stack([first, second], axis=2)
    full = full.transpose(1, 0, 5, 2, 3, 4, 6).reshape(cross, count, hp, HALF, 2 * HALF)
    full = lax.all_to_all(full.transpose(1, 0, 2, 3, 4), "tensor", 0, 0)
    full = full.transpose(1, 0, 2, 3, 4).reshape(cross, groups, 2, 2, 2, HALF, 2 * HALF)
    full = full.transpose(1, 0, 3, 4, 5, 2, 6).reshape(groups, cross, 2, 64, 128)
    return jnp.where(core == 0, full[:, :, 0], full[:, :, 1])


def cycle(count):
    return list(range(0, count, 2)) + list(range(count - 1, 0, -2))


def shift(block, order, step):
    pairs = [(order[i], order[(i + step) % len(order)]) for i in range(len(order))]
    return lax.ppermute(block, "tensor", pairs)


def ring_sum(pieces, order, first_work, second_work):
    count = len(pieces)
    far = count // 2
    cut = pieces[far].shape[2] // 2
    up = shift(pieces[far][:, :, :cut], order, 1)
    down = shift(pieces[far][:, :, cut:], order, -1)
    up, down, first = lax.optimization_barrier((up, down, first_work()))
    for distance in range(far - 1, 0, -1):
        above, below = pieces[distance], pieces[count - distance]
        if distance == far - 1:
            above = jnp.concatenate(
                [add_pair(above[:, :, :cut], up).astype(BF16), above[:, :, cut:]], axis=2
            )
            below = jnp.concatenate(
                [below[:, :, :cut], add_pair(below[:, :, cut:], down).astype(BF16)], axis=2
            )
        else:
            above = add_pair(above, up).astype(BF16)
            below = add_pair(below, down).astype(BF16)
        up = shift(above, order, 1)
        down = shift(below, order, -1)
        if distance == far - 1:
            up, down, second = lax.optimization_barrier((up, down, second_work(first)))
    total = (pieces[0].astype(F32) + up.astype(F32) + down.astype(F32)).astype(BF16)
    return total, second


def ring_gather(piece, order):
    count = len(order)
    far = count // 2
    cut = piece.shape[2] // 2
    result = [None] * count
    result[0] = [piece]
    up = down = piece
    for distance in range(1, far):
        up = shift(up, order, 1)
        down = shift(down, order, -1)
        result[count - distance] = [up]
        result[distance] = [down]
    result[far] = [shift(up[:, :, :cut], order, 1), shift(down[:, :, cut:], order, -1)]
    return result


def body(gate_pre, up_pre, down_weight, factors, out_grad):
    rows, width = gate_pre.shape
    features = down_weight.shape[1]
    halves = width // HALF
    groups = width // LANES
    local_bits = halves.bit_length() - 1
    cross = FACTORS - local_bits
    count = lax.axis_size("tensor")
    chips = lax.axis_size("dp") // 2
    hp = halves // count
    dp = lax.axis_index("dp").astype(jnp.int32)
    tensor = lax.axis_index("tensor").astype(jnp.int32)
    core = dp & 1
    chip = dp >> 1
    grouped = factors.reshape(FACTORS, groups, LANES, 2 * HALF)
    aligned = hp == PER
    place = jnp.stack([tensor, chip, core])

    slices = [
        lax.dynamic_slice_in_dim(out_grad, (chip ^ r) * 2 * features, 2 * features, 1)
        for r in range(1, chips)
    ]
    grouped, slices = lax.optimization_barrier((grouped, slices))

    if aligned:
        own_mixing = prepare_mixing(grouped, jnp.stack([tensor, core]), local_bits)
        own_mixing = lax.all_to_all(own_mixing, "tensor", 0, 0)
        other_mixing = flip(own_mixing, "dp", 1)
        order = jnp.stack([core, core])
    else:
        row_index = jnp.arange(HALF, dtype=jnp.int32)[None, None, :, None]
        col_index = jnp.arange(2 * HALF, dtype=jnp.int32)[None, None, None, :]
        bits = (tensor >> jnp.arange(cross, dtype=jnp.int32)) & 1
        select = col_index == bits[:, None, None, None] * HALF + row_index
        mixing = (factors[local_bits:] + select.astype(F32)).astype(BF16)
        mixing = mixing.reshape(cross, count, hp * HALF, 2 * HALF).transpose(1, 0, 2, 3)
        mixing = lax.all_to_all(mixing, "tensor", 0, 0).transpose(1, 0, 2, 3)
        mixing = mixing.reshape(cross, groups, LANES, 2 * HALF).transpose(1, 0, 2, 3)
        mixing = jnp.concatenate([mixing[:, :, :128], mixing[:, :, 128:]], axis=-1)
        own_mixing, other_mixing = mixing[:, :, :64], mixing[:, :, 64:]
        order = jnp.stack([0 * core, core])

    other_weight = flip(down_weight, "dp", 1)

    strides = [hp * 2**bit for bit in range(cross)]
    crossing = [flip(part, "dp", 2 * (r + 1)) for r, part in enumerate(slices)]
    saved_local, values = forward_local(gate_pre, up_pre, grouped, local_bits)
    values, crossing = lax.optimization_barrier((values, crossing))

    values = swap_layout(values, count)
    sent = [
        back_matmul(part, lambda c: 0, down_weight, other_weight, place, BF16) for part in crossing
    ]
    received = [flip(part, "dp", 2 * (r + 1)) for r, part in enumerate(sent)]
    values, _ = lax.optimization_barrier((values, sent))
    saved_cross, values = forward_cross(values, own_mixing, other_mixing, order, strides)
    out_grad, _ = lax.optimization_barrier((out_grad, sent))
    back = back_matmul(out_grad, lambda c: 2 * c[1], down_weight, other_weight, place, F32)
    for term in received:
        back = back + term.astype(F32)
    back = swap_layout(back.astype(BF16), count)
    values, back = lax.optimization_barrier((values, back))
    values = swap_layout(values, count)
    back, grads_cross = backward_cross(back, saved_cross, own_mixing, other_mixing, order, strides)
    values, back = lax.optimization_barrier((values, back))
    all_values = [values] + [flip(values, "dp", 2 * r) for r in range(1, chips)]
    back = swap_layout(back, count)

    circle = cycle(count)
    spot = jnp.argmax(jnp.array(circle, jnp.int32) == tensor).astype(jnp.int32)
    steps = (spot + jnp.arange(count, dtype=jnp.int32)) % count
    ring = jnp.where(steps < count // 2, 2 * steps, 2 * (count - steps) - 1)
    mine_cross = over_cores(grads_cross)
    all_values, mine_cross = lax.optimization_barrier((all_values, mine_cross))
    shares = output_matmul(all_values, down_weight, other_weight, ring)
    back, shares, mine_cross = lax.optimization_barrier((back, shares, mine_cross))
    mine_cross = to_owners(mine_cross, core, cross, count, hp)
    middle = local_bits // 2

    def first_half():
        return backward_local(back, saved_local, grouped, order, middle, local_bits)

    def second_half(first):
        lower, grads = first
        results = backward_local(lower, saved_local, grouped, order, 0, middle, gate_pre, up_pre)
        return results, mine_cross, (grads[0], flip(grads[1], "dp", 1))

    summed, second = ring_sum(shares, circle, first_half, second_half)
    (gate_grad, up_grad, grads_low), mine_cross, high_pair = second
    mine_high = (high_pair[0] + high_pair[1]).astype(BF16)
    piece = jnp.stack([summed[0]] + [flip(summed[r], "dp", 2 * r) for r in range(1, chips)])
    gathered = ring_gather(piece, circle)

    scale = 1.0 / math.sqrt(rows * lax.axis_size("dp"))
    parts_cross = (local_bits,) + with_other(over_chips(mine_cross, chips))
    parts_high = (middle,) + with_other(over_chips(mine_high, chips))
    parts_low = (0,) + with_other(over_chips(over_cores(grads_low), chips))
    early = place_grads([parts_high, parts_cross], order, factors.shape, scale)
    output = place_output(gathered, ring, place)
    factor_grads = place_grads([parts_low], order, factors.shape, scale, early)
    return (output, gate_grad, up_grad, factor_grads)


def solution(mesh):
    return jax.shard_map(
        body,
        mesh=mesh,
        in_specs=(
            P("dp", "tensor"),
            P("dp", "tensor"),
            P("tensor", "dp"),
            P(None, "tensor", None, None),
            P("dp", None),
        ),
        out_specs=(
            P("dp", None),
            P("dp", "tensor"),
            P("dp", "tensor"),
            P(None, "tensor", None, None),
        ),
        check_vma=False,
    )
```

```python
import functools
import math

import jax
import jax.numpy as jnp
from jax import lax
from jax.experimental import pallas as pl
from jax.experimental.pallas import tpu as pltpu
from jax.sharding import PartitionSpec as P

HALF = 32
FACTORS = 9
LANES = 256
PER = LANES // HALF
VMEM_LIMIT = 48 * 1024 * 1024


def estimate(microseconds):
    return pl.CostEstimate(flops=0, transcendentals=0, bytes_accessed=int(3.6e5 * microseconds))


F32 = jnp.float32
BF16 = jnp.bfloat16


def in_hbm(shape, dtype):
    return pltpu.HBM(shape, dtype)


def from_hbm(*arrays):
    return [pltpu.with_memory_space_constraint(array, pltpu.HBM) for array in arrays]


def iota(shape, axis):
    return lax.broadcasted_iota(jnp.int32, shape, axis)


def with_identity(block, stride, group):
    row = iota((LANES, 2 * HALF), 0)
    col = iota((LANES, 2 * HALF), 1)
    if stride < PER:
        bit = (row // HALF // stride) & 1
    else:
        bit = (group // (stride // PER)) & 1
    select = (col == bit * HALF + (row & (HALF - 1))).astype(F32)
    return (block + select).astype(BF16)


def spread_matrix(depth, bit, offset):
    col = iota((depth, LANES), 0)
    lane = iota((depth, LANES), 1)
    return (col == bit(lane) * HALF + (lane & (HALF - 1)) + offset).astype(BF16)


def expand(mixing, bit):
    depth = mixing.shape[1]
    full = jnp.dot(mixing, spread_matrix(depth, bit, 0), preferred_element_type=F32)
    if depth == 2 * HALF:
        return full
    rest = jnp.dot(mixing, spread_matrix(depth, bit, 2 * HALF), preferred_element_type=F32)
    return jnp.concatenate([full, rest], axis=0)


def inner_matrix(mixing, stride):
    full = expand(mixing, lambda lane: (lane // HALF // stride) & 1)
    row = iota((LANES, LANES), 0) // HALF
    unit = iota((LANES, LANES), 1) // HALF
    mask = (unit == row) | (unit == (row ^ stride))
    return jnp.where(mask, full, 0.0).astype(BF16)


def outer_matrix(mixing):
    full = jnp.concatenate([expand(mixing, lambda lane: bit) for bit in range(2)], axis=1)
    row = iota((LANES, 2 * LANES), 0) // HALF
    unit = (iota((LANES, 2 * LANES), 1) & (LANES - 1)) // HALF
    return jnp.where(row == unit, full, 0.0).astype(BF16)


def dot_nt(a, b):
    return lax.dot_general(a, b, (((1,), (1,)), ((), ())), preferred_element_type=F32)


def dot_tn(a, b):
    return lax.dot_general(a, b, (((0,), (0,)), ((), ())), preferred_element_type=F32)


def fold(get_tile, columns_of):
    lane = iota((HALF, 128), 1)
    rows = []
    for low in range(PER // 2):
        out = None
        for upper in range(2):
            i = low + upper * (PER // 2)
            for unit_block, source, column in columns_of(i):
                tile = get_tile(source, i, unit_block // 4)
                place = upper * 2 * HALF + column * HALF
                shift = (place - (unit_block % 4) * HALF) % 128
                if shift:
                    tile = pltpu.roll(tile, shift, 1)
                if out is None:
                    out = tile
                else:
                    out = jnp.where((lane >= place) & (lane < place + HALF), tile, out)
        rows.append(out)
    return rows


def apply_forward(values, mixing_of, stride, groups):
    if stride < PER:
        for g in range(groups):
            matrix = inner_matrix(mixing_of(g), stride)
            values[g] = dot_nt(values[g], matrix).astype(BF16)
        return
    step = stride // PER
    for g in range(groups):
        if g & step:
            continue
        h = g | step
        pair = jnp.concatenate([values[g], values[h]], axis=1)
        for member in (g, h):
            new = dot_nt(pair, outer_matrix(mixing_of(member)))
            values[member] = new.astype(BF16)


def apply_backward(grads, inputs, mixing_of, stride, groups, store_grad):
    if stride < PER:
        for g in range(groups):
            matrix = inner_matrix(mixing_of(g), stride)
            grad = grads[g]
            outer = dot_tn(grad, inputs(g))

            def columns_of(i):
                bit = (i // stride) & 1
                return ((i, 0, bit), (i ^ stride, 0, 1 - bit))

            def tile(source, i, part):
                return outer[i * HALF : (i + 1) * HALF, part * 128 : (part + 1) * 128]

            store_grad(g, fold(tile, columns_of))
            grads[g] = jnp.dot(grad, matrix, preferred_element_type=F32).astype(BF16)
        return
    step = stride // PER
    for g in range(groups):
        if g & step:
            continue
        h = g | step
        pair = jnp.concatenate([inputs(g), inputs(h)], axis=1)
        total = None
        for member in (g, h):
            grad = grads[member]
            product = dot_tn(grad, pair)

            def tile(source, i, part):
                column = source * LANES + part * 128
                return product[i * HALF : (i + 1) * HALF, column : column + 128]

            store_grad(member, fold(tile, lambda i: ((i, 0, 0), (i, 1, 1))))
            term = jnp.dot(grad, outer_matrix(mixing_of(member)), preferred_element_type=F32)
            total = term if total is None else total + term
        grads[g] = total[:, :LANES].astype(BF16)
        grads[h] = total[:, LANES:].astype(BF16)


def forward_local(gate_pre, up_pre, factors, count):
    rows, width = gate_pre.shape
    groups = width // LANES

    def kernel(gate_ref, up_ref, factor_ref, saved_ref, out_ref, values):
        k = pl.program_id(0)

        @pl.when(k == 0)
        def _():
            for g in range(groups):
                cut = pl.ds(g * LANES, LANES)
                gate = gate_ref[:, cut].astype(F32)
                hidden = gate * jax.nn.sigmoid(gate) * up_ref[:, cut].astype(F32)
                values[g] = hidden.astype(BF16)

        for step in range(count):

            @pl.when(k == step)
            def _(step=step):
                saved_ref[0] = values[...]
                stride = 2**step
                apply_forward(
                    values,
                    lambda g: with_identity(factor_ref[0, g], stride, g),
                    stride,
                    groups,
                )

        @pl.when(k == count - 1)
        def _():
            out_ref[...] = values[...]

    shape = (groups, rows, LANES)
    return pl.pallas_call(
        kernel,
        grid=(count,),
        in_specs=[
            pl.BlockSpec((rows, width), lambda k: (0, 0)),
            pl.BlockSpec((rows, width), lambda k: (0, 0)),
            pl.BlockSpec((1, groups, LANES, 2 * HALF), lambda k: (k, 0, 0, 0)),
        ],
        out_specs=[
            pl.BlockSpec((1,) + shape, lambda k: (k, 0, 0, 0)),
            pl.BlockSpec(shape, lambda k: (0, 0, 0)),
        ],
        out_shape=[
            in_hbm((count,) + shape, BF16),
            in_hbm(shape, BF16),
        ],
        scratch_shapes=[pltpu.VMEM(shape, BF16)],
        compiler_params=pltpu.CompilerParams(vmem_limit_bytes=VMEM_LIMIT),
        name="forward_local",
        cost_estimate=estimate(11),
    )(*from_hbm(gate_pre, up_pre, factors))


def prepare_mixing(factors, place, local_bits):
    _, groups, _, _ = factors.shape
    cross = factors.shape[0] - local_bits
    half = LANES // 4

    def kernel(place_ref, low_ref, high_ref, out_ref):
        bit = lax.shift_right_logical(place_ref[0], pl.program_id(0)) & 1
        row = iota((half, 2 * HALF), 0) & (HALF - 1)
        select = (iota((half, 2 * HALF), 1) == bit * HALF + row).astype(F32)
        for g in range(groups):
            low = low_ref[0, g] + select
            high = high_ref[0, g] + select
            out_ref[g, 0] = jnp.concatenate([low, high], axis=1).astype(BF16)

    def spec(offset):
        return pl.BlockSpec(
            (1, groups, half, 2 * HALF), lambda k, c: (local_bits + k, 0, c[1] + offset, 0)
        )

    return pl.pallas_call(
        kernel,
        grid_spec=pltpu.PrefetchScalarGridSpec(
            num_scalar_prefetch=1,
            grid=(cross,),
            in_specs=[spec(0), spec(2)],
            out_specs=pl.BlockSpec((groups, 1, half, 128), lambda k, c: (0, k, 0, 0)),
        ),
        out_shape=in_hbm((groups, cross, half, 128), BF16),
        compiler_params=pltpu.CompilerParams(vmem_limit_bytes=VMEM_LIMIT),
        name="prepare_mixing",
        cost_estimate=estimate(3),
    )(place, *from_hbm(factors, factors))


def packed_block(core, own_ref, other_ref, g):
    own, other = own_ref[g, 0], other_ref[g, 0]
    first = jnp.where(core == 0, own, other)
    second = jnp.where(core == 0, other, own)
    return jnp.concatenate([first, second], axis=0)


def store_tiles(grad_ref, core, g, tiles):
    for low, tile in enumerate(tiles):
        row = (low % 2) * HALF
        grad_ref[(low // 2) ^ core, g, 0, row : row + HALF, :] = tile


def forward_cross(values_in, own_mixing, other_mixing, order, strides):
    groups, rows, _ = values_in.shape
    count = len(strides)

    def kernel(order_ref, in_ref, own_ref, other_ref, saved_ref, out_ref, values):
        k = pl.program_id(0)

        @pl.when(k == 0)
        def _():
            values[...] = in_ref[...]

        for step in range(count):

            @pl.when(k == step)
            def _(step=step):
                saved_ref[0] = values[...]
                apply_forward(
                    values,
                    lambda g: packed_block(order_ref[0], own_ref, other_ref, g),
                    strides[step],
                    groups,
                )

        @pl.when(k == count - 1)
        def _():
            out_ref[...] = values[...]

    shape = (groups, rows, LANES)
    mixing_spec = pl.BlockSpec((groups, 1, LANES // 4, 128), lambda k, c: (0, k, 0, 0))
    return pl.pallas_call(
        kernel,
        grid_spec=pltpu.PrefetchScalarGridSpec(
            num_scalar_prefetch=1,
            grid=(count,),
            in_specs=[pl.BlockSpec(shape, lambda k, c: (0, 0, 0)), mixing_spec, mixing_spec],
            out_specs=[
                pl.BlockSpec((1,) + shape, lambda k, c: (k, 0, 0, 0)),
                pl.BlockSpec(shape, lambda k, c: (0, 0, 0)),
            ],
            scratch_shapes=[pltpu.VMEM(shape, BF16)],
        ),
        out_shape=[
            in_hbm((count,) + shape, BF16),
            in_hbm(shape, BF16),
        ],
        compiler_params=pltpu.CompilerParams(vmem_limit_bytes=VMEM_LIMIT),
        name="forward_cross",
        cost_estimate=estimate(5),
    )(order, *from_hbm(values_in, own_mixing, other_mixing))


def backward_cross(back, saved, own_mixing, other_mixing, order, strides):
    groups, rows, _ = back.shape
    count = len(strides)
    last = count - 1

    def kernel(order_ref, in_ref, saved_ref, own_ref, other_ref, out_ref, grad_ref, grads):
        k = pl.program_id(0)

        @pl.when(k == 0)
        def _():
            grads[...] = in_ref[...]

        for step in range(count):

            @pl.when(k == step)
            def _(step=step):
                apply_backward(
                    grads,
                    lambda g: saved_ref[0, g],
                    lambda g: packed_block(order_ref[0], own_ref, other_ref, g),
                    strides[last - step],
                    groups,
                    lambda g, tiles: store_tiles(grad_ref, order_ref[1], g, tiles),
                )

        @pl.when(k == last)
        def _():
            out_ref[...] = grads[...]

    shape = (groups, rows, LANES)
    mixing_spec = pl.BlockSpec((groups, 1, LANES // 4, 128), lambda k, c: (0, last - k, 0, 0))
    return pl.pallas_call(
        kernel,
        grid_spec=pltpu.PrefetchScalarGridSpec(
            num_scalar_prefetch=1,
            grid=(count,),
            in_specs=[
                pl.BlockSpec(shape, lambda k, c: (0, 0, 0)),
                pl.BlockSpec((1,) + shape, lambda k, c: (last - k, 0, 0, 0)),
                mixing_spec,
                mixing_spec,
            ],
            out_specs=[
                pl.BlockSpec(shape, lambda k, c: (0, 0, 0)),
                pl.BlockSpec((2, groups, 1, 64, 128), lambda k, c: (0, 0, last - k, 0, 0)),
            ],
            scratch_shapes=[pltpu.VMEM(shape, BF16)],
        ),
        out_shape=[
            in_hbm(shape, BF16),
            in_hbm((2, groups, count, 64, 128), F32),
        ],
        compiler_params=pltpu.CompilerParams(vmem_limit_bytes=VMEM_LIMIT),
        name="backward_cross",
        cost_estimate=estimate(90),
    )(order, *from_hbm(back, saved, own_mixing, other_mixing))


def backward_local(back, saved, factors, order, first, end, gate_pre=None, up_pre=None):
    groups, rows, _ = saved.shape[1:]
    width = groups * LANES
    count = end - first
    final = gate_pre is not None

    def kernel(order_ref, in_ref, saved_ref, factor_ref, *refs):
        if final:
            gate_ref, up_ref, dgate_ref, dup_ref, grad_ref, grads = refs
        else:
            out_ref, grad_ref, grads = refs
        k = pl.program_id(0)

        @pl.when(k == 0)
        def _():
            grads[...] = in_ref[...]

        for step in range(count):

            @pl.when(k == step)
            def _(step=step):
                stride = 2 ** (end - 1 - step)
                apply_backward(
                    grads,
                    lambda g: saved_ref[0, g],
                    lambda g: with_identity(factor_ref[0, g], stride, g),
                    stride,
                    groups,
                    lambda g, tiles: store_tiles(grad_ref, order_ref[1], g, tiles),
                )

        @pl.when(k == count - 1)
        def _():
            if not final:
                out_ref[...] = grads[...]
                return
            for g in range(groups):
                cut = pl.ds(g * LANES, LANES)
                gate = gate_ref[:, cut].astype(F32)
                value = grads[g].astype(F32)
                sig = jax.nn.sigmoid(gate)
                dgate = value * up_ref[:, cut].astype(F32) * sig * (1.0 + gate * (1.0 - sig))
                dgate_ref[:, cut] = dgate.astype(BF16)
                dup_ref[:, cut] = (value * gate * sig).astype(BF16)

    shape = (groups, rows, LANES)
    whole = pl.BlockSpec((rows, width), lambda k, c: (0, 0))
    kept = pl.BlockSpec(shape, lambda k, c: (0, 0, 0))
    whole_shape = in_hbm((rows, width), BF16)
    return pl.pallas_call(
        kernel,
        grid_spec=pltpu.PrefetchScalarGridSpec(
            num_scalar_prefetch=1,
            grid=(count,),
            in_specs=[
                kept,
                pl.BlockSpec((1,) + shape, lambda k, c: (end - 1 - k, 0, 0, 0)),
                pl.BlockSpec((1, groups, LANES, 2 * HALF), lambda k, c: (end - 1 - k, 0, 0, 0)),
            ]
            + ([whole, whole] if final else []),
            out_specs=([whole, whole] if final else [kept])
            + [pl.BlockSpec((2, groups, 1, 64, 128), lambda k, c: (0, 0, count - 1 - k, 0, 0))],
            scratch_shapes=[pltpu.VMEM(shape, BF16)],
        ),
        out_shape=([whole_shape, whole_shape] if final else [in_hbm(shape, BF16)])
        + [in_hbm((2, groups, count, 64, 128), F32)],
        compiler_params=pltpu.CompilerParams(vmem_limit_bytes=VMEM_LIMIT),
        name="backward_local",
        cost_estimate=estimate(90),
    )(order, *from_hbm(back, saved, factors, *([gate_pre, up_pre] if final else [])))


def place_grads(parts, order, shape, scale, before=None):
    groups = parts[0][1][0].shape[0]
    numbers = [own[0].shape[1] for _, own, _ in parts]
    begins = [sum(numbers[:p]) for p in range(len(parts))]
    steps = sum(numbers)
    firsts = [first for first, _, _ in parts]
    arrays = [array for _, own, other in parts for array in own + other]
    terms = len(parts[0][1])

    def factor_at(k):
        index = firsts[0] + k
        for begin, first in zip(begins[1:], firsts[1:]):
            index = jnp.where(k >= begin, first + k - begin, index)
        return index

    def kernel(order_ref, *refs):
        out_ref = refs[-1]
        k = pl.program_id(0)
        for p in range(len(parts)):
            own = refs[2 * terms * p : 2 * terms * p + terms]
            other = refs[2 * terms * p + terms : 2 * terms * (p + 1)]

            @pl.when((k >= begins[p]) & (k < begins[p] + numbers[p]))
            def _(own=own, other=other):
                for g in range(groups):
                    for members, swap in ((own, 0), (other, 1)):
                        total = members[0][g, 0].astype(F32)
                        for member in members[1:]:
                            total = total + member[g, 0].astype(F32)
                        total = total * scale
                        turned = pltpu.roll(total, 64, 1)
                        start = ((order_ref[1] ^ swap) * 2) + g * PER
                        for low in range(2):
                            row = low * HALF
                            out_ref[0, start + low] = total[row : row + HALF, : 2 * HALF]
                            out_ref[0, start + low + PER // 2] = turned[row : row + HALF, : 2 * HALF]

    def spec(p):
        return pl.BlockSpec(
            (groups, 1, 64, 128),
            lambda k, c: (0, jnp.clip(k - begins[p], 0, numbers[p] - 1), 0, 0),
        )

    in_specs = [spec(p) for p in range(len(parts)) for _ in range(2 * terms)]
    if before is not None:
        in_specs.append(pl.BlockSpec(memory_space=pl.ANY))
        arrays.append(before)
    return pl.pallas_call(
        kernel,
        grid_spec=pltpu.PrefetchScalarGridSpec(
            num_scalar_prefetch=1,
            grid=(steps,),
            in_specs=in_specs,
            out_specs=pl.BlockSpec((1,) + shape[1:], lambda k, c: (factor_at(k), 0, 0, 0)),
        ),
        out_shape=in_hbm(shape, F32),
        input_output_aliases={} if before is None else {len(arrays): 0},
        compiler_params=pltpu.CompilerParams(vmem_limit_bytes=VMEM_LIMIT),
        name="place_grads",
        cost_estimate=estimate(4),
    )(order, *arrays)


def back_matmul(grads, first, own_weight, other_weight, place, dtype):
    rows = grads.shape[0]
    features = own_weight.shape[1]
    groups = own_weight.shape[0] // LANES

    def kernel(place_ref, a_ref, b_ref, w_ref, v_ref, out_ref):
        out_ref[0] = (dot_nt(a_ref[...], w_ref[...]) + dot_nt(b_ref[...], v_ref[...])).astype(dtype)

    weights = pl.BlockSpec((LANES, features), lambda g, c: (g, 0))
    return pl.pallas_call(
        kernel,
        grid_spec=pltpu.PrefetchScalarGridSpec(
            num_scalar_prefetch=1,
            grid=(groups,),
            in_specs=[
                pl.BlockSpec((rows, features), lambda g, c: (0, first(c) + c[2])),
                pl.BlockSpec((rows, features), lambda g, c: (0, first(c) + 1 - c[2])),
                weights,
                weights,
            ],
            out_specs=pl.BlockSpec((1, rows, LANES), lambda g, c: (g, 0, 0)),
        ),
        out_shape=in_hbm((groups, rows, LANES), dtype),
        compiler_params=pltpu.CompilerParams(vmem_limit_bytes=VMEM_LIMIT),
        name="back_matmul",
        cost_estimate=estimate(5),
    )(place, *from_hbm(grads, grads, own_weight, other_weight))


def output_matmul(values, own_weight, other_weight, ring):
    chips = len(values)
    groups, rows, _ = values[0].shape
    features = own_weight.shape[1]
    tile = min(2 * LANES, features)
    tiles = features // tile
    pieces = ring.shape[0]
    part = rows // pieces

    def kernel(ring_ref, *refs):
        value_refs, own_ref, other_ref = refs[:chips], refs[chips], refs[chips + 1]
        out_refs, total_ref, left_ref = refs[chips + 2 : -2], refs[-2], refs[-1]
        j = pl.program_id(0)

        @pl.when(j == 0)
        def _():
            for chip in range(chips):
                for g in range(groups):
                    left_ref[
                        chip * rows : (chip + 1) * rows, g * LANES : (g + 1) * LANES
                    ] = value_refs[chip][g]

        def run(w_ref):
            total = jnp.dot(left_ref[...], w_ref[...], preferred_element_type=F32).astype(BF16)
            for chip in range(chips):
                total_ref[chip] = total[chip * rows : (chip + 1) * rows]
                for r in range(pieces):
                    start = pl.multiple_of(ring_ref[r] * part, part)
                    out_refs[r][chip] = total_ref[chip, pl.ds(start, part), :]

        @pl.when(j < tiles)
        def _():
            run(own_ref)

        @pl.when(j >= tiles)
        def _():
            run(other_ref)

    value_spec = pl.BlockSpec((groups, rows, LANES), lambda j, c: (0, 0, 0))
    weight_shape = (groups * LANES, tile)
    return pl.pallas_call(
        kernel,
        grid_spec=pltpu.PrefetchScalarGridSpec(
            num_scalar_prefetch=1,
            grid=(2 * tiles,),
            in_specs=[value_spec] * chips
            + [
                pl.BlockSpec(weight_shape, lambda j, c: (0, jnp.minimum(j, tiles - 1))),
                pl.BlockSpec(weight_shape, lambda j, c: (0, jnp.maximum(j - tiles, 0))),
            ],
            out_specs=[pl.BlockSpec((chips, part, tile), lambda j, c: (0, 0, j))] * pieces,
            scratch_shapes=[
                pltpu.VMEM((chips, rows, tile), BF16),
                pltpu.VMEM((chips * rows, groups * LANES), BF16),
            ],
        ),
        out_shape=[in_hbm((chips, part, 2 * features), BF16)] * pieces,
        compiler_params=pltpu.CompilerParams(vmem_limit_bytes=VMEM_LIMIT),
        name="output_matmul",
        cost_estimate=estimate(10),
    )(ring, *from_hbm(*values, own_weight, other_weight))


def place_output(pieces, ring, place):
    flat = [(r, n, array) for r, cuts in enumerate(pieces) for n, array in enumerate(cuts)]
    chips, part, _ = pieces[0][0].shape
    features = sum(array.shape[2] for array in pieces[0]) // 2
    shape = (len(pieces) * part, 2 * chips * features)

    def kernel(ring_ref, place_ref, *refs):
        out_ref = refs[-1]
        for (r, n, _), ref in zip(flat, refs[:-1]):
            row = pl.multiple_of(ring_ref[r] * part, part)
            width = ref.shape[2]
            for chip in range(chips):
                for k in range(2):
                    begin = max(k * features - n * width, 0)
                    end = min((k + 1) * features - n * width, width)
                    if begin >= end:
                        continue
                    block = (place_ref[1] ^ chip) * 2 + (place_ref[2] ^ k)
                    column = block * features + (n * width + begin - k * features)
                    column = pl.multiple_of(column, 128)
                    out_ref[pl.ds(row, part), pl.ds(column, end - begin)] = ref[chip, :, begin:end]

    return pl.pallas_call(
        kernel,
        grid_spec=pltpu.PrefetchScalarGridSpec(
            num_scalar_prefetch=2,
            grid=(1,),
            in_specs=[pl.BlockSpec(a.shape, lambda k, c, d: (0, 0, 0)) for _, _, a in flat],
            out_specs=pl.BlockSpec(shape, lambda k, c, d: (0, 0)),
        ),
        out_shape=in_hbm(shape, BF16),
        compiler_params=pltpu.CompilerParams(vmem_limit_bytes=VMEM_LIMIT),
        name="place_output",
        cost_estimate=estimate(3),
    )(ring, place, *[array for _, _, array in flat])


def flip(block, axis, bits):
    count = lax.axis_size(axis)
    return lax.ppermute(block, axis, [(i, i ^ bits) for i in range(count)])


def to_pieces(values, count):
    groups, rows, _ = values.shape
    if groups == count:
        return values
    return values.transpose(1, 0, 2).reshape(rows, count, -1).transpose(1, 0, 2)


def from_pieces(pieces):
    count, rows, lanes = pieces.shape
    if lanes == LANES:
        return pieces
    return pieces.transpose(1, 0, 2).reshape(rows, -1, LANES).transpose(1, 0, 2)


def swap_layout(values, count):
    if values.shape[0] == count:
        return lax.all_to_all(values, "tensor", 0, 0)
    moved = lax.all_to_all(to_pieces(values, count), "tensor", 0, 0)
    return from_pieces(moved)


def add_pair(a, b):
    return a.astype(F32) + b.astype(F32)


def over_chips(mine, chips):
    return [mine] + [flip(mine, "dp", 2 * r) for r in range(1, chips)]


def with_other(own):
    return own, [flip(term, "dp", 1) for term in own]


def over_cores(grads):
    return (grads[0] + flip(grads[1], "dp", 1)).astype(BF16)


def join_rows(values, mine):
    flat = mine.reshape(mine.shape[0], -1, 128)
    middle = flat.shape[1] // 2
    flat = jnp.concatenate([flat[:, :middle], flat[:, middle:]], axis=2)
    return jnp.concatenate([values, flat], axis=1)


def split_rows(joined, rows, cross):
    flat = joined[:, rows:]
    flat = jnp.concatenate([flat[:, :, :128], flat[:, :, 128:]], axis=1)
    return flat.reshape(flat.shape[0], cross, 64, 128)


def to_owners(mine, core, cross, count, hp):
    groups = mine.shape[0]
    mine = mine.reshape(groups, cross, 2, HALF, 2, 2 * HALF)
    other = flip(mine, "dp", 1)
    first = jnp.where(core == 0, mine, other)
    second = jnp.where(core == 0, other, mine)
    full = jnp.stack([first, second], axis=2)
    full = full.transpose(1, 0, 5, 2, 3, 4, 6).reshape(cross, count, hp, HALF, 2 * HALF)
    full = lax.all_to_all(full.transpose(1, 0, 2, 3, 4), "tensor", 0, 0)
    full = full.transpose(1, 0, 2, 3, 4).reshape(cross, groups, 2, 2, 2, HALF, 2 * HALF)
    full = full.transpose(1, 0, 3, 4, 5, 2, 6).reshape(groups, cross, 2, 64, 128)
    return jnp.where(core == 0, full[:, :, 0], full[:, :, 1])


def cycle(count):
    return list(range(0, count, 2)) + list(range(count - 1, 0, -2))


def shift(block, order, step):
    pairs = [(order[i], order[(i + step) % len(order)]) for i in range(len(order))]
    return lax.ppermute(block, "tensor", pairs)


def ring_sum(pieces, order, first_work, second_work):
    count = len(pieces)
    far = count // 2
    cut = pieces[far].shape[2] // 2
    up = shift(pieces[far][:, :, :cut], order, 1)
    down = shift(pieces[far][:, :, cut:], order, -1)
    up, down, first = lax.optimization_barrier((up, down, first_work()))
    for distance in range(far - 1, 0, -1):
        above, below = pieces[distance], pieces[count - distance]
        if distance == far - 1:
            up = jnp.pad(up.astype(F32), ((0, 0), (0, 0), (0, cut)))
            down = jnp.pad(down.astype(F32), ((0, 0), (0, 0), (cut, 0)))
        above = add_pair(above, up).astype(BF16)
        below = add_pair(below, down).astype(BF16)
        up = shift(above, order, 1)
        down = shift(below, order, -1)
        if distance == far - 1:
            up, down, second = lax.optimization_barrier((up, down, second_work(first)))
    total = (pieces[0].astype(F32) + up.astype(F32) + down.astype(F32)).astype(BF16)
    return total, second


def ring_gather(piece, order):
    count = len(order)
    far = count // 2
    cut = piece.shape[2] // 2
    result = [None] * count
    result[0] = [piece]
    up = down = piece
    for distance in range(1, far):
        up = shift(up, order, 1)
        down = shift(down, order, -1)
        result[count - distance] = [up]
        result[distance] = [down]
    result[far] = [shift(up[:, :, :cut], order, 1), shift(down[:, :, cut:], order, -1)]
    return result


def body(gate_pre, up_pre, down_weight, factors, out_grad):
    rows, width = gate_pre.shape
    features = down_weight.shape[1]
    halves = width // HALF
    groups = width // LANES
    local_bits = halves.bit_length() - 1
    cross = FACTORS - local_bits
    count = lax.axis_size("tensor")
    chips = lax.axis_size("dp") // 2
    hp = halves // count
    dp = lax.axis_index("dp").astype(jnp.int32)
    tensor = lax.axis_index("tensor").astype(jnp.int32)
    core = dp & 1
    chip = dp >> 1
    grouped = factors.reshape(FACTORS, groups, LANES, 2 * HALF)
    aligned = hp == PER
    place = jnp.stack([tensor, chip, core])

    slices = [
        lax.dynamic_slice_in_dim(out_grad, (chip ^ r) * 2 * features, 2 * features, 1)
        for r in range(1, chips)
    ]
    grouped, slices = lax.optimization_barrier((grouped, slices))

    if aligned:
        own_mixing = prepare_mixing(grouped, jnp.stack([tensor, core]), local_bits)
        own_mixing = lax.all_to_all(own_mixing, "tensor", 0, 0)
        other_mixing = flip(own_mixing, "dp", 1)
        order = jnp.stack([core, core])
    else:
        row_index = jnp.arange(HALF, dtype=jnp.int32)[None, None, :, None]
        col_index = jnp.arange(2 * HALF, dtype=jnp.int32)[None, None, None, :]
        bits = (tensor >> jnp.arange(cross, dtype=jnp.int32)) & 1
        select = col_index == bits[:, None, None, None] * HALF + row_index
        mixing = (factors[local_bits:] + select.astype(F32)).astype(BF16)
        mixing = mixing.reshape(cross, count, hp * HALF, 2 * HALF).transpose(1, 0, 2, 3)
        mixing = lax.all_to_all(mixing, "tensor", 0, 0).transpose(1, 0, 2, 3)
        mixing = mixing.reshape(cross, groups, LANES, 2 * HALF).transpose(1, 0, 2, 3)
        mixing = jnp.concatenate([mixing[:, :, :128], mixing[:, :, 128:]], axis=-1)
        own_mixing, other_mixing = mixing[:, :, :64], mixing[:, :, 64:]
        order = jnp.stack([0 * core, core])

    other_weight = flip(down_weight, "dp", 1)

    strides = [hp * 2**bit for bit in range(cross)]
    crossing = [flip(part, "dp", 2 * (r + 1)) for r, part in enumerate(slices)]
    saved_local, values = forward_local(gate_pre, up_pre, grouped, local_bits)
    values, crossing = lax.optimization_barrier((values, crossing))

    values = swap_layout(values, count)
    sent = [
        back_matmul(part, lambda c: 0, down_weight, other_weight, place, BF16) for part in crossing
    ]
    received = [flip(part, "dp", 2 * (r + 1)) for r, part in enumerate(sent)]
    values, _ = lax.optimization_barrier((values, sent))
    saved_cross, values = forward_cross(values, own_mixing, other_mixing, order, strides)
    out_grad, _ = lax.optimization_barrier((out_grad, sent))
    back = back_matmul(out_grad, lambda c: 2 * c[1], down_weight, other_weight, place, F32)
    for term in received:
        back = back + term.astype(F32)
    back = swap_layout(back.astype(BF16), count)
    values, back = lax.optimization_barrier((values, back))
    values = swap_layout(values, count)
    back, grads_cross = backward_cross(back, saved_cross, own_mixing, other_mixing, order, strides)
    mine_cross = over_cores(grads_cross)
    if aligned:
        back = join_rows(back, mine_cross)
    values, back, mine_cross = lax.optimization_barrier((values, back, mine_cross))
    all_values = [values] + [flip(values, "dp", 2 * r) for r in range(1, chips)]
    back = swap_layout(back, count)

    circle = cycle(count)
    spot = jnp.argmax(jnp.array(circle, jnp.int32) == tensor).astype(jnp.int32)
    steps = (spot + jnp.arange(count, dtype=jnp.int32)) % count
    ring = jnp.where(steps < count // 2, 2 * steps, 2 * (count - steps) - 1)
    shares = output_matmul(all_values, down_weight, other_weight, ring)
    back, shares, mine_cross = lax.optimization_barrier((back, shares, mine_cross))
    if aligned:
        mine_cross = split_rows(back, rows, cross)
    else:
        mine_cross = to_owners(mine_cross, core, cross, count, hp)
    middle = local_bits // 2

    def first_half():
        return backward_local(back, saved_local, grouped, order, middle, local_bits)

    def second_half(first):
        lower, grads = first
        results = backward_local(lower, saved_local, grouped, order, 0, middle, gate_pre, up_pre)
        return results, mine_cross, (grads[0], flip(grads[1], "dp", 1))

    summed, second = ring_sum(shares, circle, first_half, second_half)
    (gate_grad, up_grad, grads_low), mine_cross, high_pair = second
    mine_high = (high_pair[0] + high_pair[1]).astype(BF16)
    piece = jnp.stack([summed[0]] + [flip(summed[r], "dp", 2 * r) for r in range(1, chips)])
    gathered = ring_gather(piece, circle)

    scale = 1.0 / math.sqrt(rows * lax.axis_size("dp"))
    parts_cross = (local_bits,) + with_other(over_chips(mine_cross, chips))
    parts_high = (middle,) + with_other(over_chips(mine_high, chips))
    parts_low = (0,) + with_other(over_chips(over_cores(grads_low), chips))
    early = place_grads([parts_high, parts_cross], order, factors.shape, scale)
    output = place_output(gathered, ring, place)
    factor_grads = place_grads([parts_low], order, factors.shape, scale, early)
    return (output, gate_grad, up_grad, factor_grads)


def solution(mesh):
    return jax.shard_map(
        body,
        mesh=mesh,
        in_specs=(
            P("dp", "tensor"),
            P("dp", "tensor"),
            P("tensor", "dp"),
            P(None, "tensor", None, None),
            P("dp", None),
        ),
        out_specs=(
            P("dp", None),
            P("dp", "tensor"),
            P("dp", "tensor"),
            P(None, "tensor", None, None),
        ),
        check_vma=False,
    )
```

```python
import functools
import math

import jax
import jax.numpy as jnp
from jax import lax
from jax.experimental import pallas as pl
from jax.experimental.pallas import tpu as pltpu
from jax.sharding import PartitionSpec as P

HALF = 32
FACTORS = 9
LANES = 256
PER = LANES // HALF
VMEM_LIMIT = 48 * 1024 * 1024


def estimate(microseconds):
    return pl.CostEstimate(flops=0, transcendentals=0, bytes_accessed=int(3.6e5 * microseconds))


F32 = jnp.float32
BF16 = jnp.bfloat16


def in_hbm(shape, dtype):
    return pltpu.HBM(shape, dtype)


def from_hbm(*arrays):
    return [pltpu.with_memory_space_constraint(array, pltpu.HBM) for array in arrays]


def iota(shape, axis):
    return lax.broadcasted_iota(jnp.int32, shape, axis)


def with_identity(block, stride, group):
    row = iota((LANES, 2 * HALF), 0)
    col = iota((LANES, 2 * HALF), 1)
    if stride < PER:
        bit = (row // HALF // stride) & 1
    else:
        bit = (group // (stride // PER)) & 1
    select = (col == bit * HALF + (row & (HALF - 1))).astype(F32)
    return (block + select).astype(BF16)


def spread_matrix(depth, bit, offset):
    col = iota((depth, LANES), 0)
    lane = iota((depth, LANES), 1)
    return (col == bit(lane) * HALF + (lane & (HALF - 1)) + offset).astype(BF16)


def expand(mixing, bit):
    depth = mixing.shape[1]
    full = jnp.dot(mixing, spread_matrix(depth, bit, 0), preferred_element_type=F32)
    if depth == 2 * HALF:
        return full
    rest = jnp.dot(mixing, spread_matrix(depth, bit, 2 * HALF), preferred_element_type=F32)
    return jnp.concatenate([full, rest], axis=0)


def inner_matrix(mixing, stride):
    full = expand(mixing, lambda lane: (lane // HALF // stride) & 1)
    row = iota((LANES, LANES), 0) // HALF
    unit = iota((LANES, LANES), 1) // HALF
    mask = (unit == row) | (unit == (row ^ stride))
    return jnp.where(mask, full, 0.0).astype(BF16)


def outer_matrix(mixing):
    full = jnp.concatenate([expand(mixing, lambda lane: bit) for bit in range(2)], axis=1)
    row = iota((LANES, 2 * LANES), 0) // HALF
    unit = (iota((LANES, 2 * LANES), 1) & (LANES - 1)) // HALF
    return jnp.where(row == unit, full, 0.0).astype(BF16)


def dot_nt(a, b):
    return lax.dot_general(a, b, (((1,), (1,)), ((), ())), preferred_element_type=F32)


def dot_tn(a, b):
    return lax.dot_general(a, b, (((0,), (0,)), ((), ())), preferred_element_type=F32)


def fold(get_tile, columns_of):
    lane = iota((HALF, 128), 1)
    rows = []
    for low in range(PER // 2):
        out = None
        for upper in range(2):
            i = low + upper * (PER // 2)
            for unit_block, source, column in columns_of(i):
                tile = get_tile(source, i, unit_block // 4)
                place = upper * 2 * HALF + column * HALF
                shift = (place - (unit_block % 4) * HALF) % 128
                if shift:
                    tile = pltpu.roll(tile, shift, 1)
                if out is None:
                    out = tile
                else:
                    out = jnp.where((lane >= place) & (lane < place + HALF), tile, out)
        rows.append(out)
    return rows


def apply_forward(values, mixing_of, stride, groups):
    if stride < PER:
        for g in range(groups):
            matrix = inner_matrix(mixing_of(g), stride)
            values[g] = dot_nt(values[g], matrix).astype(BF16)
        return
    step = stride // PER
    for g in range(groups):
        if g & step:
            continue
        h = g | step
        pair = jnp.concatenate([values[g], values[h]], axis=1)
        for member in (g, h):
            new = dot_nt(pair, outer_matrix(mixing_of(member)))
            values[member] = new.astype(BF16)


def apply_backward(grads, inputs, mixing_of, stride, groups, store_grad):
    if stride < PER:
        for g in range(groups):
            matrix = inner_matrix(mixing_of(g), stride)
            grad = grads[g]
            outer = dot_tn(grad, inputs(g))

            def columns_of(i):
                bit = (i // stride) & 1
                return ((i, 0, bit), (i ^ stride, 0, 1 - bit))

            def tile(source, i, part):
                return outer[i * HALF : (i + 1) * HALF, part * 128 : (part + 1) * 128]

            store_grad(g, fold(tile, columns_of))
            grads[g] = jnp.dot(grad, matrix, preferred_element_type=F32).astype(BF16)
        return
    step = stride // PER
    for g in range(groups):
        if g & step:
            continue
        h = g | step
        pair = jnp.concatenate([inputs(g), inputs(h)], axis=1)
        total = None
        for member in (g, h):
            grad = grads[member]
            product = dot_tn(grad, pair)

            def tile(source, i, part):
                column = source * LANES + part * 128
                return product[i * HALF : (i + 1) * HALF, column : column + 128]

            store_grad(member, fold(tile, lambda i: ((i, 0, 0), (i, 1, 1))))
            term = jnp.dot(grad, outer_matrix(mixing_of(member)), preferred_element_type=F32)
            total = term if total is None else total + term
        grads[g] = total[:, :LANES].astype(BF16)
        grads[h] = total[:, LANES:].astype(BF16)


def forward_local(gate_pre, up_pre, factors, count):
    rows, width = gate_pre.shape
    groups = width // LANES

    def kernel(gate_ref, up_ref, factor_ref, saved_ref, out_ref, values):
        k = pl.program_id(0)

        @pl.when(k == 0)
        def _():
            for g in range(groups):
                cut = pl.ds(g * LANES, LANES)
                gate = gate_ref[:, cut].astype(F32)
                hidden = gate * jax.nn.sigmoid(gate) * up_ref[:, cut].astype(F32)
                values[g] = hidden.astype(BF16)

        for step in range(count):

            @pl.when(k == step)
            def _(step=step):
                saved_ref[0] = values[...]
                stride = 2**step
                apply_forward(
                    values,
                    lambda g: with_identity(factor_ref[0, g], stride, g),
                    stride,
                    groups,
                )

        @pl.when(k == count - 1)
        def _():
            out_ref[...] = values[...]

    shape = (groups, rows, LANES)
    return pl.pallas_call(
        kernel,
        grid=(count,),
        in_specs=[
            pl.BlockSpec((rows, width), lambda k: (0, 0)),
            pl.BlockSpec((rows, width), lambda k: (0, 0)),
            pl.BlockSpec((1, groups, LANES, 2 * HALF), lambda k: (k, 0, 0, 0)),
        ],
        out_specs=[
            pl.BlockSpec((1,) + shape, lambda k: (k, 0, 0, 0)),
            pl.BlockSpec(shape, lambda k: (0, 0, 0)),
        ],
        out_shape=[
            in_hbm((count,) + shape, BF16),
            in_hbm(shape, BF16),
        ],
        scratch_shapes=[pltpu.VMEM(shape, BF16)],
        compiler_params=pltpu.CompilerParams(vmem_limit_bytes=VMEM_LIMIT),
        name="forward_local",
        cost_estimate=estimate(11),
    )(*from_hbm(gate_pre, up_pre, factors))


def prepare_mixing(factors, place, local_bits):
    _, groups, _, _ = factors.shape
    cross = factors.shape[0] - local_bits
    half = LANES // 4

    def kernel(place_ref, low_ref, high_ref, out_ref):
        bit = lax.shift_right_logical(place_ref[0], pl.program_id(0)) & 1
        row = iota((half, 2 * HALF), 0) & (HALF - 1)
        select = (iota((half, 2 * HALF), 1) == bit * HALF + row).astype(F32)
        for g in range(groups):
            low = low_ref[0, g] + select
            high = high_ref[0, g] + select
            out_ref[g, 0] = jnp.concatenate([low, high], axis=1).astype(BF16)

    def spec(offset):
        return pl.BlockSpec(
            (1, groups, half, 2 * HALF), lambda k, c: (local_bits + k, 0, c[1] + offset, 0)
        )

    return pl.pallas_call(
        kernel,
        grid_spec=pltpu.PrefetchScalarGridSpec(
            num_scalar_prefetch=1,
            grid=(cross,),
            in_specs=[spec(0), spec(2)],
            out_specs=pl.BlockSpec((groups, 1, half, 128), lambda k, c: (0, k, 0, 0)),
        ),
        out_shape=in_hbm((groups, cross, half, 128), BF16),
        compiler_params=pltpu.CompilerParams(vmem_limit_bytes=VMEM_LIMIT),
        name="prepare_mixing",
        cost_estimate=estimate(3),
    )(place, *from_hbm(factors, factors))


def packed_block(core, own_ref, other_ref, g):
    own, other = own_ref[g, 0], other_ref[g, 0]
    first = jnp.where(core == 0, own, other)
    second = jnp.where(core == 0, other, own)
    return jnp.concatenate([first, second], axis=0)


def store_tiles(grad_ref, core, g, tiles):
    for low, tile in enumerate(tiles):
        row = (low % 2) * HALF
        grad_ref[(low // 2) ^ core, g, 0, row : row + HALF, :] = tile


def forward_cross(values_in, own_mixing, other_mixing, order, strides):
    groups, rows, _ = values_in.shape
    count = len(strides)

    def kernel(order_ref, in_ref, own_ref, other_ref, saved_ref, out_ref, values):
        k = pl.program_id(0)

        @pl.when(k == 0)
        def _():
            values[...] = in_ref[...]

        for step in range(count):

            @pl.when(k == step)
            def _(step=step):
                saved_ref[0] = values[...]
                apply_forward(
                    values,
                    lambda g: packed_block(order_ref[0], own_ref, other_ref, g),
                    strides[step],
                    groups,
                )

        @pl.when(k == count - 1)
        def _():
            out_ref[...] = values[...]

    shape = (groups, rows, LANES)
    mixing_spec = pl.BlockSpec((groups, 1, LANES // 4, 128), lambda k, c: (0, k, 0, 0))
    return pl.pallas_call(
        kernel,
        grid_spec=pltpu.PrefetchScalarGridSpec(
            num_scalar_prefetch=1,
            grid=(count,),
            in_specs=[pl.BlockSpec(shape, lambda k, c: (0, 0, 0)), mixing_spec, mixing_spec],
            out_specs=[
                pl.BlockSpec((1,) + shape, lambda k, c: (k, 0, 0, 0)),
                pl.BlockSpec(shape, lambda k, c: (0, 0, 0)),
            ],
            scratch_shapes=[pltpu.VMEM(shape, BF16)],
        ),
        out_shape=[
            in_hbm((count,) + shape, BF16),
            in_hbm(shape, BF16),
        ],
        compiler_params=pltpu.CompilerParams(vmem_limit_bytes=VMEM_LIMIT),
        name="forward_cross",
        cost_estimate=estimate(5),
    )(order, *from_hbm(values_in, own_mixing, other_mixing))


def backward_cross(back, saved, own_mixing, other_mixing, order, strides):
    groups, rows, _ = back.shape
    count = len(strides)
    last = count - 1

    def kernel(order_ref, in_ref, saved_ref, own_ref, other_ref, out_ref, grad_ref, grads):
        k = pl.program_id(0)

        @pl.when(k == 0)
        def _():
            grads[...] = in_ref[...]

        for step in range(count):

            @pl.when(k == step)
            def _(step=step):
                apply_backward(
                    grads,
                    lambda g: saved_ref[0, g],
                    lambda g: packed_block(order_ref[0], own_ref, other_ref, g),
                    strides[last - step],
                    groups,
                    lambda g, tiles: store_tiles(grad_ref, order_ref[1], g, tiles),
                )

        @pl.when(k == last)
        def _():
            out_ref[...] = grads[...]

    shape = (groups, rows, LANES)
    mixing_spec = pl.BlockSpec((groups, 1, LANES // 4, 128), lambda k, c: (0, last - k, 0, 0))
    return pl.pallas_call(
        kernel,
        grid_spec=pltpu.PrefetchScalarGridSpec(
            num_scalar_prefetch=1,
            grid=(count,),
            in_specs=[
                pl.BlockSpec(shape, lambda k, c: (0, 0, 0)),
                pl.BlockSpec((1,) + shape, lambda k, c: (last - k, 0, 0, 0)),
                mixing_spec,
                mixing_spec,
            ],
            out_specs=[
                pl.BlockSpec(shape, lambda k, c: (0, 0, 0)),
                pl.BlockSpec((2, groups, 1, 64, 128), lambda k, c: (0, 0, last - k, 0, 0)),
            ],
            scratch_shapes=[pltpu.VMEM(shape, BF16)],
        ),
        out_shape=[
            in_hbm(shape, BF16),
            in_hbm((2, groups, count, 64, 128), F32),
        ],
        compiler_params=pltpu.CompilerParams(vmem_limit_bytes=VMEM_LIMIT),
        name="backward_cross",
        cost_estimate=estimate(90),
    )(order, *from_hbm(back, saved, own_mixing, other_mixing))


def backward_local(back, saved, factors, order, first, end, gate_pre=None, up_pre=None):
    groups, rows, _ = saved.shape[1:]
    width = groups * LANES
    count = end - first
    final = gate_pre is not None

    def kernel(order_ref, in_ref, saved_ref, factor_ref, *refs):
        if final:
            gate_ref, up_ref, dgate_ref, dup_ref, grad_ref, grads = refs
        else:
            out_ref, grad_ref, grads = refs
        k = pl.program_id(0)

        @pl.when(k == 0)
        def _():
            grads[...] = in_ref[...]

        for step in range(count):

            @pl.when(k == step)
            def _(step=step):
                stride = 2 ** (end - 1 - step)
                apply_backward(
                    grads,
                    lambda g: saved_ref[0, g],
                    lambda g: with_identity(factor_ref[0, g], stride, g),
                    stride,
                    groups,
                    lambda g, tiles: store_tiles(grad_ref, order_ref[1], g, tiles),
                )

        @pl.when(k == count - 1)
        def _():
            if not final:
                out_ref[...] = grads[...]
                return
            for g in range(groups):
                cut = pl.ds(g * LANES, LANES)
                gate = gate_ref[:, cut].astype(F32)
                value = grads[g].astype(F32)
                sig = jax.nn.sigmoid(gate)
                dgate = value * up_ref[:, cut].astype(F32) * sig * (1.0 + gate * (1.0 - sig))
                dgate_ref[:, cut] = dgate.astype(BF16)
                dup_ref[:, cut] = (value * gate * sig).astype(BF16)

    shape = (groups, rows, LANES)
    whole = pl.BlockSpec((rows, width), lambda k, c: (0, 0))
    kept = pl.BlockSpec(shape, lambda k, c: (0, 0, 0))
    whole_shape = in_hbm((rows, width), BF16)
    return pl.pallas_call(
        kernel,
        grid_spec=pltpu.PrefetchScalarGridSpec(
            num_scalar_prefetch=1,
            grid=(count,),
            in_specs=[
                kept,
                pl.BlockSpec((1,) + shape, lambda k, c: (end - 1 - k, 0, 0, 0)),
                pl.BlockSpec((1, groups, LANES, 2 * HALF), lambda k, c: (end - 1 - k, 0, 0, 0)),
            ]
            + ([whole, whole] if final else []),
            out_specs=([whole, whole] if final else [kept])
            + [pl.BlockSpec((2, groups, 1, 64, 128), lambda k, c: (0, 0, count - 1 - k, 0, 0))],
            scratch_shapes=[pltpu.VMEM(shape, BF16)],
        ),
        out_shape=([whole_shape, whole_shape] if final else [in_hbm(shape, BF16)])
        + [in_hbm((2, groups, count, 64, 128), F32)],
        compiler_params=pltpu.CompilerParams(vmem_limit_bytes=VMEM_LIMIT),
        name="backward_local",
        cost_estimate=estimate(90),
    )(order, *from_hbm(back, saved, factors, *([gate_pre, up_pre] if final else [])))


def place_grads(parts, order, shape, scale, before=None):
    groups = parts[0][1][0].shape[0]
    numbers = [own[0].shape[1] for _, own, _ in parts]
    begins = [sum(numbers[:p]) for p in range(len(parts))]
    steps = sum(numbers)
    firsts = [first for first, _, _ in parts]
    arrays = [array for _, own, other in parts for array in own + other]
    terms = len(parts[0][1])

    def factor_at(k):
        index = firsts[0] + k
        for begin, first in zip(begins[1:], firsts[1:]):
            index = jnp.where(k >= begin, first + k - begin, index)
        return index

    def kernel(order_ref, *refs):
        out_ref = refs[-1]
        k = pl.program_id(0)
        for p in range(len(parts)):
            own = refs[2 * terms * p : 2 * terms * p + terms]
            other = refs[2 * terms * p + terms : 2 * terms * (p + 1)]

            @pl.when((k >= begins[p]) & (k < begins[p] + numbers[p]))
            def _(own=own, other=other):
                for g in range(groups):
                    for members, swap in ((own, 0), (other, 1)):
                        total = members[0][g, 0].astype(F32)
                        for member in members[1:]:
                            total = total + member[g, 0].astype(F32)
                        total = total * scale
                        turned = pltpu.roll(total, 64, 1)
                        start = ((order_ref[1] ^ swap) * 2) + g * PER
                        for low in range(2):
                            row = low * HALF
                            out_ref[0, start + low] = total[row : row + HALF, : 2 * HALF]
                            out_ref[0, start + low + PER // 2] = turned[row : row + HALF, : 2 * HALF]

    def spec(p):
        return pl.BlockSpec(
            (groups, 1, 64, 128),
            lambda k, c: (0, jnp.clip(k - begins[p], 0, numbers[p] - 1), 0, 0),
        )

    in_specs = [spec(p) for p in range(len(parts)) for _ in range(2 * terms)]
    if before is not None:
        in_specs.append(pl.BlockSpec(memory_space=pl.ANY))
        arrays.append(before)
    return pl.pallas_call(
        kernel,
        grid_spec=pltpu.PrefetchScalarGridSpec(
            num_scalar_prefetch=1,
            grid=(steps,),
            in_specs=in_specs,
            out_specs=pl.BlockSpec((1,) + shape[1:], lambda k, c: (factor_at(k), 0, 0, 0)),
        ),
        out_shape=in_hbm(shape, F32),
        input_output_aliases={} if before is None else {len(arrays): 0},
        compiler_params=pltpu.CompilerParams(vmem_limit_bytes=VMEM_LIMIT),
        name="place_grads",
        cost_estimate=estimate(4),
    )(order, *arrays)


def back_matmul(grads, first, own_weight, other_weight, place, dtype, begin, groups):
    rows = grads.shape[0]
    features = own_weight.shape[1]

    def kernel(place_ref, a_ref, b_ref, w_ref, v_ref, out_ref):
        out_ref[0] = (dot_nt(a_ref[...], w_ref[...]) + dot_nt(b_ref[...], v_ref[...])).astype(dtype)

    weights = pl.BlockSpec((LANES, features), lambda g, c: (begin + g, 0))
    return pl.pallas_call(
        kernel,
        grid_spec=pltpu.PrefetchScalarGridSpec(
            num_scalar_prefetch=1,
            grid=(groups,),
            in_specs=[
                pl.BlockSpec((rows, features), lambda g, c: (0, first(c) + c[2])),
                pl.BlockSpec((rows, features), lambda g, c: (0, first(c) + 1 - c[2])),
                weights,
                weights,
            ],
            out_specs=pl.BlockSpec((1, rows, LANES), lambda g, c: (g, 0, 0)),
        ),
        out_shape=in_hbm((groups, rows, LANES), dtype),
        compiler_params=pltpu.CompilerParams(vmem_limit_bytes=VMEM_LIMIT),
        name="back_matmul",
        cost_estimate=estimate(5),
    )(place, *from_hbm(grads, grads, own_weight, other_weight))


def output_matmul(values, own_weight, other_weight, ring):
    chips = len(values)
    groups, rows, _ = values[0].shape
    features = own_weight.shape[1]
    tile = min(2 * LANES, features)
    tiles = features // tile
    pieces = ring.shape[0]
    part = rows // pieces

    def kernel(ring_ref, *refs):
        value_refs, own_ref, other_ref = refs[:chips], refs[chips], refs[chips + 1]
        out_refs, total_ref, left_ref = refs[chips + 2 : -2], refs[-2], refs[-1]
        j = pl.program_id(0)

        @pl.when(j == 0)
        def _():
            for chip in range(chips):
                for g in range(groups):
                    left_ref[
                        chip * rows : (chip + 1) * rows, g * LANES : (g + 1) * LANES
                    ] = value_refs[chip][g]

        def run(w_ref):
            total = jnp.dot(left_ref[...], w_ref[...], preferred_element_type=F32).astype(BF16)
            for chip in range(chips):
                total_ref[chip] = total[chip * rows : (chip + 1) * rows]
                for r in range(pieces):
                    start = pl.multiple_of(ring_ref[r] * part, part)
                    out_refs[r][chip] = total_ref[chip, pl.ds(start, part), :]

        @pl.when(j < tiles)
        def _():
            run(own_ref)

        @pl.when(j >= tiles)
        def _():
            run(other_ref)

    value_spec = pl.BlockSpec((groups, rows, LANES), lambda j, c: (0, 0, 0))
    weight_shape = (groups * LANES, tile)
    return pl.pallas_call(
        kernel,
        grid_spec=pltpu.PrefetchScalarGridSpec(
            num_scalar_prefetch=1,
            grid=(2 * tiles,),
            in_specs=[value_spec] * chips
            + [
                pl.BlockSpec(weight_shape, lambda j, c: (0, jnp.minimum(j, tiles - 1))),
                pl.BlockSpec(weight_shape, lambda j, c: (0, jnp.maximum(j - tiles, 0))),
            ],
            out_specs=[pl.BlockSpec((chips, part, tile), lambda j, c: (0, 0, j))] * pieces,
            scratch_shapes=[
                pltpu.VMEM((chips, rows, tile), BF16),
                pltpu.VMEM((chips * rows, groups * LANES), BF16),
            ],
        ),
        out_shape=[in_hbm((chips, part, 2 * features), BF16)] * pieces,
        compiler_params=pltpu.CompilerParams(vmem_limit_bytes=VMEM_LIMIT),
        name="output_matmul",
        cost_estimate=estimate(10),
    )(ring, *from_hbm(*values, own_weight, other_weight))


def place_output(pieces, ring, place):
    flat = [(r, n, array) for r, cuts in enumerate(pieces) for n, array in enumerate(cuts)]
    chips, part, _ = pieces[0][0].shape
    features = sum(array.shape[2] for array in pieces[0]) // 2
    shape = (len(pieces) * part, 2 * chips * features)

    def kernel(ring_ref, place_ref, *refs):
        out_ref = refs[-1]
        for (r, n, _), ref in zip(flat, refs[:-1]):
            row = pl.multiple_of(ring_ref[r] * part, part)
            width = ref.shape[2]
            for chip in range(chips):
                for k in range(2):
                    begin = max(k * features - n * width, 0)
                    end = min((k + 1) * features - n * width, width)
                    if begin >= end:
                        continue
                    block = (place_ref[1] ^ chip) * 2 + (place_ref[2] ^ k)
                    column = block * features + (n * width + begin - k * features)
                    column = pl.multiple_of(column, 128)
                    out_ref[pl.ds(row, part), pl.ds(column, end - begin)] = ref[chip, :, begin:end]

    return pl.pallas_call(
        kernel,
        grid_spec=pltpu.PrefetchScalarGridSpec(
            num_scalar_prefetch=2,
            grid=(1,),
            in_specs=[pl.BlockSpec(a.shape, lambda k, c, d: (0, 0, 0)) for _, _, a in flat],
            out_specs=pl.BlockSpec(shape, lambda k, c, d: (0, 0)),
        ),
        out_shape=in_hbm(shape, BF16),
        compiler_params=pltpu.CompilerParams(vmem_limit_bytes=VMEM_LIMIT),
        name="place_output",
        cost_estimate=estimate(3),
    )(ring, place, *[array for _, _, array in flat])


def flip(block, axis, bits):
    count = lax.axis_size(axis)
    return lax.ppermute(block, axis, [(i, i ^ bits) for i in range(count)])


def to_pieces(values, count):
    groups, rows, _ = values.shape
    if groups == count:
        return values
    return values.transpose(1, 0, 2).reshape(rows, count, -1).transpose(1, 0, 2)


def from_pieces(pieces):
    count, rows, lanes = pieces.shape
    if lanes == LANES:
        return pieces
    return pieces.transpose(1, 0, 2).reshape(rows, -1, LANES).transpose(1, 0, 2)


def swap_layout(values, count):
    if values.shape[0] == count:
        return lax.all_to_all(values, "tensor", 0, 0)
    moved = lax.all_to_all(to_pieces(values, count), "tensor", 0, 0)
    return from_pieces(moved)


def add_pair(a, b):
    return a.astype(F32) + b.astype(F32)


def over_chips(mine, chips):
    return [mine] + [flip(mine, "dp", 2 * r) for r in range(1, chips)]


def with_other(own):
    return own, [flip(term, "dp", 1) for term in own]


def over_cores(grads):
    return (grads[0] + flip(grads[1], "dp", 1)).astype(BF16)


def join_rows(values, mine):
    flat = mine.reshape(mine.shape[0], -1, 128)
    middle = flat.shape[1] // 2
    flat = jnp.concatenate([flat[:, :middle], flat[:, middle:]], axis=2)
    return jnp.concatenate([values, flat], axis=1)


def split_rows(joined, rows, cross):
    flat = joined[:, rows:]
    flat = jnp.concatenate([flat[:, :, :128], flat[:, :, 128:]], axis=1)
    return flat.reshape(flat.shape[0], cross, 64, 128)


def to_owners(mine, core, cross, count, hp):
    groups = mine.shape[0]
    mine = mine.reshape(groups, cross, 2, HALF, 2, 2 * HALF)
    other = flip(mine, "dp", 1)
    first = jnp.where(core == 0, mine, other)
    second = jnp.where(core == 0, other, mine)
    full = jnp.stack([first, second], axis=2)
    full = full.transpose(1, 0, 5, 2, 3, 4, 6).reshape(cross, count, hp, HALF, 2 * HALF)
    full = lax.all_to_all(full.transpose(1, 0, 2, 3, 4), "tensor", 0, 0)
    full = full.transpose(1, 0, 2, 3, 4).reshape(cross, groups, 2, 2, 2, HALF, 2 * HALF)
    full = full.transpose(1, 0, 3, 4, 5, 2, 6).reshape(groups, cross, 2, 64, 128)
    return jnp.where(core == 0, full[:, :, 0], full[:, :, 1])


def cycle(count):
    return list(range(0, count, 2)) + list(range(count - 1, 0, -2))


def shift(block, order, step):
    pairs = [(order[i], order[(i + step) % len(order)]) for i in range(len(order))]
    return lax.ppermute(block, "tensor", pairs)


def ring_sum(pieces, order, first_work, second_work):
    count = len(pieces)
    far = count // 2
    cut = pieces[far].shape[2] // 2
    up = shift(pieces[far][:, :, :cut], order, 1)
    down = shift(pieces[far][:, :, cut:], order, -1)
    up, down, first = lax.optimization_barrier((up, down, first_work()))
    for distance in range(far - 1, 0, -1):
        above, below = pieces[distance], pieces[count - distance]
        if distance == far - 1:
            up = jnp.pad(up.astype(F32), ((0, 0), (0, 0), (0, cut)))
            down = jnp.pad(down.astype(F32), ((0, 0), (0, 0), (cut, 0)))
        above = add_pair(above, up).astype(BF16)
        below = add_pair(below, down).astype(BF16)
        up = shift(above, order, 1)
        down = shift(below, order, -1)
        if distance == far - 1:
            up, down, second = lax.optimization_barrier((up, down, second_work(first)))
    total = (pieces[0].astype(F32) + up.astype(F32) + down.astype(F32)).astype(BF16)
    return total, second


def ring_gather(piece, order):
    count = len(order)
    far = count // 2
    cut = piece.shape[2] // 2
    result = [None] * count
    result[0] = [piece]
    up = down = piece
    for distance in range(1, far):
        up = shift(up, order, 1)
        down = shift(down, order, -1)
        result[count - distance] = [up]
        result[distance] = [down]
    result[far] = [shift(up[:, :, :cut], order, 1), shift(down[:, :, cut:], order, -1)]
    return result


def body(gate_pre, up_pre, down_weight, factors, out_grad):
    rows, width = gate_pre.shape
    features = down_weight.shape[1]
    halves = width // HALF
    groups = width // LANES
    local_bits = halves.bit_length() - 1
    cross = FACTORS - local_bits
    count = lax.axis_size("tensor")
    chips = lax.axis_size("dp") // 2
    hp = halves // count
    dp = lax.axis_index("dp").astype(jnp.int32)
    tensor = lax.axis_index("tensor").astype(jnp.int32)
    core = dp & 1
    chip = dp >> 1
    grouped = factors.reshape(FACTORS, groups, LANES, 2 * HALF)
    aligned = hp == PER
    place = jnp.stack([tensor, chip, core])

    slices = [
        lax.dynamic_slice_in_dim(out_grad, (chip ^ r) * 2 * features, 2 * features, 1)
        for r in range(1, chips)
    ]
    grouped, slices = lax.optimization_barrier((grouped, slices))

    if aligned:
        own_mixing = prepare_mixing(grouped, jnp.stack([tensor, core]), local_bits)
        own_mixing = lax.all_to_all(own_mixing, "tensor", 0, 0)
        other_mixing = flip(own_mixing, "dp", 1)
        order = jnp.stack([core, core])
    else:
        row_index = jnp.arange(HALF, dtype=jnp.int32)[None, None, :, None]
        col_index = jnp.arange(2 * HALF, dtype=jnp.int32)[None, None, None, :]
        bits = (tensor >> jnp.arange(cross, dtype=jnp.int32)) & 1
        select = col_index == bits[:, None, None, None] * HALF + row_index
        mixing = (factors[local_bits:] + select.astype(F32)).astype(BF16)
        mixing = mixing.reshape(cross, count, hp * HALF, 2 * HALF).transpose(1, 0, 2, 3)
        mixing = lax.all_to_all(mixing, "tensor", 0, 0).transpose(1, 0, 2, 3)
        mixing = mixing.reshape(cross, groups, LANES, 2 * HALF).transpose(1, 0, 2, 3)
        mixing = jnp.concatenate([mixing[:, :, :128], mixing[:, :, 128:]], axis=-1)
        own_mixing, other_mixing = mixing[:, :, :64], mixing[:, :, 64:]
        order = jnp.stack([0 * core, core])

    other_weight = flip(down_weight, "dp", 1)

    strides = [hp * 2**bit for bit in range(cross)]
    crossing = [flip(part, "dp", 2 * (r + 1)) for r, part in enumerate(slices)]
    saved_local, values = forward_local(gate_pre, up_pre, grouped, local_bits)
    values, crossing = lax.optimization_barrier((values, crossing))

    values = swap_layout(values, count)
    half = groups // 2
    weights = down_weight, other_weight, place
    sent = [
        [back_matmul(part, lambda c: 0, *weights, BF16, begin, half) for part in crossing]
        for begin in (0, half)
    ]
    received = [
        [flip(part, "dp", 2 * (r + 1)) for r, part in enumerate(parts)] for parts in sent
    ]
    values, _ = lax.optimization_barrier((values, sent))
    saved_cross, values = forward_cross(values, own_mixing, other_mixing, order, strides)
    out_grad, _ = lax.optimization_barrier((out_grad, sent))
    back = back_matmul(out_grad, lambda c: 2 * c[1], *weights, F32, 0, groups)
    sums = []
    for n, terms in enumerate(received):
        total = back[n * half : (n + 1) * half]
        for term in terms:
            total = total + term.astype(F32)
        sums.append(total.astype(BF16))
    back = jnp.concatenate(sums, axis=0)
    back = swap_layout(back, count)
    values, back = lax.optimization_barrier((values, back))
    values = swap_layout(values, count)
    back, grads_cross = backward_cross(back, saved_cross, own_mixing, other_mixing, order, strides)
    mine_cross = over_cores(grads_cross)
    if aligned:
        back = join_rows(back, mine_cross)
    values, back, mine_cross = lax.optimization_barrier((values, back, mine_cross))
    all_values = [values] + [flip(values, "dp", 2 * r) for r in range(1, chips)]
    back = swap_layout(back, count)

    circle = cycle(count)
    spot = jnp.argmax(jnp.array(circle, jnp.int32) == tensor).astype(jnp.int32)
    steps = (spot + jnp.arange(count, dtype=jnp.int32)) % count
    ring = jnp.where(steps < count // 2, 2 * steps, 2 * (count - steps) - 1)
    shares = output_matmul(all_values, down_weight, other_weight, ring)
    back, shares, mine_cross = lax.optimization_barrier((back, shares, mine_cross))
    if aligned:
        mine_cross = split_rows(back, rows, cross)
    else:
        mine_cross = to_owners(mine_cross, core, cross, count, hp)
    middle = local_bits // 2

    def first_half():
        return backward_local(back, saved_local, grouped, order, middle, local_bits)

    def second_half(first):
        lower, grads = first
        results = backward_local(lower, saved_local, grouped, order, 0, middle, gate_pre, up_pre)
        return results, mine_cross, (grads[0], flip(grads[1], "dp", 1))

    summed, second = ring_sum(shares, circle, first_half, second_half)
    (gate_grad, up_grad, grads_low), mine_cross, high_pair = second
    mine_high = (high_pair[0] + high_pair[1]).astype(BF16)
    piece = jnp.stack([summed[0]] + [flip(summed[r], "dp", 2 * r) for r in range(1, chips)])
    gathered = ring_gather(piece, circle)

    scale = 1.0 / math.sqrt(rows * lax.axis_size("dp"))
    parts_cross = (local_bits,) + with_other(over_chips(mine_cross, chips))
    parts_high = (middle,) + with_other(over_chips(mine_high, chips))
    early = place_grads([parts_high, parts_cross], order, factors.shape, scale)
    own_low = over_chips(over_cores(grads_low), chips)
    own_low, gathered, early = lax.optimization_barrier((own_low, gathered, early))
    parts_low = (0,) + with_other(own_low)
    output = place_output(gathered, ring, place)
    factor_grads = place_grads([parts_low], order, factors.shape, scale, early)
    return (output, gate_grad, up_grad, factor_grads)


def solution(mesh):
    return jax.shard_map(
        body,
        mesh=mesh,
        in_specs=(
            P("dp", "tensor"),
            P("dp", "tensor"),
            P("tensor", "dp"),
            P(None, "tensor", None, None),
            P("dp", None),
        ),
        out_specs=(
            P("dp", None),
            P("dp", "tensor"),
            P("dp", "tensor"),
            P(None, "tensor", None, None),
        ),
        check_vma=False,
    )
```

```python
import functools
import math

import jax
import jax.numpy as jnp
from jax import lax
from jax.experimental import pallas as pl
from jax.experimental.pallas import tpu as pltpu
from jax.sharding import PartitionSpec as P

HALF = 32
FACTORS = 9
LANES = 256
PER = LANES // HALF
VMEM_LIMIT = 48 * 1024 * 1024


def estimate(microseconds):
    return pl.CostEstimate(flops=0, transcendentals=0, bytes_accessed=int(3.6e5 * microseconds))


F32 = jnp.float32
BF16 = jnp.bfloat16


def in_hbm(shape, dtype):
    return pltpu.HBM(shape, dtype)


def from_hbm(*arrays):
    return [pltpu.with_memory_space_constraint(array, pltpu.HBM) for array in arrays]


def iota(shape, axis):
    return lax.broadcasted_iota(jnp.int32, shape, axis)


def with_identity(block, stride, group):
    row = iota((LANES, 2 * HALF), 0)
    col = iota((LANES, 2 * HALF), 1)
    if stride < PER:
        bit = (row // HALF // stride) & 1
    else:
        bit = (group // (stride // PER)) & 1
    select = (col == bit * HALF + (row & (HALF - 1))).astype(F32)
    return (block + select).astype(BF16)


def spread_matrix(depth, bit, offset):
    col = iota((depth, LANES), 0)
    lane = iota((depth, LANES), 1)
    return (col == bit(lane) * HALF + (lane & (HALF - 1)) + offset).astype(BF16)


def expand(mixing, bit):
    depth = mixing.shape[1]
    full = jnp.dot(mixing, spread_matrix(depth, bit, 0), preferred_element_type=F32)
    if depth == 2 * HALF:
        return full
    rest = jnp.dot(mixing, spread_matrix(depth, bit, 2 * HALF), preferred_element_type=F32)
    return jnp.concatenate([full, rest], axis=0)


def inner_matrix(mixing, stride):
    full = expand(mixing, lambda lane: (lane // HALF // stride) & 1)
    row = iota((LANES, LANES), 0) // HALF
    unit = iota((LANES, LANES), 1) // HALF
    mask = (unit == row) | (unit == (row ^ stride))
    return jnp.where(mask, full, 0.0).astype(BF16)


def outer_matrix(mixing):
    full = jnp.concatenate([expand(mixing, lambda lane: bit) for bit in range(2)], axis=1)
    row = iota((LANES, 2 * LANES), 0) // HALF
    unit = (iota((LANES, 2 * LANES), 1) & (LANES - 1)) // HALF
    return jnp.where(row == unit, full, 0.0).astype(BF16)


def dot_nt(a, b):
    return lax.dot_general(a, b, (((1,), (1,)), ((), ())), preferred_element_type=F32)


def dot_tn(a, b):
    return lax.dot_general(a, b, (((0,), (0,)), ((), ())), preferred_element_type=F32)


def fold(get_tile, columns_of):
    lane = iota((HALF, 128), 1)
    rows = []
    for low in range(PER // 2):
        out = None
        for upper in range(2):
            i = low + upper * (PER // 2)
            for unit_block, source, column in columns_of(i):
                tile = get_tile(source, i, unit_block // 4)
                place = upper * 2 * HALF + column * HALF
                shift = (place - (unit_block % 4) * HALF) % 128
                if shift:
                    tile = pltpu.roll(tile, shift, 1)
                if out is None:
                    out = tile
                else:
                    out = jnp.where((lane >= place) & (lane < place + HALF), tile, out)
        rows.append(out)
    return rows


def apply_forward(values, mixing_of, stride, groups):
    if stride < PER:
        for g in range(groups):
            matrix = inner_matrix(mixing_of(g), stride)
            values[g] = dot_nt(values[g], matrix).astype(BF16)
        return
    step = stride // PER
    for g in range(groups):
        if g & step:
            continue
        h = g | step
        pair = jnp.concatenate([values[g], values[h]], axis=1)
        for member in (g, h):
            new = dot_nt(pair, outer_matrix(mixing_of(member)))
            values[member] = new.astype(BF16)


def apply_backward(grads, inputs, mixing_of, stride, groups, store_grad):
    if stride < PER:
        for g in range(groups):
            matrix = inner_matrix(mixing_of(g), stride)
            grad = grads[g]
            outer = dot_tn(grad, inputs(g))

            def columns_of(i):
                bit = (i // stride) & 1
                return ((i, 0, bit), (i ^ stride, 0, 1 - bit))

            def tile(source, i, part):
                return outer[i * HALF : (i + 1) * HALF, part * 128 : (part + 1) * 128]

            store_grad(g, fold(tile, columns_of))
            grads[g] = jnp.dot(grad, matrix, preferred_element_type=F32).astype(BF16)
        return
    step = stride // PER
    for g in range(groups):
        if g & step:
            continue
        h = g | step
        pair = jnp.concatenate([inputs(g), inputs(h)], axis=1)
        total = None
        for member in (g, h):
            grad = grads[member]
            product = dot_tn(grad, pair)

            def tile(source, i, part):
                column = source * LANES + part * 128
                return product[i * HALF : (i + 1) * HALF, column : column + 128]

            store_grad(member, fold(tile, lambda i: ((i, 0, 0), (i, 1, 1))))
            term = jnp.dot(grad, outer_matrix(mixing_of(member)), preferred_element_type=F32)
            total = term if total is None else total + term
        grads[g] = total[:, :LANES].astype(BF16)
        grads[h] = total[:, LANES:].astype(BF16)


def forward_local(gate_pre, up_pre, factors, count):
    rows, width = gate_pre.shape
    groups = width // LANES

    def kernel(gate_ref, up_ref, factor_ref, saved_ref, out_ref, values):
        k = pl.program_id(0)

        @pl.when(k == 0)
        def _():
            for g in range(groups):
                cut = pl.ds(g * LANES, LANES)
                gate = gate_ref[:, cut].astype(F32)
                hidden = gate * jax.nn.sigmoid(gate) * up_ref[:, cut].astype(F32)
                values[g] = hidden.astype(BF16)

        for step in range(count):

            @pl.when(k == step)
            def _(step=step):
                saved_ref[0] = values[...]
                stride = 2**step
                apply_forward(
                    values,
                    lambda g: with_identity(factor_ref[0, g], stride, g),
                    stride,
                    groups,
                )

        @pl.when(k == count - 1)
        def _():
            out_ref[...] = values[...]

    shape = (groups, rows, LANES)
    return pl.pallas_call(
        kernel,
        grid=(count,),
        in_specs=[
            pl.BlockSpec((rows, width), lambda k: (0, 0)),
            pl.BlockSpec((rows, width), lambda k: (0, 0)),
            pl.BlockSpec((1, groups, LANES, 2 * HALF), lambda k: (k, 0, 0, 0)),
        ],
        out_specs=[
            pl.BlockSpec((1,) + shape, lambda k: (k, 0, 0, 0)),
            pl.BlockSpec(shape, lambda k: (0, 0, 0)),
        ],
        out_shape=[
            in_hbm((count,) + shape, BF16),
            in_hbm(shape, BF16),
        ],
        scratch_shapes=[pltpu.VMEM(shape, BF16)],
        compiler_params=pltpu.CompilerParams(vmem_limit_bytes=VMEM_LIMIT),
        name="forward_local",
        cost_estimate=estimate(11),
    )(*from_hbm(gate_pre, up_pre, factors))


def prepare_mixing(factors, place, local_bits):
    _, groups, _, _ = factors.shape
    cross = factors.shape[0] - local_bits
    half = LANES // 4

    def kernel(place_ref, low_ref, high_ref, out_ref):
        bit = lax.shift_right_logical(place_ref[0], pl.program_id(0)) & 1
        row = iota((half, 2 * HALF), 0) & (HALF - 1)
        select = (iota((half, 2 * HALF), 1) == bit * HALF + row).astype(F32)
        for g in range(groups):
            low = low_ref[0, g] + select
            high = high_ref[0, g] + select
            out_ref[g, 0] = jnp.concatenate([low, high], axis=1).astype(BF16)

    def spec(offset):
        return pl.BlockSpec(
            (1, groups, half, 2 * HALF), lambda k, c: (local_bits + k, 0, c[1] + offset, 0)
        )

    return pl.pallas_call(
        kernel,
        grid_spec=pltpu.PrefetchScalarGridSpec(
            num_scalar_prefetch=1,
            grid=(cross,),
            in_specs=[spec(0), spec(2)],
            out_specs=pl.BlockSpec((groups, 1, half, 128), lambda k, c: (0, k, 0, 0)),
        ),
        out_shape=in_hbm((groups, cross, half, 128), BF16),
        compiler_params=pltpu.CompilerParams(vmem_limit_bytes=VMEM_LIMIT),
        name="prepare_mixing",
        cost_estimate=estimate(3),
    )(place, *from_hbm(factors, factors))


def packed_block(core, own_ref, other_ref, g):
    own, other = own_ref[g, 0], other_ref[g, 0]
    first = jnp.where(core == 0, own, other)
    second = jnp.where(core == 0, other, own)
    return jnp.concatenate([first, second], axis=0)


def store_tiles(grad_ref, core, g, tiles):
    for low, tile in enumerate(tiles):
        row = (low % 2) * HALF
        grad_ref[(low // 2) ^ core, g, 0, row : row + HALF, :] = tile


def forward_cross(values_in, own_mixing, other_mixing, order, strides):
    groups, rows, _ = values_in.shape
    count = len(strides)

    def kernel(order_ref, in_ref, own_ref, other_ref, saved_ref, out_ref, values):
        k = pl.program_id(0)

        @pl.when(k == 0)
        def _():
            values[...] = in_ref[...]

        for step in range(count):

            @pl.when(k == step)
            def _(step=step):
                saved_ref[0] = values[...]
                apply_forward(
                    values,
                    lambda g: packed_block(order_ref[0], own_ref, other_ref, g),
                    strides[step],
                    groups,
                )

        @pl.when(k == count - 1)
        def _():
            out_ref[...] = values[...]

    shape = (groups, rows, LANES)
    mixing_spec = pl.BlockSpec((groups, 1, LANES // 4, 128), lambda k, c: (0, k, 0, 0))
    return pl.pallas_call(
        kernel,
        grid_spec=pltpu.PrefetchScalarGridSpec(
            num_scalar_prefetch=1,
            grid=(count,),
            in_specs=[pl.BlockSpec(shape, lambda k, c: (0, 0, 0)), mixing_spec, mixing_spec],
            out_specs=[
                pl.BlockSpec((1,) + shape, lambda k, c: (k, 0, 0, 0)),
                pl.BlockSpec(shape, lambda k, c: (0, 0, 0)),
            ],
            scratch_shapes=[pltpu.VMEM(shape, BF16)],
        ),
        out_shape=[
            in_hbm((count,) + shape, BF16),
            in_hbm(shape, BF16),
        ],
        compiler_params=pltpu.CompilerParams(vmem_limit_bytes=VMEM_LIMIT),
        name="forward_cross",
        cost_estimate=estimate(5),
    )(order, *from_hbm(values_in, own_mixing, other_mixing))


def backward_cross(back, saved, own_mixing, other_mixing, order, strides):
    groups, rows, _ = back.shape
    count = len(strides)
    last = count - 1

    def kernel(order_ref, in_ref, saved_ref, own_ref, other_ref, out_ref, grad_ref, grads):
        k = pl.program_id(0)

        @pl.when(k == 0)
        def _():
            grads[...] = in_ref[...]

        for step in range(count):

            @pl.when(k == step)
            def _(step=step):
                apply_backward(
                    grads,
                    lambda g: saved_ref[0, g],
                    lambda g: packed_block(order_ref[0], own_ref, other_ref, g),
                    strides[last - step],
                    groups,
                    lambda g, tiles: store_tiles(grad_ref, order_ref[1], g, tiles),
                )

        @pl.when(k == last)
        def _():
            out_ref[...] = grads[...]

    shape = (groups, rows, LANES)
    mixing_spec = pl.BlockSpec((groups, 1, LANES // 4, 128), lambda k, c: (0, last - k, 0, 0))
    return pl.pallas_call(
        kernel,
        grid_spec=pltpu.PrefetchScalarGridSpec(
            num_scalar_prefetch=1,
            grid=(count,),
            in_specs=[
                pl.BlockSpec(shape, lambda k, c: (0, 0, 0)),
                pl.BlockSpec((1,) + shape, lambda k, c: (last - k, 0, 0, 0)),
                mixing_spec,
                mixing_spec,
            ],
            out_specs=[
                pl.BlockSpec(shape, lambda k, c: (0, 0, 0)),
                pl.BlockSpec((2, groups, 1, 64, 128), lambda k, c: (0, 0, last - k, 0, 0)),
            ],
            scratch_shapes=[pltpu.VMEM(shape, BF16)],
        ),
        out_shape=[
            in_hbm(shape, BF16),
            in_hbm((2, groups, count, 64, 128), F32),
        ],
        compiler_params=pltpu.CompilerParams(vmem_limit_bytes=VMEM_LIMIT),
        name="backward_cross",
        cost_estimate=estimate(90),
    )(order, *from_hbm(back, saved, own_mixing, other_mixing))


def backward_local(back, saved, factors, order, first, end, gate_pre=None, up_pre=None):
    groups, rows, _ = saved.shape[1:]
    width = groups * LANES
    count = end - first
    final = gate_pre is not None

    def kernel(order_ref, in_ref, saved_ref, factor_ref, *refs):
        if final:
            gate_ref, up_ref, dgate_ref, dup_ref, grad_ref, grads = refs
        else:
            out_ref, grad_ref, grads = refs
        k = pl.program_id(0)

        @pl.when(k == 0)
        def _():
            grads[...] = in_ref[...]

        for step in range(count):

            @pl.when(k == step)
            def _(step=step):
                stride = 2 ** (end - 1 - step)
                apply_backward(
                    grads,
                    lambda g: saved_ref[0, g],
                    lambda g: with_identity(factor_ref[0, g], stride, g),
                    stride,
                    groups,
                    lambda g, tiles: store_tiles(grad_ref, order_ref[1], g, tiles),
                )

        @pl.when(k == count - 1)
        def _():
            if not final:
                out_ref[...] = grads[...]
                return
            for g in range(groups):
                cut = pl.ds(g * LANES, LANES)
                gate = gate_ref[:, cut].astype(F32)
                value = grads[g].astype(F32)
                sig = jax.nn.sigmoid(gate)
                dgate = value * up_ref[:, cut].astype(F32) * sig * (1.0 + gate * (1.0 - sig))
                dgate_ref[:, cut] = dgate.astype(BF16)
                dup_ref[:, cut] = (value * gate * sig).astype(BF16)

    shape = (groups, rows, LANES)
    whole = pl.BlockSpec((rows, width), lambda k, c: (0, 0))
    kept = pl.BlockSpec(shape, lambda k, c: (0, 0, 0))
    whole_shape = in_hbm((rows, width), BF16)
    return pl.pallas_call(
        kernel,
        grid_spec=pltpu.PrefetchScalarGridSpec(
            num_scalar_prefetch=1,
            grid=(count,),
            in_specs=[
                kept,
                pl.BlockSpec((1,) + shape, lambda k, c: (end - 1 - k, 0, 0, 0)),
                pl.BlockSpec((1, groups, LANES, 2 * HALF), lambda k, c: (end - 1 - k, 0, 0, 0)),
            ]
            + ([whole, whole] if final else []),
            out_specs=([whole, whole] if final else [kept])
            + [pl.BlockSpec((2, groups, 1, 64, 128), lambda k, c: (0, 0, count - 1 - k, 0, 0))],
            scratch_shapes=[pltpu.VMEM(shape, BF16)],
        ),
        out_shape=([whole_shape, whole_shape] if final else [in_hbm(shape, BF16)])
        + [in_hbm((2, groups, count, 64, 128), F32)],
        compiler_params=pltpu.CompilerParams(vmem_limit_bytes=VMEM_LIMIT),
        name="backward_local",
        cost_estimate=estimate(90),
    )(order, *from_hbm(back, saved, factors, *([gate_pre, up_pre] if final else [])))


def place_grads(parts, order, shape, scale, before=None):
    groups = parts[0][1][0].shape[0]
    numbers = [own[0].shape[1] for _, own, _ in parts]
    begins = [sum(numbers[:p]) for p in range(len(parts))]
    steps = sum(numbers)
    firsts = [first for first, _, _ in parts]
    arrays = [array for _, own, other in parts for array in own + other]
    terms = len(parts[0][1])

    def factor_at(k):
        index = firsts[0] + k
        for begin, first in zip(begins[1:], firsts[1:]):
            index = jnp.where(k >= begin, first + k - begin, index)
        return index

    def kernel(order_ref, *refs):
        out_ref = refs[-1]
        k = pl.program_id(0)
        for p in range(len(parts)):
            own = refs[2 * terms * p : 2 * terms * p + terms]
            other = refs[2 * terms * p + terms : 2 * terms * (p + 1)]

            @pl.when((k >= begins[p]) & (k < begins[p] + numbers[p]))
            def _(own=own, other=other):
                for g in range(groups):
                    for members, swap in ((own, 0), (other, 1)):
                        total = members[0][g, 0].astype(F32)
                        for member in members[1:]:
                            total = total + member[g, 0].astype(F32)
                        total = total * scale
                        turned = pltpu.roll(total, 64, 1)
                        start = ((order_ref[1] ^ swap) * 2) + g * PER
                        for low in range(2):
                            row = low * HALF
                            out_ref[0, start + low] = total[row : row + HALF, : 2 * HALF]
                            out_ref[0, start + low + PER // 2] = turned[row : row + HALF, : 2 * HALF]

    def spec(p):
        return pl.BlockSpec(
            (groups, 1, 64, 128),
            lambda k, c: (0, jnp.clip(k - begins[p], 0, numbers[p] - 1), 0, 0),
        )

    in_specs = [spec(p) for p in range(len(parts)) for _ in range(2 * terms)]
    if before is not None:
        in_specs.append(pl.BlockSpec(memory_space=pl.ANY))
        arrays.append(before)
    return pl.pallas_call(
        kernel,
        grid_spec=pltpu.PrefetchScalarGridSpec(
            num_scalar_prefetch=1,
            grid=(steps,),
            in_specs=in_specs,
            out_specs=pl.BlockSpec((1,) + shape[1:], lambda k, c: (factor_at(k), 0, 0, 0)),
        ),
        out_shape=in_hbm(shape, F32),
        input_output_aliases={} if before is None else {len(arrays): 0},
        compiler_params=pltpu.CompilerParams(vmem_limit_bytes=VMEM_LIMIT),
        name="place_grads",
        cost_estimate=estimate(4),
    )(order, *arrays)


def back_matmul(grads, first, own_weight, other_weight, place, dtype, begin, groups):
    rows = grads.shape[0]
    features = own_weight.shape[1]

    def kernel(place_ref, a_ref, b_ref, w_ref, v_ref, out_ref):
        out_ref[0] = (dot_nt(a_ref[...], w_ref[...]) + dot_nt(b_ref[...], v_ref[...])).astype(dtype)

    weights = pl.BlockSpec((LANES, features), lambda g, c: (begin + g, 0))
    return pl.pallas_call(
        kernel,
        grid_spec=pltpu.PrefetchScalarGridSpec(
            num_scalar_prefetch=1,
            grid=(groups,),
            in_specs=[
                pl.BlockSpec((rows, features), lambda g, c: (0, first(c) + c[2])),
                pl.BlockSpec((rows, features), lambda g, c: (0, first(c) + 1 - c[2])),
                weights,
                weights,
            ],
            out_specs=pl.BlockSpec((1, rows, LANES), lambda g, c: (g, 0, 0)),
        ),
        out_shape=in_hbm((groups, rows, LANES), dtype),
        compiler_params=pltpu.CompilerParams(vmem_limit_bytes=VMEM_LIMIT),
        name="back_matmul",
        cost_estimate=estimate(5),
    )(place, *from_hbm(grads, grads, own_weight, other_weight))


def output_matmul(values, chip, chips, own_weight, other_weight, ring, before=()):
    groups, rows, _ = values.shape
    features = own_weight.shape[1]
    tile = min(2 * LANES, features)
    tiles = features // tile
    pieces = ring.shape[0]
    part = rows // pieces

    def kernel(ring_ref, value_ref, own_ref, other_ref, *refs):
        out_refs, total_ref, left_ref = refs[len(before) : -2], refs[-2], refs[-1]
        j = pl.program_id(0)

        @pl.when(j == 0)
        def _():
            for g in range(groups):
                left_ref[:, g * LANES : (g + 1) * LANES] = value_ref[g]

        def run(w_ref):
            total = jnp.dot(left_ref[...], w_ref[...], preferred_element_type=F32)
            total_ref[...] = total.astype(BF16)
            for r in range(pieces):
                start = pl.multiple_of(ring_ref[r] * part, part)
                out_refs[r][0] = total_ref[pl.ds(start, part), :]

        @pl.when(j < tiles)
        def _():
            run(own_ref)

        @pl.when(j >= tiles)
        def _():
            run(other_ref)

    weight_shape = (groups * LANES, tile)
    return pl.pallas_call(
        kernel,
        grid_spec=pltpu.PrefetchScalarGridSpec(
            num_scalar_prefetch=1,
            grid=(2 * tiles,),
            in_specs=[
                pl.BlockSpec((groups, rows, LANES), lambda j, c: (0, 0, 0)),
                pl.BlockSpec(weight_shape, lambda j, c: (0, jnp.minimum(j, tiles - 1))),
                pl.BlockSpec(weight_shape, lambda j, c: (0, jnp.maximum(j - tiles, 0))),
            ]
            + [pl.BlockSpec(memory_space=pl.ANY)] * len(before),
            out_specs=[pl.BlockSpec((1, part, tile), lambda j, c: (chip, 0, j))] * pieces,
            scratch_shapes=[
                pltpu.VMEM((rows, tile), BF16),
                pltpu.VMEM((rows, groups * LANES), BF16),
            ],
        ),
        out_shape=[in_hbm((chips, part, 2 * features), BF16)] * pieces,
        input_output_aliases={4 + r: r for r in range(len(before))},
        compiler_params=pltpu.CompilerParams(vmem_limit_bytes=VMEM_LIMIT),
        name="output_matmul",
        cost_estimate=estimate(60),
    )(ring, *from_hbm(values, own_weight, other_weight), *before)


def place_output(pieces, ring, place):
    flat = [(r, n, array) for r, cuts in enumerate(pieces) for n, array in enumerate(cuts)]
    chips, part, _ = pieces[0][0].shape
    features = sum(array.shape[2] for array in pieces[0]) // 2
    shape = (len(pieces) * part, 2 * chips * features)

    def kernel(ring_ref, place_ref, *refs):
        out_ref = refs[-1]
        for (r, n, _), ref in zip(flat, refs[:-1]):
            row = pl.multiple_of(ring_ref[r] * part, part)
            width = ref.shape[2]
            for chip in range(chips):
                for k in range(2):
                    begin = max(k * features - n * width, 0)
                    end = min((k + 1) * features - n * width, width)
                    if begin >= end:
                        continue
                    block = (place_ref[1] ^ chip) * 2 + (place_ref[2] ^ k)
                    column = block * features + (n * width + begin - k * features)
                    column = pl.multiple_of(column, 128)
                    out_ref[pl.ds(row, part), pl.ds(column, end - begin)] = ref[chip, :, begin:end]

    return pl.pallas_call(
        kernel,
        grid_spec=pltpu.PrefetchScalarGridSpec(
            num_scalar_prefetch=2,
            grid=(1,),
            in_specs=[pl.BlockSpec(a.shape, lambda k, c, d: (0, 0, 0)) for _, _, a in flat],
            out_specs=pl.BlockSpec(shape, lambda k, c, d: (0, 0)),
        ),
        out_shape=in_hbm(shape, BF16),
        compiler_params=pltpu.CompilerParams(vmem_limit_bytes=VMEM_LIMIT),
        name="place_output",
        cost_estimate=estimate(3),
    )(ring, place, *[array for _, _, array in flat])


def flip(block, axis, bits):
    count = lax.axis_size(axis)
    return lax.ppermute(block, axis, [(i, i ^ bits) for i in range(count)])


def to_pieces(values, count):
    groups, rows, _ = values.shape
    if groups == count:
        return values
    return values.transpose(1, 0, 2).reshape(rows, count, -1).transpose(1, 0, 2)


def from_pieces(pieces):
    count, rows, lanes = pieces.shape
    if lanes == LANES:
        return pieces
    return pieces.transpose(1, 0, 2).reshape(rows, -1, LANES).transpose(1, 0, 2)


def swap_layout(values, count):
    if values.shape[0] == count:
        return lax.all_to_all(values, "tensor", 0, 0)
    moved = lax.all_to_all(to_pieces(values, count), "tensor", 0, 0)
    return from_pieces(moved)


def add_pair(a, b):
    return a.astype(F32) + b.astype(F32)


def over_chips(mine, chips):
    return [mine] + [flip(mine, "dp", 2 * r) for r in range(1, chips)]


def with_other(own):
    return own, [flip(term, "dp", 1) for term in own]


def over_cores(grads):
    return (grads[0] + flip(grads[1], "dp", 1)).astype(BF16)


def join_rows(values, mine):
    flat = mine.reshape(mine.shape[0], -1, 128)
    middle = flat.shape[1] // 2
    flat = jnp.concatenate([flat[:, :middle], flat[:, middle:]], axis=2)
    return jnp.concatenate([values, flat], axis=1)


def split_rows(joined, rows, cross):
    flat = joined[:, rows:]
    flat = jnp.concatenate([flat[:, :, :128], flat[:, :, 128:]], axis=1)
    return flat.reshape(flat.shape[0], cross, 64, 128)


def to_owners(mine, core, cross, count, hp):
    groups = mine.shape[0]
    mine = mine.reshape(groups, cross, 2, HALF, 2, 2 * HALF)
    other = flip(mine, "dp", 1)
    first = jnp.where(core == 0, mine, other)
    second = jnp.where(core == 0, other, mine)
    full = jnp.stack([first, second], axis=2)
    full = full.transpose(1, 0, 5, 2, 3, 4, 6).reshape(cross, count, hp, HALF, 2 * HALF)
    full = lax.all_to_all(full.transpose(1, 0, 2, 3, 4), "tensor", 0, 0)
    full = full.transpose(1, 0, 2, 3, 4).reshape(cross, groups, 2, 2, 2, HALF, 2 * HALF)
    full = full.transpose(1, 0, 3, 4, 5, 2, 6).reshape(groups, cross, 2, 64, 128)
    return jnp.where(core == 0, full[:, :, 0], full[:, :, 1])


def cycle(count):
    return list(range(0, count, 2)) + list(range(count - 1, 0, -2))


def shift(block, order, step):
    pairs = [(order[i], order[(i + step) % len(order)]) for i in range(len(order))]
    return lax.ppermute(block, "tensor", pairs)


def ring_sum(pieces, order, first_work, second_work):
    count = len(pieces)
    far = count // 2
    cut = pieces[far].shape[2] // 2
    up = shift(pieces[far][:, :, :cut], order, 1)
    down = shift(pieces[far][:, :, cut:], order, -1)
    up, down, first = lax.optimization_barrier((up, down, first_work()))
    for distance in range(far - 1, 0, -1):
        above, below = pieces[distance], pieces[count - distance]
        if distance == far - 1:
            up = jnp.pad(up.astype(F32), ((0, 0), (0, 0), (0, cut)))
            down = jnp.pad(down.astype(F32), ((0, 0), (0, 0), (cut, 0)))
        above = add_pair(above, up).astype(BF16)
        below = add_pair(below, down).astype(BF16)
        up = shift(above, order, 1)
        down = shift(below, order, -1)
        if distance == far - 1:
            up, down, second = lax.optimization_barrier((up, down, second_work(first)))
    total = (pieces[0].astype(F32) + up.astype(F32) + down.astype(F32)).astype(BF16)
    return total, second


def ring_gather(piece, order):
    count = len(order)
    far = count // 2
    cut = piece.shape[2] // 2
    result = [None] * count
    result[0] = [piece]
    up = down = piece
    for distance in range(1, far):
        up = shift(up, order, 1)
        down = shift(down, order, -1)
        result[count - distance] = [up]
        result[distance] = [down]
    result[far] = [shift(up[:, :, :cut], order, 1), shift(down[:, :, cut:], order, -1)]
    return result


def body(gate_pre, up_pre, down_weight, factors, out_grad):
    rows, width = gate_pre.shape
    features = down_weight.shape[1]
    halves = width // HALF
    groups = width // LANES
    local_bits = halves.bit_length() - 1
    cross = FACTORS - local_bits
    count = lax.axis_size("tensor")
    chips = lax.axis_size("dp") // 2
    hp = halves // count
    dp = lax.axis_index("dp").astype(jnp.int32)
    tensor = lax.axis_index("tensor").astype(jnp.int32)
    core = dp & 1
    chip = dp >> 1
    grouped = factors.reshape(FACTORS, groups, LANES, 2 * HALF)
    aligned = hp == PER
    place = jnp.stack([tensor, chip, core])

    slices = [
        lax.dynamic_slice_in_dim(out_grad, (chip ^ r) * 2 * features, 2 * features, 1)
        for r in range(1, chips)
    ]
    grouped, slices = lax.optimization_barrier((grouped, slices))

    if aligned:
        own_mixing = prepare_mixing(grouped, jnp.stack([tensor, core]), local_bits)
        own_mixing = lax.all_to_all(own_mixing, "tensor", 0, 0)
        other_mixing = flip(own_mixing, "dp", 1)
        order = jnp.stack([core, core])
    else:
        row_index = jnp.arange(HALF, dtype=jnp.int32)[None, None, :, None]
        col_index = jnp.arange(2 * HALF, dtype=jnp.int32)[None, None, None, :]
        bits = (tensor >> jnp.arange(cross, dtype=jnp.int32)) & 1
        select = col_index == bits[:, None, None, None] * HALF + row_index
        mixing = (factors[local_bits:] + select.astype(F32)).astype(BF16)
        mixing = mixing.reshape(cross, count, hp * HALF, 2 * HALF).transpose(1, 0, 2, 3)
        mixing = lax.all_to_all(mixing, "tensor", 0, 0).transpose(1, 0, 2, 3)
        mixing = mixing.reshape(cross, groups, LANES, 2 * HALF).transpose(1, 0, 2, 3)
        mixing = jnp.concatenate([mixing[:, :, :128], mixing[:, :, 128:]], axis=-1)
        own_mixing, other_mixing = mixing[:, :, :64], mixing[:, :, 64:]
        order = jnp.stack([0 * core, core])

    other_weight = flip(down_weight, "dp", 1)

    strides = [hp * 2**bit for bit in range(cross)]
    crossing = [flip(part, "dp", 2 * (r + 1)) for r, part in enumerate(slices)]
    saved_local, values = forward_local(gate_pre, up_pre, grouped, local_bits)
    values, crossing = lax.optimization_barrier((values, crossing))

    values = swap_layout(values, count)
    half = groups // 2
    weights = down_weight, other_weight, place
    sent = [
        [back_matmul(part, lambda c: 0, *weights, BF16, begin, half) for part in crossing]
        for begin in (0, half)
    ]
    received = [
        [flip(part, "dp", 2 * (r + 1)) for r, part in enumerate(parts)] for parts in sent
    ]
    values, _ = lax.optimization_barrier((values, sent))
    saved_cross, values = forward_cross(values, own_mixing, other_mixing, order, strides)
    out_grad, _ = lax.optimization_barrier((out_grad, sent))
    back = back_matmul(out_grad, lambda c: 2 * c[1], *weights, F32, 0, groups)
    sums = []
    for n, terms in enumerate(received):
        total = back[n * half : (n + 1) * half]
        for term in terms:
            total = total + term.astype(F32)
        sums.append(total.astype(BF16))
    back = jnp.concatenate(sums, axis=0)
    back = swap_layout(back, count)
    values, back = lax.optimization_barrier((values, back))
    values = swap_layout(values, count)
    back, grads_cross = backward_cross(back, saved_cross, own_mixing, other_mixing, order, strides)
    mine_cross = over_cores(grads_cross)
    if aligned:
        back = join_rows(back, mine_cross)
    values, back, mine_cross = lax.optimization_barrier((values, back, mine_cross))
    all_values = [values] + [flip(values, "dp", 2 * r) for r in range(1, chips)]
    back = swap_layout(back, count)

    circle = cycle(count)
    spot = jnp.argmax(jnp.array(circle, jnp.int32) == tensor).astype(jnp.int32)
    steps = (spot + jnp.arange(count, dtype=jnp.int32)) % count
    ring = jnp.where(steps < count // 2, 2 * steps, 2 * (count - steps) - 1)
    shares = ()
    for r in range(chips):
        if r == 1:
            all_values, shares = lax.optimization_barrier((all_values, shares))
        shares = output_matmul(
            all_values[r], r, chips, down_weight, other_weight, ring, tuple(shares)
        )
    back, shares, mine_cross = lax.optimization_barrier((back, shares, mine_cross))
    if aligned:
        mine_cross = split_rows(back, rows, cross)
    else:
        mine_cross = to_owners(mine_cross, core, cross, count, hp)
    middle = local_bits // 2

    def first_half():
        return backward_local(back, saved_local, grouped, order, middle, local_bits)

    def second_half(first):
        lower, grads = first
        results = backward_local(lower, saved_local, grouped, order, 0, middle, gate_pre, up_pre)
        return results, mine_cross, (grads[0], flip(grads[1], "dp", 1))

    summed, second = ring_sum(shares, circle, first_half, second_half)
    (gate_grad, up_grad, grads_low), mine_cross, high_pair = second
    mine_high = (high_pair[0] + high_pair[1]).astype(BF16)
    piece = jnp.stack([summed[0]] + [flip(summed[r], "dp", 2 * r) for r in range(1, chips)])
    gathered = ring_gather(piece, circle)

    scale = 1.0 / math.sqrt(rows * lax.axis_size("dp"))
    parts_cross = (local_bits,) + with_other(over_chips(mine_cross, chips))
    parts_high = (middle,) + with_other(over_chips(mine_high, chips))
    early = place_grads([parts_high, parts_cross], order, factors.shape, scale)
    own_low = over_chips(over_cores(grads_low), chips)
    own_low, gathered, early = lax.optimization_barrier((own_low, gathered, early))
    parts_low = (0,) + with_other(own_low)
    output = place_output(gathered, ring, place)
    factor_grads = place_grads([parts_low], order, factors.shape, scale, early)
    return (output, gate_grad, up_grad, factor_grads)


def solution(mesh):
    return jax.shard_map(
        body,
        mesh=mesh,
        in_specs=(
            P("dp", "tensor"),
            P("dp", "tensor"),
            P("tensor", "dp"),
            P(None, "tensor", None, None),
            P("dp", None),
        ),
        out_specs=(
            P("dp", None),
            P("dp", "tensor"),
            P("dp", "tensor"),
            P(None, "tensor", None, None),
        ),
        check_vma=False,
    )
```

```python
import functools
import math

import jax
import jax.numpy as jnp
from jax import lax
from jax.experimental import pallas as pl
from jax.experimental.pallas import tpu as pltpu
from jax.sharding import PartitionSpec as P

HALF = 32
FACTORS = 9
LANES = 256
PER = LANES // HALF
VMEM_LIMIT = 48 * 1024 * 1024


def estimate(microseconds):
    return pl.CostEstimate(flops=0, transcendentals=0, bytes_accessed=int(3.6e5 * microseconds))


F32 = jnp.float32
BF16 = jnp.bfloat16


def in_hbm(shape, dtype):
    return pltpu.HBM(shape, dtype)


def from_hbm(*arrays):
    return [pltpu.with_memory_space_constraint(array, pltpu.HBM) for array in arrays]


def iota(shape, axis):
    return lax.broadcasted_iota(jnp.int32, shape, axis)


def with_identity(block, stride, group):
    row = iota((LANES, 2 * HALF), 0)
    col = iota((LANES, 2 * HALF), 1)
    if stride < PER:
        bit = (row // HALF // stride) & 1
    else:
        bit = (group // (stride // PER)) & 1
    select = (col == bit * HALF + (row & (HALF - 1))).astype(F32)
    return (block + select).astype(BF16)


def spread_matrix(depth, bit, offset):
    col = iota((depth, LANES), 0)
    lane = iota((depth, LANES), 1)
    return (col == bit(lane) * HALF + (lane & (HALF - 1)) + offset).astype(BF16)


def expand(mixing, bit):
    depth = mixing.shape[1]
    full = jnp.dot(mixing, spread_matrix(depth, bit, 0), preferred_element_type=F32)
    if depth == 2 * HALF:
        return full
    rest = jnp.dot(mixing, spread_matrix(depth, bit, 2 * HALF), preferred_element_type=F32)
    return jnp.concatenate([full, rest], axis=0)


def inner_matrix(mixing, stride):
    full = expand(mixing, lambda lane: (lane // HALF // stride) & 1)
    row = iota((LANES, LANES), 0) // HALF
    unit = iota((LANES, LANES), 1) // HALF
    mask = (unit == row) | (unit == (row ^ stride))
    return jnp.where(mask, full, 0.0).astype(BF16)


def outer_matrix(mixing):
    full = jnp.concatenate([expand(mixing, lambda lane: bit) for bit in range(2)], axis=1)
    row = iota((LANES, 2 * LANES), 0) // HALF
    unit = (iota((LANES, 2 * LANES), 1) & (LANES - 1)) // HALF
    return jnp.where(row == unit, full, 0.0).astype(BF16)


def dot_nt(a, b):
    return lax.dot_general(a, b, (((1,), (1,)), ((), ())), preferred_element_type=F32)


def dot_tn(a, b):
    return lax.dot_general(a, b, (((0,), (0,)), ((), ())), preferred_element_type=F32)


def fold(get_tile, columns_of):
    lane = iota((HALF, 128), 1)
    rows = []
    for low in range(PER // 2):
        out = None
        for upper in range(2):
            i = low + upper * (PER // 2)
            for unit_block, source, column in columns_of(i):
                tile = get_tile(source, i, unit_block // 4)
                place = upper * 2 * HALF + column * HALF
                shift = (place - (unit_block % 4) * HALF) % 128
                if shift:
                    tile = pltpu.roll(tile, shift, 1)
                if out is None:
                    out = tile
                else:
                    out = jnp.where((lane >= place) & (lane < place + HALF), tile, out)
        rows.append(out)
    return rows


def apply_forward(values, mixing_of, stride, groups):
    if stride < PER:
        for g in range(groups):
            matrix = inner_matrix(mixing_of(g), stride)
            values[g] = dot_nt(values[g], matrix).astype(BF16)
        return
    step = stride // PER
    for g in range(groups):
        if g & step:
            continue
        h = g | step
        pair = jnp.concatenate([values[g], values[h]], axis=1)
        for member in (g, h):
            new = dot_nt(pair, outer_matrix(mixing_of(member)))
            values[member] = new.astype(BF16)


def apply_backward(grads, inputs, mixing_of, stride, groups, store_grad):
    if stride < PER:
        for g in range(groups):
            matrix = inner_matrix(mixing_of(g), stride)
            grad = grads[g]
            outer = dot_tn(grad, inputs(g))

            def columns_of(i):
                bit = (i // stride) & 1
                return ((i, 0, bit), (i ^ stride, 0, 1 - bit))

            def tile(source, i, part):
                return outer[i * HALF : (i + 1) * HALF, part * 128 : (part + 1) * 128]

            store_grad(g, fold(tile, columns_of))
            grads[g] = jnp.dot(grad, matrix, preferred_element_type=F32).astype(BF16)
        return
    step = stride // PER
    for g in range(groups):
        if g & step:
            continue
        h = g | step
        pair = jnp.concatenate([inputs(g), inputs(h)], axis=1)
        total = None
        for member in (g, h):
            grad = grads[member]
            product = dot_tn(grad, pair)

            def tile(source, i, part):
                column = source * LANES + part * 128
                return product[i * HALF : (i + 1) * HALF, column : column + 128]

            store_grad(member, fold(tile, lambda i: ((i, 0, 0), (i, 1, 1))))
            term = jnp.dot(grad, outer_matrix(mixing_of(member)), preferred_element_type=F32)
            total = term if total is None else total + term
        grads[g] = total[:, :LANES].astype(BF16)
        grads[h] = total[:, LANES:].astype(BF16)


def forward_local(gate_pre, up_pre, factors, count):
    rows, width = gate_pre.shape
    groups = width // LANES

    def kernel(gate_ref, up_ref, factor_ref, saved_ref, out_ref, values):
        k = pl.program_id(0)

        @pl.when(k == 0)
        def _():
            for g in range(groups):
                cut = pl.ds(g * LANES, LANES)
                gate = gate_ref[:, cut].astype(F32)
                hidden = gate * jax.nn.sigmoid(gate) * up_ref[:, cut].astype(F32)
                values[g] = hidden.astype(BF16)

        for step in range(count):

            @pl.when(k == step)
            def _(step=step):
                saved_ref[0] = values[...]
                stride = 2**step
                apply_forward(
                    values,
                    lambda g: with_identity(factor_ref[0, g], stride, g),
                    stride,
                    groups,
                )

        @pl.when(k == count - 1)
        def _():
            out_ref[...] = values[...]

    shape = (groups, rows, LANES)
    return pl.pallas_call(
        kernel,
        grid=(count,),
        in_specs=[
            pl.BlockSpec((rows, width), lambda k: (0, 0)),
            pl.BlockSpec((rows, width), lambda k: (0, 0)),
            pl.BlockSpec((1, groups, LANES, 2 * HALF), lambda k: (k, 0, 0, 0)),
        ],
        out_specs=[
            pl.BlockSpec((1,) + shape, lambda k: (k, 0, 0, 0)),
            pl.BlockSpec(shape, lambda k: (0, 0, 0)),
        ],
        out_shape=[
            in_hbm((count,) + shape, BF16),
            in_hbm(shape, BF16),
        ],
        scratch_shapes=[pltpu.VMEM(shape, BF16)],
        compiler_params=pltpu.CompilerParams(vmem_limit_bytes=VMEM_LIMIT),
        name="forward_local",
        cost_estimate=estimate(11),
    )(*from_hbm(gate_pre, up_pre, factors))


def prepare_mixing(factors, place, local_bits):
    _, groups, _, _ = factors.shape
    cross = factors.shape[0] - local_bits
    half = LANES // 4

    def kernel(place_ref, low_ref, high_ref, out_ref):
        bit = lax.shift_right_logical(place_ref[0], pl.program_id(0)) & 1
        row = iota((half, 2 * HALF), 0) & (HALF - 1)
        select = (iota((half, 2 * HALF), 1) == bit * HALF + row).astype(F32)
        for g in range(groups):
            low = low_ref[0, g] + select
            high = high_ref[0, g] + select
            out_ref[g, 0] = jnp.concatenate([low, high], axis=1).astype(BF16)

    def spec(offset):
        return pl.BlockSpec(
            (1, groups, half, 2 * HALF), lambda k, c: (local_bits + k, 0, c[1] + offset, 0)
        )

    return pl.pallas_call(
        kernel,
        grid_spec=pltpu.PrefetchScalarGridSpec(
            num_scalar_prefetch=1,
            grid=(cross,),
            in_specs=[spec(0), spec(2)],
            out_specs=pl.BlockSpec((groups, 1, half, 128), lambda k, c: (0, k, 0, 0)),
        ),
        out_shape=in_hbm((groups, cross, half, 128), BF16),
        compiler_params=pltpu.CompilerParams(vmem_limit_bytes=VMEM_LIMIT),
        name="prepare_mixing",
        cost_estimate=estimate(3),
    )(place, *from_hbm(factors, factors))


def packed_block(core, own_ref, other_ref, g):
    own, other = own_ref[g, 0], other_ref[g, 0]
    first = jnp.where(core == 0, own, other)
    second = jnp.where(core == 0, other, own)
    return jnp.concatenate([first, second], axis=0)


def store_tiles(grad_ref, core, g, tiles):
    for low, tile in enumerate(tiles):
        row = (low % 2) * HALF
        grad_ref[(low // 2) ^ core, g, 0, row : row + HALF, :] = tile


def forward_cross(values_in, own_mixing, other_mixing, order, strides):
    groups, rows, _ = values_in.shape
    count = len(strides)

    def kernel(order_ref, in_ref, own_ref, other_ref, saved_ref, out_ref, values):
        k = pl.program_id(0)

        @pl.when(k == 0)
        def _():
            values[...] = in_ref[...]

        for step in range(count):

            @pl.when(k == step)
            def _(step=step):
                saved_ref[0] = values[...]
                apply_forward(
                    values,
                    lambda g: packed_block(order_ref[0], own_ref, other_ref, g),
                    strides[step],
                    groups,
                )

        @pl.when(k == count - 1)
        def _():
            out_ref[...] = values[...]

    shape = (groups, rows, LANES)
    mixing_spec = pl.BlockSpec((groups, 1, LANES // 4, 128), lambda k, c: (0, k, 0, 0))
    return pl.pallas_call(
        kernel,
        grid_spec=pltpu.PrefetchScalarGridSpec(
            num_scalar_prefetch=1,
            grid=(count,),
            in_specs=[pl.BlockSpec(shape, lambda k, c: (0, 0, 0)), mixing_spec, mixing_spec],
            out_specs=[
                pl.BlockSpec((1,) + shape, lambda k, c: (k, 0, 0, 0)),
                pl.BlockSpec(shape, lambda k, c: (0, 0, 0)),
            ],
            scratch_shapes=[pltpu.VMEM(shape, BF16)],
        ),
        out_shape=[
            in_hbm((count,) + shape, BF16),
            in_hbm(shape, BF16),
        ],
        compiler_params=pltpu.CompilerParams(vmem_limit_bytes=VMEM_LIMIT),
        name="forward_cross",
        cost_estimate=estimate(5),
    )(order, *from_hbm(values_in, own_mixing, other_mixing))


def backward_cross(back, saved, own_mixing, other_mixing, order, strides):
    groups, rows, _ = back.shape
    count = len(strides)
    last = count - 1

    def kernel(order_ref, in_ref, saved_ref, own_ref, other_ref, out_ref, grad_ref, grads):
        k = pl.program_id(0)

        @pl.when(k == 0)
        def _():
            grads[...] = in_ref[...]

        for step in range(count):

            @pl.when(k == step)
            def _(step=step):
                apply_backward(
                    grads,
                    lambda g: saved_ref[0, g],
                    lambda g: packed_block(order_ref[0], own_ref, other_ref, g),
                    strides[last - step],
                    groups,
                    lambda g, tiles: store_tiles(grad_ref, order_ref[1], g, tiles),
                )

        @pl.when(k == last)
        def _():
            out_ref[...] = grads[...]

    shape = (groups, rows, LANES)
    mixing_spec = pl.BlockSpec((groups, 1, LANES // 4, 128), lambda k, c: (0, last - k, 0, 0))
    return pl.pallas_call(
        kernel,
        grid_spec=pltpu.PrefetchScalarGridSpec(
            num_scalar_prefetch=1,
            grid=(count,),
            in_specs=[
                pl.BlockSpec(shape, lambda k, c: (0, 0, 0)),
                pl.BlockSpec((1,) + shape, lambda k, c: (last - k, 0, 0, 0)),
                mixing_spec,
                mixing_spec,
            ],
            out_specs=[
                pl.BlockSpec(shape, lambda k, c: (0, 0, 0)),
                pl.BlockSpec((2, groups, 1, 64, 128), lambda k, c: (0, 0, last - k, 0, 0)),
            ],
            scratch_shapes=[pltpu.VMEM(shape, BF16)],
        ),
        out_shape=[
            in_hbm(shape, BF16),
            in_hbm((2, groups, count, 64, 128), F32),
        ],
        compiler_params=pltpu.CompilerParams(vmem_limit_bytes=VMEM_LIMIT),
        name="backward_cross",
        cost_estimate=estimate(90),
    )(order, *from_hbm(back, saved, own_mixing, other_mixing))


def backward_local(back, saved, factors, order, first, end, gate_pre=None, up_pre=None):
    groups, rows, _ = saved.shape[1:]
    width = groups * LANES
    count = end - first
    final = gate_pre is not None

    def kernel(order_ref, in_ref, saved_ref, factor_ref, *refs):
        if final:
            gate_ref, up_ref, dgate_ref, dup_ref, grad_ref, grads = refs
        else:
            out_ref, grad_ref, grads = refs
        k = pl.program_id(0)

        @pl.when(k == 0)
        def _():
            grads[...] = in_ref[...]

        for step in range(count):

            @pl.when(k == step)
            def _(step=step):
                stride = 2 ** (end - 1 - step)
                apply_backward(
                    grads,
                    lambda g: saved_ref[0, g],
                    lambda g: with_identity(factor_ref[0, g], stride, g),
                    stride,
                    groups,
                    lambda g, tiles: store_tiles(grad_ref, order_ref[1], g, tiles),
                )

        @pl.when(k == count - 1)
        def _():
            if not final:
                out_ref[...] = grads[...]
                return
            for g in range(groups):
                cut = pl.ds(g * LANES, LANES)
                gate = gate_ref[:, cut].astype(F32)
                value = grads[g].astype(F32)
                sig = jax.nn.sigmoid(gate)
                dgate = value * up_ref[:, cut].astype(F32) * sig * (1.0 + gate * (1.0 - sig))
                dgate_ref[:, cut] = dgate.astype(BF16)
                dup_ref[:, cut] = (value * gate * sig).astype(BF16)

    shape = (groups, rows, LANES)
    whole = pl.BlockSpec((rows, width), lambda k, c: (0, 0))
    kept = pl.BlockSpec(shape, lambda k, c: (0, 0, 0))
    whole_shape = in_hbm((rows, width), BF16)
    return pl.pallas_call(
        kernel,
        grid_spec=pltpu.PrefetchScalarGridSpec(
            num_scalar_prefetch=1,
            grid=(count,),
            in_specs=[
                kept,
                pl.BlockSpec((1,) + shape, lambda k, c: (end - 1 - k, 0, 0, 0)),
                pl.BlockSpec((1, groups, LANES, 2 * HALF), lambda k, c: (end - 1 - k, 0, 0, 0)),
            ]
            + ([whole, whole] if final else []),
            out_specs=([whole, whole] if final else [kept])
            + [pl.BlockSpec((2, groups, 1, 64, 128), lambda k, c: (0, 0, count - 1 - k, 0, 0))],
            scratch_shapes=[pltpu.VMEM(shape, BF16)],
        ),
        out_shape=([whole_shape, whole_shape] if final else [in_hbm(shape, BF16)])
        + [in_hbm((2, groups, count, 64, 128), F32)],
        compiler_params=pltpu.CompilerParams(vmem_limit_bytes=VMEM_LIMIT),
        name="backward_local",
        cost_estimate=estimate(90),
    )(order, *from_hbm(back, saved, factors, *([gate_pre, up_pre] if final else [])))


def place_grads(parts, order, shape, scale, before=None):
    groups = parts[0][1][0].shape[0]
    numbers = [own[0].shape[1] for _, own, _ in parts]
    begins = [sum(numbers[:p]) for p in range(len(parts))]
    steps = sum(numbers)
    firsts = [first for first, _, _ in parts]
    arrays = [array for _, own, other in parts for array in own + other]
    terms = len(parts[0][1])

    def factor_at(k):
        index = firsts[0] + k
        for begin, first in zip(begins[1:], firsts[1:]):
            index = jnp.where(k >= begin, first + k - begin, index)
        return index

    def kernel(order_ref, *refs):
        out_ref = refs[-1]
        k = pl.program_id(0)
        for p in range(len(parts)):
            own = refs[2 * terms * p : 2 * terms * p + terms]
            other = refs[2 * terms * p + terms : 2 * terms * (p + 1)]

            @pl.when((k >= begins[p]) & (k < begins[p] + numbers[p]))
            def _(own=own, other=other):
                for g in range(groups):
                    for members, swap in ((own, 0), (other, 1)):
                        total = members[0][g, 0].astype(F32)
                        for member in members[1:]:
                            total = total + member[g, 0].astype(F32)
                        total = total * scale
                        turned = pltpu.roll(total, 64, 1)
                        start = ((order_ref[1] ^ swap) * 2) + g * PER
                        for low in range(2):
                            row = low * HALF
                            out_ref[0, start + low] = total[row : row + HALF, : 2 * HALF]
                            out_ref[0, start + low + PER // 2] = turned[row : row + HALF, : 2 * HALF]

    def spec(p):
        return pl.BlockSpec(
            (groups, 1, 64, 128),
            lambda k, c: (0, jnp.clip(k - begins[p], 0, numbers[p] - 1), 0, 0),
        )

    in_specs = [spec(p) for p in range(len(parts)) for _ in range(2 * terms)]
    if before is not None:
        in_specs.append(pl.BlockSpec(memory_space=pl.ANY))
        arrays.append(before)
    return pl.pallas_call(
        kernel,
        grid_spec=pltpu.PrefetchScalarGridSpec(
            num_scalar_prefetch=1,
            grid=(steps,),
            in_specs=in_specs,
            out_specs=pl.BlockSpec((1,) + shape[1:], lambda k, c: (factor_at(k), 0, 0, 0)),
        ),
        out_shape=in_hbm(shape, F32),
        input_output_aliases={} if before is None else {len(arrays): 0},
        compiler_params=pltpu.CompilerParams(vmem_limit_bytes=VMEM_LIMIT),
        name="place_grads",
        cost_estimate=estimate(4),
    )(order, *arrays)


def back_matmul(grads, first, own_weight, other_weight, place, dtype, begin, groups):
    rows = grads.shape[0]
    features = own_weight.shape[1]

    def kernel(place_ref, a_ref, b_ref, w_ref, v_ref, out_ref):
        out_ref[0] = (dot_nt(a_ref[...], w_ref[...]) + dot_nt(b_ref[...], v_ref[...])).astype(dtype)

    weights = pl.BlockSpec((LANES, features), lambda g, c: (begin + g, 0))
    return pl.pallas_call(
        kernel,
        grid_spec=pltpu.PrefetchScalarGridSpec(
            num_scalar_prefetch=1,
            grid=(groups,),
            in_specs=[
                pl.BlockSpec((rows, features), lambda g, c: (0, first(c) + c[2])),
                pl.BlockSpec((rows, features), lambda g, c: (0, first(c) + 1 - c[2])),
                weights,
                weights,
            ],
            out_specs=pl.BlockSpec((1, rows, LANES), lambda g, c: (g, 0, 0)),
        ),
        out_shape=in_hbm((groups, rows, LANES), dtype),
        compiler_params=pltpu.CompilerParams(vmem_limit_bytes=VMEM_LIMIT),
        name="back_matmul",
        cost_estimate=estimate(5),
    )(place, *from_hbm(grads, grads, own_weight, other_weight))


def output_matmul(values, chip, chips, own_weight, other_weight, ring, before=()):
    groups, rows, _ = values.shape
    features = own_weight.shape[1]
    tile = min(2 * LANES, features)
    tiles = features // tile
    pieces = ring.shape[0]
    part = rows // pieces

    def kernel(ring_ref, value_ref, own_ref, other_ref, *refs):
        out_refs, total_ref, left_ref = refs[len(before) : -2], refs[-2], refs[-1]
        j = pl.program_id(0)

        @pl.when(j == 0)
        def _():
            for g in range(groups):
                left_ref[:, g * LANES : (g + 1) * LANES] = value_ref[g]

        def run(w_ref):
            total = jnp.dot(left_ref[...], w_ref[...], preferred_element_type=F32)
            total_ref[...] = total.astype(BF16)
            for r in range(pieces):
                start = pl.multiple_of(ring_ref[r] * part, part)
                out_refs[r][0] = total_ref[pl.ds(start, part), :]

        @pl.when(j < tiles)
        def _():
            run(own_ref)

        @pl.when(j >= tiles)
        def _():
            run(other_ref)

    weight_shape = (groups * LANES, tile)
    return pl.pallas_call(
        kernel,
        grid_spec=pltpu.PrefetchScalarGridSpec(
            num_scalar_prefetch=1,
            grid=(2 * tiles,),
            in_specs=[
                pl.BlockSpec((groups, rows, LANES), lambda j, c: (0, 0, 0)),
                pl.BlockSpec(weight_shape, lambda j, c: (0, jnp.minimum(j, tiles - 1))),
                pl.BlockSpec(weight_shape, lambda j, c: (0, jnp.maximum(j - tiles, 0))),
            ]
            + [pl.BlockSpec(memory_space=pl.ANY)] * len(before),
            out_specs=[pl.BlockSpec((1, part, tile), lambda j, c: (chip, 0, j))] * pieces,
            scratch_shapes=[
                pltpu.VMEM((rows, tile), BF16),
                pltpu.VMEM((rows, groups * LANES), BF16),
            ],
        ),
        out_shape=[in_hbm((chips, part, 2 * features), BF16)] * pieces,
        input_output_aliases={4 + r: r for r in range(len(before))},
        compiler_params=pltpu.CompilerParams(vmem_limit_bytes=VMEM_LIMIT),
        name="output_matmul",
        cost_estimate=estimate(60),
    )(ring, *from_hbm(values, own_weight, other_weight), *before)


def place_output(pieces, ring, place):
    flat = [(r, n, array) for r, cuts in enumerate(pieces) for n, array in enumerate(cuts)]
    chips, part, _ = pieces[0][0].shape
    features = sum(array.shape[2] for array in pieces[0]) // 2
    shape = (len(pieces) * part, 2 * chips * features)

    def kernel(ring_ref, place_ref, *refs):
        out_ref = refs[-1]
        for (r, n, _), ref in zip(flat, refs[:-1]):
            row = pl.multiple_of(ring_ref[r] * part, part)
            width = ref.shape[2]
            for chip in range(chips):
                for k in range(2):
                    begin = max(k * features - n * width, 0)
                    end = min((k + 1) * features - n * width, width)
                    if begin >= end:
                        continue
                    block = (place_ref[1] ^ chip) * 2 + (place_ref[2] ^ k)
                    column = block * features + (n * width + begin - k * features)
                    column = pl.multiple_of(column, 128)
                    out_ref[pl.ds(row, part), pl.ds(column, end - begin)] = ref[chip, :, begin:end]

    return pl.pallas_call(
        kernel,
        grid_spec=pltpu.PrefetchScalarGridSpec(
            num_scalar_prefetch=2,
            grid=(1,),
            in_specs=[pl.BlockSpec(a.shape, lambda k, c, d: (0, 0, 0)) for _, _, a in flat],
            out_specs=pl.BlockSpec(shape, lambda k, c, d: (0, 0)),
        ),
        out_shape=in_hbm(shape, BF16),
        compiler_params=pltpu.CompilerParams(vmem_limit_bytes=VMEM_LIMIT),
        name="place_output",
        cost_estimate=estimate(3),
    )(ring, place, *[array for _, _, array in flat])


def flip(block, axis, bits):
    count = lax.axis_size(axis)
    return lax.ppermute(block, axis, [(i, i ^ bits) for i in range(count)])


def to_pieces(values, count):
    groups, rows, _ = values.shape
    if groups == count:
        return values
    return values.transpose(1, 0, 2).reshape(rows, count, -1).transpose(1, 0, 2)


def from_pieces(pieces):
    count, rows, lanes = pieces.shape
    if lanes == LANES:
        return pieces
    return pieces.transpose(1, 0, 2).reshape(rows, -1, LANES).transpose(1, 0, 2)


def swap_layout(values, count):
    if values.shape[0] == count:
        return lax.all_to_all(values, "tensor", 0, 0)
    moved = lax.all_to_all(to_pieces(values, count), "tensor", 0, 0)
    return from_pieces(moved)


def add_pair(a, b):
    return a.astype(F32) + b.astype(F32)


def over_chips(mine, chips):
    return [mine] + [flip(mine, "dp", 2 * r) for r in range(1, chips)]


def with_other(own):
    return own, [flip(term, "dp", 1) for term in own]


def over_cores(grads):
    return (grads[0] + flip(grads[1], "dp", 1)).astype(BF16)


def join_rows(values, mine):
    flat = mine.reshape(mine.shape[0], -1, 128)
    middle = flat.shape[1] // 2
    flat = jnp.concatenate([flat[:, :middle], flat[:, middle:]], axis=2)
    return jnp.concatenate([values, flat], axis=1)


def split_rows(joined, rows, cross):
    flat = joined[:, rows:]
    flat = jnp.concatenate([flat[:, :, :128], flat[:, :, 128:]], axis=1)
    return flat.reshape(flat.shape[0], cross, 64, 128)


def to_owners(mine, core, cross, count, hp):
    groups = mine.shape[0]
    mine = mine.reshape(groups, cross, 2, HALF, 2, 2 * HALF)
    other = flip(mine, "dp", 1)
    first = jnp.where(core == 0, mine, other)
    second = jnp.where(core == 0, other, mine)
    full = jnp.stack([first, second], axis=2)
    full = full.transpose(1, 0, 5, 2, 3, 4, 6).reshape(cross, count, hp, HALF, 2 * HALF)
    full = lax.all_to_all(full.transpose(1, 0, 2, 3, 4), "tensor", 0, 0)
    full = full.transpose(1, 0, 2, 3, 4).reshape(cross, groups, 2, 2, 2, HALF, 2 * HALF)
    full = full.transpose(1, 0, 3, 4, 5, 2, 6).reshape(groups, cross, 2, 64, 128)
    return jnp.where(core == 0, full[:, :, 0], full[:, :, 1])


def cycle(count):
    return list(range(0, count, 2)) + list(range(count - 1, 0, -2))


def shift(block, order, step):
    pairs = [(order[i], order[(i + step) % len(order)]) for i in range(len(order))]
    return lax.ppermute(block, "tensor", pairs)


def ring_sum(pieces, order, first_work, second_work):
    count = len(pieces)
    far = count // 2
    cut = pieces[far].shape[2] // 2
    up = shift(pieces[far][:, :, :cut], order, 1)
    down = shift(pieces[far][:, :, cut:], order, -1)
    up, down, first = lax.optimization_barrier((up, down, first_work()))
    for distance in range(far - 1, 0, -1):
        above, below = pieces[distance], pieces[count - distance]
        if distance == far - 1:
            up = jnp.pad(up.astype(F32), ((0, 0), (0, 0), (0, cut)))
            down = jnp.pad(down.astype(F32), ((0, 0), (0, 0), (cut, 0)))
        above = add_pair(above, up).astype(BF16)
        below = add_pair(below, down).astype(BF16)
        up = shift(above, order, 1)
        down = shift(below, order, -1)
        if distance == far - 1:
            up, down, second = lax.optimization_barrier((up, down, second_work(first)))
    total = (pieces[0].astype(F32) + up.astype(F32) + down.astype(F32)).astype(BF16)
    return total, second


def ring_gather(piece, order, ready):
    count = len(order)
    far = count // 2
    cut = piece.shape[2] // 2
    result = [None] * count
    result[0] = [piece]
    up = down = piece
    for distance in range(1, far):
        up = shift(up, order, 1)
        down = shift(down, order, -1)
        if distance == far - 1:
            up, down, ready = lax.optimization_barrier((up, down, ready))
        result[count - distance] = [up]
        result[distance] = [down]
    result[far] = [shift(up[:, :, :cut], order, 1), shift(down[:, :, cut:], order, -1)]
    return result, ready


def body(gate_pre, up_pre, down_weight, factors, out_grad):
    rows, width = gate_pre.shape
    features = down_weight.shape[1]
    halves = width // HALF
    groups = width // LANES
    local_bits = halves.bit_length() - 1
    cross = FACTORS - local_bits
    count = lax.axis_size("tensor")
    chips = lax.axis_size("dp") // 2
    hp = halves // count
    dp = lax.axis_index("dp").astype(jnp.int32)
    tensor = lax.axis_index("tensor").astype(jnp.int32)
    core = dp & 1
    chip = dp >> 1
    grouped = factors.reshape(FACTORS, groups, LANES, 2 * HALF)
    aligned = hp == PER
    place = jnp.stack([tensor, chip, core])

    slices = [
        lax.dynamic_slice_in_dim(out_grad, (chip ^ r) * 2 * features, 2 * features, 1)
        for r in range(1, chips)
    ]
    grouped, slices = lax.optimization_barrier((grouped, slices))

    if aligned:
        own_mixing = prepare_mixing(grouped, jnp.stack([tensor, core]), local_bits)
        own_mixing = lax.all_to_all(own_mixing, "tensor", 0, 0)
        other_mixing = flip(own_mixing, "dp", 1)
        order = jnp.stack([core, core])
    else:
        row_index = jnp.arange(HALF, dtype=jnp.int32)[None, None, :, None]
        col_index = jnp.arange(2 * HALF, dtype=jnp.int32)[None, None, None, :]
        bits = (tensor >> jnp.arange(cross, dtype=jnp.int32)) & 1
        select = col_index == bits[:, None, None, None] * HALF + row_index
        mixing = (factors[local_bits:] + select.astype(F32)).astype(BF16)
        mixing = mixing.reshape(cross, count, hp * HALF, 2 * HALF).transpose(1, 0, 2, 3)
        mixing = lax.all_to_all(mixing, "tensor", 0, 0).transpose(1, 0, 2, 3)
        mixing = mixing.reshape(cross, groups, LANES, 2 * HALF).transpose(1, 0, 2, 3)
        mixing = jnp.concatenate([mixing[:, :, :128], mixing[:, :, 128:]], axis=-1)
        own_mixing, other_mixing = mixing[:, :, :64], mixing[:, :, 64:]
        order = jnp.stack([0 * core, core])

    other_weight = flip(down_weight, "dp", 1)

    strides = [hp * 2**bit for bit in range(cross)]
    crossing = [flip(part, "dp", 2 * (r + 1)) for r, part in enumerate(slices)]
    saved_local, values = forward_local(gate_pre, up_pre, grouped, local_bits)
    values, crossing = lax.optimization_barrier((values, crossing))

    values = swap_layout(values, count)
    half = groups // 2
    weights = down_weight, other_weight, place
    sent = [
        [back_matmul(part, lambda c: 0, *weights, BF16, begin, half) for part in crossing]
        for begin in (0, half)
    ]
    received = [
        [flip(part, "dp", 2 * (r + 1)) for r, part in enumerate(parts)] for parts in sent
    ]
    values, _ = lax.optimization_barrier((values, sent))
    saved_cross, values = forward_cross(values, own_mixing, other_mixing, order, strides)
    out_grad, _ = lax.optimization_barrier((out_grad, sent))
    back = back_matmul(out_grad, lambda c: 2 * c[1], *weights, F32, 0, groups)
    sums = []
    for n, terms in enumerate(received):
        total = back[n * half : (n + 1) * half]
        for term in terms:
            total = total + term.astype(F32)
        sums.append(total.astype(BF16))
    back = jnp.concatenate(sums, axis=0)
    back = swap_layout(back, count)
    values, back = lax.optimization_barrier((values, back))
    values = swap_layout(values, count)
    back, grads_cross = backward_cross(back, saved_cross, own_mixing, other_mixing, order, strides)
    mine_cross = over_cores(grads_cross)
    if aligned:
        back = join_rows(back, mine_cross)
    values, back, mine_cross = lax.optimization_barrier((values, back, mine_cross))
    all_values = [values] + [flip(values, "dp", 2 * r) for r in range(1, chips)]
    back = swap_layout(back, count)

    circle = cycle(count)
    spot = jnp.argmax(jnp.array(circle, jnp.int32) == tensor).astype(jnp.int32)
    steps = (spot + jnp.arange(count, dtype=jnp.int32)) % count
    ring = jnp.where(steps < count // 2, 2 * steps, 2 * (count - steps) - 1)
    shares = ()
    for r in range(chips):
        if r == 1:
            all_values, shares = lax.optimization_barrier((all_values, shares))
        shares = output_matmul(
            all_values[r], r, chips, down_weight, other_weight, ring, tuple(shares)
        )
    back, shares, mine_cross = lax.optimization_barrier((back, shares, mine_cross))
    if aligned:
        mine_cross = split_rows(back, rows, cross)
    else:
        mine_cross = to_owners(mine_cross, core, cross, count, hp)
    middle = local_bits // 2

    def first_half():
        return backward_local(back, saved_local, grouped, order, middle, local_bits)

    def second_half(first):
        lower, grads = first
        results = backward_local(lower, saved_local, grouped, order, 0, middle, gate_pre, up_pre)
        return results, mine_cross, (grads[0], flip(grads[1], "dp", 1))

    summed, second = ring_sum(shares, circle, first_half, second_half)
    (gate_grad, up_grad, grads_low), mine_cross, high_pair = second
    mine_high = (high_pair[0] + high_pair[1]).astype(BF16)
    piece = jnp.stack([summed[0]] + [flip(summed[r], "dp", 2 * r) for r in range(1, chips)])
    own_low = over_chips(over_cores(grads_low), chips)
    gathered, own_low = ring_gather(piece, circle, own_low)

    scale = 1.0 / math.sqrt(rows * lax.axis_size("dp"))
    parts_cross = (local_bits,) + with_other(over_chips(mine_cross, chips))
    parts_high = (middle,) + with_other(over_chips(mine_high, chips))
    early = place_grads([parts_high, parts_cross], order, factors.shape, scale)
    factor_grads = place_grads([(0,) + with_other(own_low)], order, factors.shape, scale, early)
    gathered, factor_grads = lax.optimization_barrier((gathered, factor_grads))
    output = place_output(gathered, ring, place)
    return (output, gate_grad, up_grad, factor_grads)


def solution(mesh):
    return jax.shard_map(
        body,
        mesh=mesh,
        in_specs=(
            P("dp", "tensor"),
            P("dp", "tensor"),
            P("tensor", "dp"),
            P(None, "tensor", None, None),
            P("dp", None),
        ),
        out_specs=(
            P("dp", None),
            P("dp", "tensor"),
            P("dp", "tensor"),
            P(None, "tensor", None, None),
        ),
        check_vma=False,
    )
```
